32 devices in a mesh: gx: 8 (over z, core), gy: 4 (over y, x).
Axes of the slice: x: 2, y: 2, z: 4, core: 2. Of those that a mesh axis runs over, the one named last changes fastest.
Arguments:
- rhs_field: float32 [128, 64, 128], P('gx', 'gy'), may hold values from -10 to 10
- diag_blocks: bfloat16 [128, 64, 128, 128], P('gx', 'gy'), may hold values from -1 to 4, as said below
- face_lift: bfloat16 [4, 128, 128], replicated, may hold values from -0.5 to 0.5
- face_state: int32 [128, 64, 4], P('gx', 'gy'), may hold values from 0 to 2
- restrict_basis: float32 [128, 8], replicated, may hold values from -0.5 to 0.5
- coarse_inverse: float32 [128, 64, 8, 8], P('gx', 'gy'), may hold values from -0.4 to 1.2
Outputs:
- solution_field: float32 [128, 64, 128], P('gx', 'gy')
- hessenberg: float32 [3, 2], replicated
The draws below stay inside these ranges and needn't reach their ends.
Inputs may be any that keep to these rules, and one draw needn't show every extreme that they name: `diag_blocks`: each block has diagonal entries between 2 and 4 and small off-diagonal entries.
All inputs are finite; a program needn't handle non-finite values.
Results may differ from the reference program's by a relative error of at most 0.0023.
Values may be sent and summed in bfloat16 or wider, within the bound.
A program may use at most 64 MiB of HBM per device.

```python
import math
import jax
import jax.numpy as jnp
from jax import lax

NODES = 128
COARSE = 8
NX = 128
NY = 64


def draw_rhs_field(key, part):
    first_key = jax.random.fold_in(key, 0)
    slope_term = 0.5 + jnp.arange(NY, dtype=jnp.float32) / NY
    base = jnp.clip(jax.random.normal(first_key, (NX, NY, NODES), jnp.float32), -6.0, 6.0)
    return base + slope_term[None, :, None]


def draw_diag_blocks(key, part):
    first_key, second_key = jax.random.split(key)
    diag_vals = jnp.exp(jax.random.uniform(first_key, (NX, NY, NODES), jnp.float32, math.log(2.0), math.log(4.0)))
    offdiag = jnp.clip(jax.random.normal(second_key, (NX, NY, NODES, NODES), jnp.float32), -4.0, 4.0)
    offdiag = offdiag / math.sqrt(NODES)
    identity = jnp.eye(NODES, dtype=jnp.float32)
    return (offdiag * (1.0 - identity) + identity * diag_vals[..., None]).astype(jnp.bfloat16)


def draw_coarse_inverse(key, part):
    first_key, second_key = jax.random.split(key)
    diag_vals = jnp.exp(jax.random.uniform(first_key, (NX, NY, COARSE), jnp.float32, math.log(0.4), math.log(1.2)))
    offdiag = jnp.clip(0.1 * jax.random.normal(second_key, (NX, NY, COARSE, COARSE), jnp.float32), -0.4, 0.4)
    identity = jnp.eye(COARSE, dtype=jnp.float32)
    return offdiag * (1.0 - identity) + identity * diag_vals[..., None]


def set_ends(values, stream_key, smallest, top_value):
    dims = values.shape
    spot = [jax.random.randint(jax.random.fold_in(stream_key, axis), (), 0, dims[axis]) for axis in range(len(dims))]
    values = values.at[tuple(spot)].set(smallest)
    longest = dims.index(max(dims))
    spot[longest] = (spot[longest] + 1) % dims[longest]
    return values.at[tuple(spot)].set(top_value)


def noise(rng, extent, scale, bound, held_as=jnp.bfloat16):
    entries = jax.random.normal(rng, extent, jnp.float32) * scale
    return jnp.minimum(jnp.maximum(entries, -bound), bound).astype(held_as)


def setup_inputs(seed: int = 0) -> dict:
    seeds = jax.random.split(jax.random.key(seed), 7)
    rhs_field = draw_rhs_field(jax.random.fold_in(seeds[6], 71), 0)
    diag_blocks = draw_diag_blocks(jax.random.fold_in(seeds[6], 71), 0)
    face_lift = noise(seeds[2], (4, NODES, NODES), NODES ** -0.5, 0.5)
    face_state = set_ends(jax.random.randint(seeds[3], (NX, NY, 4), 0, 3), jax.random.fold_in(seeds[3], 1), 0, 2).astype(jnp.int32)
    restrict_basis = noise(seeds[4], (NODES, COARSE), NODES ** -0.5, 0.5, jnp.float32)
    coarse_inverse = draw_coarse_inverse(jax.random.fold_in(seeds[6], 71), 0)
    return dict(rhs_field=rhs_field, diag_blocks=diag_blocks, face_lift=face_lift, face_state=face_state, restrict_basis=restrict_basis, coarse_inverse=coarse_inverse)


def apply_operator(field, diag_blocks, face_lift, face_state):
    rounded = field.astype(jnp.bfloat16)

    def row_product(pair):
        return jnp.einsum('ja,jab->jb', pair[0].astype(jnp.float32), pair[1].astype(jnp.float32))
    local_part = lax.map(row_product, (rounded, diag_blocks))
    padded = jnp.pad(rounded, ((1, 1), (1, 1), (0, 0)))
    neighbours = [padded[:-2, 1:-1], padded[2:, 1:-1], padded[1:-1, :-2], padded[1:-1, 2:]]
    zero_block = jnp.zeros_like(rounded)
    selected = []
    for face in range(4):
        state = face_state[:, :, face][:, :, None]
        other = neighbours[face]
        selected.append(jnp.where(state == 1, other, jnp.where(state == 2, other[:, :, ::-1], zero_block)))
    stacked = jnp.concatenate(selected, axis=-1)
    lifted = jnp.dot(stacked.reshape(-1, 4 * NODES), face_lift.reshape(4 * NODES, NODES), preferred_element_type=jnp.float32)
    return local_part + lifted.reshape(field.shape)

def coarse_correct(field, restrict_basis, coarse_inverse):
    high = lax.Precision.HIGHEST
    coarse = jnp.einsum('ija,ak->ijk', field, restrict_basis, precision=high)
    column_mean = lax.optimization_barrier(jnp.mean(coarse, axis=1, keepdims=True))
    centred = coarse - column_mean
    padded = jnp.pad(centred, ((0, 0), (1, 1), (0, 0)))
    smoothed = centred + 0.25 * (padded[:, :-2] + padded[:, 2:])
    solved = jnp.einsum('ijk,ijkl->ijl', smoothed, coarse_inverse, precision=high)
    return field + jnp.einsum('ijl,al->ija', solved, restrict_basis, precision=high)

def least_squares(start_len, hess):
    first = jnp.sqrt(hess[0, 0] ** 2 + hess[1, 0] ** 2)
    cos_one = hess[0, 0] / first
    sin_one = hess[1, 0] / first
    upper = cos_one * hess[0, 1] + sin_one * hess[1, 1]
    lower = -sin_one * hess[0, 1] + cos_one * hess[1, 1]
    second = jnp.sqrt(lower ** 2 + hess[2, 1] ** 2)
    cos_two = lower / second
    coef_two = cos_two * (-sin_one * start_len) / second
    coef_one = (cos_one * start_len - upper * coef_two) / first
    return (coef_one, coef_two)

def reference(rhs_field, diag_blocks, face_lift, face_state, restrict_basis, coarse_inverse):
    start_len = jnp.sqrt(jnp.sum(rhs_field * rhs_field))
    basis = [rhs_field / start_len]
    precon = []
    hess = jnp.zeros((3, 2), jnp.float32)
    for step in range(2):
        precond = coarse_correct(basis[step], restrict_basis, coarse_inverse)
        precon.append(precond)
        image = apply_operator(precond, diag_blocks, face_lift, face_state)
        coeffs = [jnp.sum(vector * image) for vector in basis]
        for index in range(step + 1):
            image = image - coeffs[index] * basis[index]
            hess = hess.at[index, step].set(coeffs[index])
        length = jnp.sqrt(jnp.sum(image * image))
        hess = hess.at[step + 1, step].set(length)
        if step == 0:
            basis.append(image / length)
    coef_one, coef_two = least_squares(start_len, hess)
    return (coef_one * precon[0] + coef_two * precon[1], hess)
```

```python
import functools
import jax
import jax.numpy as jnp
from jax import lax
from jax.experimental import pallas as pl
from jax.experimental.pallas import tpu as pltpu
from jax.sharding import PartitionSpec as P

MESH = pl.DeviceIdType.MESH
F32 = jnp.float32
BF16 = jnp.bfloat16


def hdot(a, b, dims=(((1,), (0,)), ((), ()))):
    return lax.dot_general(a, b, dims, precision=lax.Precision.HIGHEST, preferred_element_type=F32)


def total(x):
    return jnp.sum(jnp.sum(x, axis=0, keepdims=True), axis=1, keepdims=True)


def safe_div(a, b):
    return jnp.where(b > 0, a / jnp.where(b > 0, b, 1.0), 0.0)


def iota(shape, dim):
    return lax.broadcasted_iota(jnp.int32, shape, dim)


def kernel(nx, ny, ti, tj, n, kc, rhs_h, diag, lift_h, state_h, basis_h, cinv_h, out, hess_out,
           rhs, lift, state, basis, cinv,
           dvm, wts, masks, cext, wbuf, sends, halos, csend, chalo, sums, msgs,
           isem, dsem, ssem, rsem, lsend, lrecv, msend, mrecv, know):
    gx = lax.axis_index("gx")
    gy = lax.axis_index("gy")
    me = gx * ny + gy
    count = nx * ny
    elems = ti * tj
    kk = kc * kc

    loads = [pltpu.make_async_copy(a, b, isem.at[q]) for q, (a, b) in enumerate(
        ((rhs_h, rhs), (basis_h, basis), (cinv_h, cinv), (state_h, state), (lift_h, lift)))]
    for c in loads:
        c.start()
    dcopies = [pltpu.make_async_copy(diag.at[q], dvm.at[q], dsem.at[q]) for q in range(ti)]
    for c in dcopies:
        c.start()

    barrier = pltpu.get_barrier_semaphore()

    has_n, has_s, has_w, has_e = gx > 0, gx < nx - 1, gy > 0, gy < ny - 1
    n_i, s_i, w_i, e_i = [v.astype(jnp.int32) for v in (has_n, has_s, has_w, has_e)]
    near = [(has_n, -1, k) for k in range(ny)] + [(has_s, 1, k) for k in range(ny)] + [
        (None, 0, k) for k in range(1, ny)]
    near_count = ny - 1 + ny * (n_i + s_i)

    def when(ok, run):
        if ok is None:
            run()
        else:
            pl.when(ok)(run)

    sums[...] = jnp.zeros_like(sums)
    for ok, d, k in near:
        def hello(d=d, k=k):
            pl.semaphore_signal(barrier, inc=1, device_id=(gx + d, lax.rem(gy + k, ny)), device_id_type=MESH)
        when(ok, hello)

    steps = []
    r = 2
    while r < nx - 1:
        steps.append(r)
        r *= 2

    def tell(q):
        r = steps[q]
        for ok, d in ((gx >= r, -r), (gx + r < nx, r)):
            def one(d=d):
                pl.semaphore_signal(know.at[q], inc=1, device_id=(gx + d, gy), device_id_type=MESH)
            when(ok, one)

    def learn(q):
        r = steps[q]
        amount = (gx >= r).astype(jnp.int32) + (gx + r < nx).astype(jnp.int32)
        pl.semaphore_wait(know.at[q], amount)

    def line_copy(g, d, k):
        return pltpu.make_async_remote_copy(
            src_ref=sums.at[g, ny + gy], dst_ref=sums.at[g, (1 - d) * ny + gy],
            send_sem=lsend.at[g, d + 1], recv_sem=lrecv.at[g, 1 - d],
            device_id=(gx + d, lax.rem(gy + k, ny)), device_id_type=MESH)

    def share_lines(g):
        for ok, d, k in near:
            when(ok, lambda d=d, k=k: line_copy(g, d, k).start())

    def line_wait(g, which):
        for ok, d in ((has_n, -1), (has_s, 1), (None, 0)):
            def one(d=d):
                part = sums.at[g, pl.ds((d + 1) * ny, ny if d else ny - 1)]
                c = pltpu.make_async_remote_copy(
                    src_ref=part, dst_ref=part, send_sem=lsend.at[g, d + 1], recv_sem=lrecv.at[g, d + 1],
                    device_id=(gx, gy), device_id_type=MESH)
                if which == "send":
                    c.wait_send()
                else:
                    c.wait_recv()
            when(ok, one)

    h = 2 * ti + 2 * tj
    o_n, o_s, o_w, o_e = 0, tj, 2 * tj, 2 * tj + 2 * ti
    o_nw = 2 * tj + 4 * ti
    o_ne, o_sw, o_se = o_nw + 8, o_nw + 16, o_nw + 24
    hrows = o_nw + 32
    routes = [
        (has_n, (gx - 1, gy), o_n, o_s, tj),
        (has_s, (gx + 1, gy), o_s, o_n, tj),
        (has_w, (gx, gy - 1), o_w, o_e, 2 * ti),
        (has_e, (gx, gy + 1), o_e, o_w, 2 * ti),
        (jnp.logical_and(has_n, has_w), (gx - 1, gy - 1), o_nw, o_se, 8),
        (jnp.logical_and(has_n, has_e), (gx - 1, gy + 1), o_ne, o_sw, 8),
        (jnp.logical_and(has_s, has_w), (gx + 1, gy - 1), o_sw, o_ne, 8),
        (jnp.logical_and(has_s, has_e), (gx + 1, gy + 1), o_se, o_nw, 8),
    ]
    croutes = [
        (has_n, (gx - 1, gy), 0, tj, tj),
        (has_s, (gx + 1, gy), tj, 0, tj),
        (has_w, (gx, gy - 1), 2 * tj, 2 * tj + ti, ti),
        (has_e, (gx, gy + 1), 2 * tj + ti, 2 * tj, ti),
    ]
    opposite = [1, 0, 3, 2, 7, 6, 5, 4]

    def rim_copies(g):
        return [(ok, pltpu.make_async_remote_copy(
            src_ref=sends.at[g, pl.ds(src, rows)], dst_ref=halos.at[g, pl.ds(dst, rows)],
            send_sem=ssem.at[g, d], recv_sem=rsem.at[g, opposite[d]],
            device_id=dev, device_id_type=MESH)) for d, (ok, dev, src, dst, rows) in enumerate(routes)]

    def coarse_copies():
        return [(ok, pltpu.make_async_remote_copy(
            src_ref=csend.at[pl.ds(src, rows)], dst_ref=chalo.at[pl.ds(dst, rows)],
            send_sem=ssem.at[2, d], recv_sem=rsem.at[2, opposite[d]],
            device_id=dev, device_id_type=MESH)) for d, (ok, dev, src, dst, rows) in enumerate(croutes)]

    def rim_wait(g, which):
        table = routes if g < 2 else croutes
        for d, (ok, dev, src, dst, rows) in enumerate(table):
            @pl.when(ok)
            def _(d=d, dev=dev, src=src, rows=rows):
                if g < 2:
                    s, r = sends.at[g, pl.ds(src, rows)], halos.at[g, pl.ds(src, rows)]
                else:
                    s, r = csend.at[pl.ds(src, rows)], chalo.at[pl.ds(src, rows)]
                c = pltpu.make_async_remote_copy(
                    src_ref=s, dst_ref=r, send_sem=ssem.at[g, d], recv_sem=rsem.at[g, d],
                    device_id=dev, device_id_type=MESH)
                if which == "send":
                    c.wait_send()
                else:
                    c.wait_recv()

    def start_all(copies):
        for ok, c in copies:
            @pl.when(ok)
            def _(c=c):
                c.start()

    def broadcast():
        def one(k, carry):
            t = lax.rem(me + k, count)
            pltpu.make_async_remote_copy(
                src_ref=msgs.at[me], dst_ref=msgs.at[me], send_sem=msend.at[0], recv_sem=mrecv.at[0],
                device_id=(t // ny, lax.rem(t, ny)), device_id_type=MESH).start()
            return carry
        lax.fori_loop(1, count, one, 0)

    def bc_wait(which):
        part = msgs.at[pl.ds(0, count - 1)]
        c = pltpu.make_async_remote_copy(
            src_ref=part, dst_ref=part, send_sem=msend.at[0], recv_sem=mrecv.at[0],
            device_id=(gx, gy), device_id_type=MESH)
        if which == "send":
            c.wait_send()
        else:
            c.wait_recv()

    def fill_sends(g, ref):
        sends[g, o_n:o_n + tj] = ref[0]
        sends[g, o_s:o_s + tj] = ref[ti - 1]
        sends[g, o_w:o_w + ti] = ref[:, 0, :]
        sends[g, o_w + ti:o_w + 2 * ti] = ref[:, 1, :]
        sends[g, o_e:o_e + ti] = ref[:, tj - 1, :]
        sends[g, o_e + ti:o_e + 2 * ti] = ref[:, tj - 2, :]
        sends[g, o_nw:o_nw + 8] = jnp.broadcast_to(ref[0, 0:1, :], (8, n))
        sends[g, o_ne:o_ne + 8] = jnp.broadcast_to(ref[0, tj - 1:tj, :], (8, n))
        sends[g, o_sw:o_sw + 8] = jnp.broadcast_to(ref[ti - 1, 0:1, :], (8, n))
        sends[g, o_se:o_se + 8] = jnp.broadcast_to(ref[ti - 1, tj - 1:tj, :], (8, n))

    lane1 = iota((1, n), 1)

    def message(values):
        row = jnp.zeros((1, n), F32)
        for p, v in enumerate(values):
            row = jnp.where(lane1 == p, v, row)
        return row

    e1 = (iota((kc, n), 1) // kc == iota((kc, n), 0)).astype(F32)
    e3 = (lax.rem(iota((kc, n), 1), kc) == iota((kc, n), 0)).astype(F32)
    pick = iota((ti, n), 1) // kc == iota((ti, n), 0)
    loads[0].wait()
    loads[1].wait()
    Rt = basis[...]
    over_first = (((0,), (0,)), ((), ()))
    RT = hdot(Rt, e3, over_first)

    def packed_rowsum(f3):
        rows = hdot(jnp.sum(f3, axis=1), RT)
        return jnp.sum(jnp.where(pick, rows, 0.0), axis=0, keepdims=True)

    rhs3 = rhs[...]
    rhs2 = rhs3.reshape(elems, n)
    fill_sends(0, rhs)
    sums[0, ny + gy] = packed_rowsum(rhs3)

    pl.semaphore_wait(barrier, near_count)
    start_all(rim_copies(0))
    share_lines(0)
    loads[2].wait()
    cext[...] = jnp.zeros_like(cext)
    eye = (iota((tj, tj), 0) == iota((tj, tj), 1)).astype(F32)
    for q in range(ti):
        cext[q * tj:(q + 1) * tj, 0:kk] = hdot(eye, cinv[q], (((1,), (1,)), ((), ())))
    c3d = cext[0:elems].reshape(ti, tj, n)
    csend[0:tj] = c3d[0]
    csend[tj:2 * tj] = c3d[ti - 1]
    csend[2 * tj:2 * tj + ti] = c3d[:, 0, :]
    csend[2 * tj + ti:2 * tj + 2 * ti] = c3d[:, tj - 1, :]
    start_all(coarse_copies())

    RE = hdot(Rt, e1, over_first)
    e4 = (lax.rem(iota((n, kc), 0), kc) == iota((n, kc), 1)).astype(F32)
    RF = hdot(e4, Rt)
    G = (lax.rem(iota((n, n), 0), kc) == iota((n, n), 1) // kc).astype(F32)
    flip = (iota((n, n), 0) + iota((n, n), 1) == n - 1).astype(BF16)
    loads[4].wait()
    for f in range(4):
        wts[2 * f * n:(2 * f + 1) * n] = lift[f]
        wts[(2 * f + 1) * n:(2 * f + 2) * n] = jnp.dot(flip, lift[f], preferred_element_type=F32).astype(BF16)
    loads[3].wait()
    own_j = lax.rem(iota((elems, tj), 0), tj) == iota((elems, tj), 1)
    ones = jnp.ones((tj, n), BF16)
    for f in range(4):
        rows = state[:, f, :].astype(F32)
        wide = jnp.broadcast_to(rows[:, None, :], (ti, tj, tj)).reshape(elems, tj)
        col = jnp.dot(jnp.where(own_j, wide, 0.0).astype(BF16), ones, preferred_element_type=F32)
        masks[2 * f] = (col == 1.0).astype(F32)
        masks[2 * f + 1] = (col == 2.0).astype(F32)

    hrow = iota((hrows, 1), 0)
    valid = jnp.where(hrow < o_s, n_i, jnp.where(hrow < o_w, s_i, jnp.where(
        hrow < o_e, w_i, jnp.where(hrow < o_nw, e_i, jnp.where(
            hrow < o_ne, n_i * w_i, jnp.where(hrow < o_sw, n_i * e_i, jnp.where(
                hrow < o_se, s_i * w_i, s_i * e_i))))))) > 0

    jrow = lax.rem(iota((elems, 1), 0), tj)
    trow = iota((tj, 1), 0)

    def spread(col):
        return jnp.broadcast_to(col[:, None, :], (ti, tj, n)).reshape(elems, n)

    def left_of(x, edge):
        return jnp.where(jrow == 0, spread(edge), pltpu.roll(x, 1, 0))

    def right_of(x, edge):
        return jnp.where(jrow == tj - 1, spread(edge), pltpu.roll(x, elems - 1, 0))

    def line_sum(g, d):
        acc = sums[g, (d + 1) * ny]
        for q in range(1, ny):
            acc = acc + sums[g, (d + 1) * ny + q]
        return acc

    def three_lines(g):
        return line_sum(g, 0), line_sum(g, -1), line_sum(g, 1)

    def precondition(f_own, f_halo, lines, coarse):
        p_c, p_n, p_s = lines
        stack = jnp.concatenate([
            jnp.where(pick, jnp.broadcast_to(p_c, (ti, n)), 0.0),
            jnp.broadcast_to(jnp.where(lane1 // kc == ti - 1, p_n, 0.0), (8, n)),
            jnp.broadcast_to(jnp.where(lane1 // kc == 0, p_s, 0.0), (8, n))], axis=0)
        mean = hdot(stack, G) * (1.0 / (ny * tj))
        m_c, m_n, m_s = mean[0:ti], mean[ti:ti + 1], mean[ti + 8:ti + 9]
        c_own = coarse - spread(m_c)
        c_halo = hdot(f_halo, RE)
        m_halo = jnp.concatenate([
            jnp.broadcast_to(m_n, (tj, n)), jnp.broadcast_to(m_s, (tj, n)), m_c, m_c, m_c, m_c,
            jnp.broadcast_to(m_n, (16, n)), jnp.broadcast_to(m_s, (16, n))], axis=0)
        c_halo = jnp.where(valid, c_halo - m_halo, 0.0)
        c_w1, c_w2 = c_halo[o_w:o_w + ti], c_halo[o_w + ti:o_e]
        c_e1, c_e2 = c_halo[o_e:o_e + ti], c_halo[o_e + ti:o_nw]
        c_n, c_s = c_halo[o_n:o_n + tj], c_halo[o_s:o_s + tj]
        c3 = c_own.reshape(ti, tj, n)
        s_own = c_own + 0.25 * (left_of(c_own, c_w1) + right_of(c_own, c_e1))

        def row_smooth(x, lo, hi):
            left = jnp.where(trow == 0, lo, pltpu.roll(x, 1, 0))
            right = jnp.where(trow == tj - 1, hi, pltpu.roll(x, tj - 1, 0))
            return x + 0.25 * (left + right)
        s_n = row_smooth(c_n, c_halo[o_nw:o_nw + 1], c_halo[o_ne:o_ne + 1])
        s_s = row_smooth(c_s, c_halo[o_sw:o_sw + 1], c_halo[o_se:o_se + 1])
        s_w = c_w1 + 0.25 * (c_w2 + c3[:, 0, :])
        s_e = c_e1 + 0.25 * (c3[:, tj - 1, :] + c_e2)
        z_own = f_own + hdot(s_own * cext[0:elems], RF)
        f_rim = jnp.concatenate([f_halo[o_n:o_w], f_halo[o_w:o_w + ti], f_halo[o_e:o_e + ti]], axis=0)
        ok_rim = jnp.concatenate([valid[o_n:o_w], valid[o_w:o_w + ti], valid[o_e:o_e + ti]], axis=0)
        s_rim = jnp.concatenate([s_n, s_s, s_w, s_e], axis=0)
        z_rim = jnp.where(ok_rim, f_rim + hdot(s_rim * cext[elems:elems + h], RF), 0.0)
        return z_own, z_rim

    def operator(z, z_rim):
        nb = [
            jnp.concatenate([z_rim[0:tj], z[0:elems - tj]], axis=0),
            jnp.concatenate([z[tj:], z_rim[tj:2 * tj]], axis=0),
            left_of(z, z_rim[2 * tj:2 * tj + ti]),
            right_of(z, z_rim[2 * tj + ti:2 * tj + 2 * ti]),
        ]
        cols = []
        for f in range(4):
            cols.append((nb[f] * masks[2 * f]).astype(BF16))
            cols.append((nb[f] * masks[2 * f + 1]).astype(BF16))
        lifted = jnp.dot(jnp.concatenate(cols, axis=1), wts[...], preferred_element_type=F32)
        wbuf[...] = lifted.reshape(ti, tj, n)
        half = tj // 2
        for q in range(ti):
            a = z[q * tj:(q + 1) * tj]
            hi = a.astype(BF16)
            both = jnp.concatenate([hi, (a - hi.astype(F32)).astype(BF16)], axis=0)
            lhs = jnp.concatenate([both * keep[t] for t in range(half)], axis=1)
            rhs_w = jnp.concatenate(
                [dvm[q, 0:half].reshape(half * n, n), dvm[q, half:tj].reshape(half * n, n)], axis=1)
            prod = jnp.dot(lhs, rhs_w, preferred_element_type=F32)
            prod = prod[0:tj] + prod[tj:2 * tj]
            wbuf[q] += jnp.concatenate([prod[0:half, 0:n], prod[half:tj, n:2 * n]], axis=0)

    keep = [(lax.rem(iota((2 * tj, n), 0), tj // 2) == t).astype(F32).astype(BF16) for t in range(tj // 2)]
    coarse_rhs = hdot(rhs2, RE)
    line_wait(0, "recv")
    rim_wait(0, "recv")
    rim_wait(2, "recv")
    if steps:
        tell(0)

    cext[elems:elems + h] = chalo[...]
    z1, z1_rim = precondition(rhs2, jnp.where(valid, halos[0], 0.0), three_lines(0), coarse_rhs)
    for c in dcopies:
        c.wait()
    operator(z1, z1_rim)
    fill_sends(1, wbuf)
    start_all(rim_copies(1))
    sums[1, ny + gy] = packed_rowsum(wbuf[...])
    share_lines(1)
    w1 = wbuf[...].reshape(elems, n)
    for q in range(len(steps)):
        learn(q)
        if q + 1 < len(steps):
            tell(q + 1)
    own_n1 = total(rhs2 * rhs2)
    p_one = safe_div(total(rhs2 * w1), own_n1)
    gap = w1 - p_one * rhs2
    own_n2 = total(gap * gap)
    coarse_w = hdot(w1, RE)
    line_wait(1, "recv")
    rim_wait(1, "recv")

    z2, z2_rim = precondition(w1, jnp.where(valid, halos[1], 0.0), three_lines(1), coarse_w)
    operator(z2, z2_rim)
    w2 = wbuf[...].reshape(elems, n)
    p_two = safe_div(total(rhs2 * w2), own_n1)
    q_two = safe_div(total(gap * w2), own_n2)
    rest = w2 - p_two * rhs2 - q_two * gap
    msgs[me] = message([own_n1, p_one, own_n2, p_two, q_two, total(rest * rest)])
    broadcast()
    bc_wait("recv")
    Y = msgs[:, 0, :]
    l_n1, l_p, l_n2, l_a, l_b, l_n3 = [Y[:, q:q + 1] for q in range(6)]

    def over(x):
        return jnp.sum(x, axis=0, keepdims=True)
    len2 = over(l_n1)
    start_len = jnp.sqrt(len2)
    h11 = over(l_p * l_n1) / len2
    dev = l_p - h11
    gap2 = over(dev * dev * l_n1 + l_n2)
    gap_len = jnp.sqrt(gap2)
    h21 = gap_len / start_len
    e_one = l_a - h11 * l_p
    e_two = l_b - h11
    t12 = over(e_one * l_n1) / len2
    h12 = t12 * start_len / gap_len
    h22 = over(dev * e_one * l_n1 + e_two * l_n2) / gap2
    g_one = e_one - t12 - h22 * dev
    g_two = e_two - h22
    h32 = jnp.sqrt(over(g_one * g_one * l_n1 + g_two * g_two * l_n2 + l_n3)) / gap_len

    first = jnp.sqrt(h11 * h11 + h21 * h21)
    cos_one = h11 / first
    sin_one = h21 / first
    upper = cos_one * h12 + sin_one * h22
    lower = -sin_one * h12 + cos_one * h22
    second = jnp.sqrt(lower * lower + h32 * h32)
    cos_two = lower / second
    y2 = cos_two * (-sin_one * start_len) / second
    y1 = (cos_one * start_len - upper * y2) / first
    c2 = y2 / gap_len
    c1 = y1 / start_len - c2 * h11
    out[...] = (c1 * z1 + c2 * z2).reshape(ti, tj, n)
    hr, hc = iota((2, 3), 1), iota((2, 3), 0)
    hess_out[...] = jnp.where(
        hr == 0, jnp.where(hc == 0, h11, h12),
        jnp.where(hr == 1, jnp.where(hc == 0, h21, h22), jnp.where(hc == 0, 0.0, h32)))

    bc_wait("send")
    for g in range(2):
        line_wait(g, "send")
    for g in range(3):
        rim_wait(g, "send")


def hand_on(sol_in, hess_in, sol_out, hess_out):
    sol_out[...] = sol_in[...]
    hess_out[...] = hess_in[...]


def solution(mesh):
    nx, ny = mesh.shape["gx"], mesh.shape["gy"]

    def body(rhs, diag, lift, state, basis, cinv):
        ti, tj, n = rhs.shape
        kc = basis.shape[1]
        cflat = jnp.transpose(cinv, (0, 2, 3, 1)).reshape(ti, kc * kc, tj)
        sflat = jnp.transpose(state, (0, 2, 1))
        hrows = 2 * tj + 4 * ti + 32
        h = 2 * ti + 2 * tj
        vm = pl.BlockSpec(memory_space=pltpu.VMEM)
        hbm = pl.BlockSpec(memory_space=pltpu.HBM)
        sol, hess = pl.pallas_call(
            functools.partial(kernel, nx, ny, ti, tj, n, kc),
            out_shape=(jax.ShapeDtypeStruct((ti, tj, n), F32), jax.ShapeDtypeStruct((2, 3), F32)),
            in_specs=[hbm] * 6,
            out_specs=(vm, vm),
            scratch_shapes=[
                pltpu.VMEM((ti, tj, n), F32),
                pltpu.VMEM((4, n, n), BF16),
                pltpu.VMEM((ti, 4, tj), jnp.int32),
                pltpu.VMEM((kc, n), F32),
                pltpu.VMEM((ti, kc * kc, tj), F32),
                pltpu.VMEM((ti, tj, n, n), BF16),
                pltpu.VMEM((8 * n, n), BF16),
                pltpu.VMEM((8, ti * tj, n), F32),
                pltpu.VMEM((ti * tj + h, n), F32),
                pltpu.VMEM((ti, tj, n), F32),
                pltpu.VMEM((2, hrows, n), F32),
                pltpu.VMEM((2, hrows, n), F32),
                pltpu.VMEM((h, n), F32),
                pltpu.VMEM((h, n), F32),
                pltpu.VMEM((2, 3 * ny, 1, n), F32),
                pltpu.VMEM((nx * ny, 1, n), F32),
                pltpu.SemaphoreType.DMA((5,)),
                pltpu.SemaphoreType.DMA((ti,)),
                pltpu.SemaphoreType.DMA((3, 8)),
                pltpu.SemaphoreType.DMA((3, 8)),
                pltpu.SemaphoreType.DMA((2, 3)),
                pltpu.SemaphoreType.DMA((2, 3)),
                pltpu.SemaphoreType.DMA((1,)),
                pltpu.SemaphoreType.DMA((1,)),
                pltpu.SemaphoreType.REGULAR((max(1, nx.bit_length()),)),
            ],
            compiler_params=pltpu.CompilerParams(collective_id=0, has_side_effects=True,
                                                 vmem_limit_bytes=60 * 1024 * 1024),
        )(rhs, diag, lift, sflat, basis.T, cflat)
        sol, hess = pl.pallas_call(
            hand_on,
            out_shape=(jax.ShapeDtypeStruct(sol.shape, F32), jax.ShapeDtypeStruct(hess.shape, F32)),
            in_specs=[vm, vm],
            out_specs=(vm, vm),
            compiler_params=pltpu.CompilerParams(vmem_limit_bytes=60 * 1024 * 1024),
        )(sol, hess)
        return sol, hess.T

    in_specs = (P("gx", "gy", None), P("gx", "gy", None, None), P(), P("gx", "gy", None), P(),
                P("gx", "gy", None, None))
    return jax.shard_map(body, mesh=mesh, in_specs=in_specs, out_specs=(P("gx", "gy", None), P()), check_vma=False)
```

```python
import functools
import jax
import jax.numpy as jnp
from jax import lax
from jax.experimental import pallas as pl
from jax.experimental.pallas import tpu as pltpu
from jax.sharding import PartitionSpec as P

MESH = pl.DeviceIdType.MESH
F32 = jnp.float32
BF16 = jnp.bfloat16


def hdot(a, b, dims=(((1,), (0,)), ((), ()))):
    return lax.dot_general(a, b, dims, precision=lax.Precision.HIGHEST, preferred_element_type=F32)


def total(x):
    return jnp.sum(jnp.sum(x, axis=0, keepdims=True), axis=1, keepdims=True)


def safe_div(a, b):
    return jnp.where(b > 0, a / jnp.where(b > 0, b, 1.0), 0.0)


def iota(shape, dim):
    return lax.broadcasted_iota(jnp.int32, shape, dim)


def kernel(nx, ny, ti, tj, n, kc, rhs_h, diag, lift_h, state_h, basis_h, cinv_h, out, hess_out,
           rhs, lift, state, basis, cinv,
           dvm, wts, masks, cext, wbuf, sends, halos, csend, chalo, sums, msgs,
           isem, dsem, ssem, rsem, lsend, lrecv, msend, mrecv, know):
    gx = lax.axis_index("gx")
    gy = lax.axis_index("gy")
    me = gx * ny + gy
    count = nx * ny
    elems = ti * tj
    kk = kc * kc

    loads = [pltpu.make_async_copy(a, b, isem.at[q]) for q, (a, b) in enumerate(
        ((rhs_h, rhs), (basis_h, basis), (cinv_h, cinv), (state_h, state), (lift_h, lift)))]
    for c in loads:
        c.start()
    dcopies = [pltpu.make_async_copy(diag.at[q], dvm.at[q], dsem.at[q]) for q in range(ti)]
    for c in dcopies:
        c.start()

    barrier = pltpu.get_barrier_semaphore()

    has_n, has_s, has_w, has_e = gx > 0, gx < nx - 1, gy > 0, gy < ny - 1
    n_i, s_i, w_i, e_i = [v.astype(jnp.int32) for v in (has_n, has_s, has_w, has_e)]
    near = [(has_n, -1, k) for k in range(ny)] + [(has_s, 1, k) for k in range(ny)] + [
        (None, 0, k) for k in range(1, ny)]
    near_count = ny - 1 + ny * (n_i + s_i)

    def when(ok, run):
        if ok is None:
            run()
        else:
            pl.when(ok)(run)

    sums[...] = jnp.zeros_like(sums)
    for ok, d, k in near:
        def hello(d=d, k=k):
            pl.semaphore_signal(barrier, inc=1, device_id=(gx + d, lax.rem(gy + k, ny)), device_id_type=MESH)
        when(ok, hello)

    steps = []
    r = 2
    while r < nx - 1:
        steps.append(r)
        r *= 2

    def tell(q):
        r = steps[q]
        for ok, d in ((gx >= r, -r), (gx + r < nx, r)):
            def one(d=d):
                pl.semaphore_signal(know.at[q], inc=1, device_id=(gx + d, gy), device_id_type=MESH)
            when(ok, one)

    def learn(q):
        r = steps[q]
        amount = (gx >= r).astype(jnp.int32) + (gx + r < nx).astype(jnp.int32)
        pl.semaphore_wait(know.at[q], amount)

    def line_copy(g, d, k):
        return pltpu.make_async_remote_copy(
            src_ref=sums.at[g, ny + gy], dst_ref=sums.at[g, (1 - d) * ny + gy],
            send_sem=lsend.at[g, d + 1], recv_sem=lrecv.at[g, 1 - d],
            device_id=(gx + d, lax.rem(gy + k, ny)), device_id_type=MESH)

    def share_lines(g):
        for ok, d, k in near:
            when(ok, lambda d=d, k=k: line_copy(g, d, k).start())

    def line_wait(g, which):
        for ok, d in ((has_n, -1), (has_s, 1), (None, 0)):
            def one(d=d):
                part = sums.at[g, pl.ds((d + 1) * ny, ny if d else ny - 1)]
                c = pltpu.make_async_remote_copy(
                    src_ref=part, dst_ref=part, send_sem=lsend.at[g, d + 1], recv_sem=lrecv.at[g, d + 1],
                    device_id=(gx, gy), device_id_type=MESH)
                if which == "send":
                    c.wait_send()
                else:
                    c.wait_recv()
            when(ok, one)

    h = 2 * ti + 2 * tj
    o_n, o_s, o_w, o_e = 0, tj, 2 * tj, 2 * tj + 2 * ti
    o_nw = 2 * tj + 4 * ti
    o_ne, o_sw, o_se = o_nw + 8, o_nw + 16, o_nw + 24
    hrows = o_nw + 32
    routes = [
        (has_n, (gx - 1, gy), o_n, o_s, tj),
        (has_s, (gx + 1, gy), o_s, o_n, tj),
        (has_w, (gx, gy - 1), o_w, o_e, 2 * ti),
        (has_e, (gx, gy + 1), o_e, o_w, 2 * ti),
        (jnp.logical_and(has_n, has_w), (gx - 1, gy - 1), o_nw, o_se, 8),
        (jnp.logical_and(has_n, has_e), (gx - 1, gy + 1), o_ne, o_sw, 8),
        (jnp.logical_and(has_s, has_w), (gx + 1, gy - 1), o_sw, o_ne, 8),
        (jnp.logical_and(has_s, has_e), (gx + 1, gy + 1), o_se, o_nw, 8),
    ]
    croutes = [
        (has_n, (gx - 1, gy), 0, tj, tj),
        (has_s, (gx + 1, gy), tj, 0, tj),
        (has_w, (gx, gy - 1), 2 * tj, 2 * tj + ti, ti),
        (has_e, (gx, gy + 1), 2 * tj + ti, 2 * tj, ti),
    ]
    opposite = [1, 0, 3, 2, 7, 6, 5, 4]

    def rim_copies(g):
        return [(ok, pltpu.make_async_remote_copy(
            src_ref=sends.at[g, pl.ds(src, rows)], dst_ref=halos.at[g, pl.ds(dst, rows)],
            send_sem=ssem.at[g, d], recv_sem=rsem.at[g, opposite[d]],
            device_id=dev, device_id_type=MESH)) for d, (ok, dev, src, dst, rows) in enumerate(routes)]

    def coarse_copies():
        return [(ok, pltpu.make_async_remote_copy(
            src_ref=csend.at[pl.ds(src, rows)], dst_ref=chalo.at[pl.ds(dst, rows)],
            send_sem=ssem.at[2, d], recv_sem=rsem.at[2, opposite[d]],
            device_id=dev, device_id_type=MESH)) for d, (ok, dev, src, dst, rows) in enumerate(croutes)]

    def rim_wait(g, which):
        table = routes if g < 2 else croutes
        for d, (ok, dev, src, dst, rows) in enumerate(table):
            @pl.when(ok)
            def _(d=d, dev=dev, src=src, rows=rows):
                if g < 2:
                    s, r = sends.at[g, pl.ds(src, rows)], halos.at[g, pl.ds(src, rows)]
                else:
                    s, r = csend.at[pl.ds(src, rows)], chalo.at[pl.ds(src, rows)]
                c = pltpu.make_async_remote_copy(
                    src_ref=s, dst_ref=r, send_sem=ssem.at[g, d], recv_sem=rsem.at[g, d],
                    device_id=dev, device_id_type=MESH)
                if which == "send":
                    c.wait_send()
                else:
                    c.wait_recv()

    def start_all(copies):
        for ok, c in copies:
            @pl.when(ok)
            def _(c=c):
                c.start()

    def broadcast():
        def one(k, carry):
            t = lax.rem(me + k, count)
            pltpu.make_async_remote_copy(
                src_ref=msgs.at[me], dst_ref=msgs.at[me], send_sem=msend.at[0], recv_sem=mrecv.at[0],
                device_id=(t // ny, lax.rem(t, ny)), device_id_type=MESH).start()
            return carry
        lax.fori_loop(1, count, one, 0)

    def bc_wait(which):
        part = msgs.at[pl.ds(0, count - 1)]
        c = pltpu.make_async_remote_copy(
            src_ref=part, dst_ref=part, send_sem=msend.at[0], recv_sem=mrecv.at[0],
            device_id=(gx, gy), device_id_type=MESH)
        if which == "send":
            c.wait_send()
        else:
            c.wait_recv()

    def fill_sends(g, ref):
        sends[g, o_n:o_n + tj] = ref[0]
        sends[g, o_s:o_s + tj] = ref[ti - 1]
        sends[g, o_w:o_w + ti] = ref[:, 0, :]
        sends[g, o_w + ti:o_w + 2 * ti] = ref[:, 1, :]
        sends[g, o_e:o_e + ti] = ref[:, tj - 1, :]
        sends[g, o_e + ti:o_e + 2 * ti] = ref[:, tj - 2, :]
        sends[g, o_nw:o_nw + 8] = jnp.broadcast_to(ref[0, 0:1, :], (8, n))
        sends[g, o_ne:o_ne + 8] = jnp.broadcast_to(ref[0, tj - 1:tj, :], (8, n))
        sends[g, o_sw:o_sw + 8] = jnp.broadcast_to(ref[ti - 1, 0:1, :], (8, n))
        sends[g, o_se:o_se + 8] = jnp.broadcast_to(ref[ti - 1, tj - 1:tj, :], (8, n))

    lane1 = iota((1, n), 1)

    def message(values):
        row = jnp.zeros((1, n), F32)
        for p, v in enumerate(values):
            row = jnp.where(lane1 == p, v, row)
        return row

    e1 = (iota((kc, n), 1) // kc == iota((kc, n), 0)).astype(F32)
    e3 = (lax.rem(iota((kc, n), 1), kc) == iota((kc, n), 0)).astype(F32)
    pick = iota((ti, n), 1) // kc == iota((ti, n), 0)
    loads[0].wait()
    loads[1].wait()
    Rt = basis[...]
    over_first = (((0,), (0,)), ((), ()))
    RT = hdot(Rt, e3, over_first)

    def packed_rowsum(f3):
        rows = hdot(jnp.sum(f3, axis=1), RT)
        return jnp.sum(jnp.where(pick, rows, 0.0), axis=0, keepdims=True)

    rhs3 = rhs[...]
    rhs2 = rhs3.reshape(elems, n)
    fill_sends(0, rhs)
    sums[0, ny + gy] = packed_rowsum(rhs3)

    pl.semaphore_wait(barrier, near_count)
    start_all(rim_copies(0))
    share_lines(0)
    loads[2].wait()
    cext[...] = jnp.zeros_like(cext)
    eye = (iota((tj, tj), 0) == iota((tj, tj), 1)).astype(F32)
    for q in range(ti):
        cext[q * tj:(q + 1) * tj, 0:kk] = hdot(eye, cinv[q], (((1,), (1,)), ((), ())))
    c3d = cext[0:elems].reshape(ti, tj, n)
    csend[0:tj] = c3d[0]
    csend[tj:2 * tj] = c3d[ti - 1]
    csend[2 * tj:2 * tj + ti] = c3d[:, 0, :]
    csend[2 * tj + ti:2 * tj + 2 * ti] = c3d[:, tj - 1, :]
    start_all(coarse_copies())

    RE = hdot(Rt, e1, over_first)
    e4 = (lax.rem(iota((n, kc), 0), kc) == iota((n, kc), 1)).astype(F32)
    RF = hdot(e4, Rt)
    G = (lax.rem(iota((n, n), 0), kc) == iota((n, n), 1) // kc).astype(F32)
    flip = (iota((n, n), 0) + iota((n, n), 1) == n - 1).astype(BF16)
    loads[4].wait()
    for f in range(4):
        wts[2 * f * n:(2 * f + 1) * n] = lift[f]
        wts[(2 * f + 1) * n:(2 * f + 2) * n] = jnp.dot(flip, lift[f], preferred_element_type=F32).astype(BF16)
    loads[3].wait()
    own_j = lax.rem(iota((elems, tj), 0), tj) == iota((elems, tj), 1)
    ones = jnp.ones((tj, n), BF16)
    for f in range(4):
        rows = state[:, f, :].astype(F32)
        wide = jnp.broadcast_to(rows[:, None, :], (ti, tj, tj)).reshape(elems, tj)
        col = jnp.dot(jnp.where(own_j, wide, 0.0).astype(BF16), ones, preferred_element_type=F32)
        masks[2 * f] = (col == 1.0).astype(F32)
        masks[2 * f + 1] = (col == 2.0).astype(F32)

    hrow = iota((hrows, 1), 0)
    valid = jnp.where(hrow < o_s, n_i, jnp.where(hrow < o_w, s_i, jnp.where(
        hrow < o_e, w_i, jnp.where(hrow < o_nw, e_i, jnp.where(
            hrow < o_ne, n_i * w_i, jnp.where(hrow < o_sw, n_i * e_i, jnp.where(
                hrow < o_se, s_i * w_i, s_i * e_i))))))) > 0

    jrow = lax.rem(iota((elems, 1), 0), tj)
    trow = iota((tj, 1), 0)

    def spread(col):
        return jnp.broadcast_to(col[:, None, :], (ti, tj, n)).reshape(elems, n)

    def left_of(x, edge):
        return jnp.where(jrow == 0, spread(edge), pltpu.roll(x, 1, 0))

    def right_of(x, edge):
        return jnp.where(jrow == tj - 1, spread(edge), pltpu.roll(x, elems - 1, 0))

    def line_sum(g, d):
        acc = sums[g, (d + 1) * ny]
        for q in range(1, ny):
            acc = acc + sums[g, (d + 1) * ny + q]
        return acc

    def three_lines(g):
        return line_sum(g, 0), line_sum(g, -1), line_sum(g, 1)

    def precondition(f_own, f_halo, lines, coarse):
        p_c, p_n, p_s = lines
        stack = jnp.concatenate([
            jnp.where(pick, jnp.broadcast_to(p_c, (ti, n)), 0.0),
            jnp.broadcast_to(jnp.where(lane1 // kc == ti - 1, p_n, 0.0), (8, n)),
            jnp.broadcast_to(jnp.where(lane1 // kc == 0, p_s, 0.0), (8, n))], axis=0)
        mean = hdot(stack, G) * (1.0 / (ny * tj))
        m_c, m_n, m_s = mean[0:ti], mean[ti:ti + 1], mean[ti + 8:ti + 9]
        c_own = coarse - spread(m_c)
        c_halo = hdot(f_halo, RE)
        m_halo = jnp.concatenate([
            jnp.broadcast_to(m_n, (tj, n)), jnp.broadcast_to(m_s, (tj, n)), m_c, m_c, m_c, m_c,
            jnp.broadcast_to(m_n, (16, n)), jnp.broadcast_to(m_s, (16, n))], axis=0)
        c_halo = jnp.where(valid, c_halo - m_halo, 0.0)
        c_w1, c_w2 = c_halo[o_w:o_w + ti], c_halo[o_w + ti:o_e]
        c_e1, c_e2 = c_halo[o_e:o_e + ti], c_halo[o_e + ti:o_nw]
        c_n, c_s = c_halo[o_n:o_n + tj], c_halo[o_s:o_s + tj]
        c3 = c_own.reshape(ti, tj, n)
        s_own = c_own + 0.25 * (left_of(c_own, c_w1) + right_of(c_own, c_e1))

        def row_smooth(x, lo, hi):
            left = jnp.where(trow == 0, lo, pltpu.roll(x, 1, 0))
            right = jnp.where(trow == tj - 1, hi, pltpu.roll(x, tj - 1, 0))
            return x + 0.25 * (left + right)
        s_n = row_smooth(c_n, c_halo[o_nw:o_nw + 1], c_halo[o_ne:o_ne + 1])
        s_s = row_smooth(c_s, c_halo[o_sw:o_sw + 1], c_halo[o_se:o_se + 1])
        s_w = c_w1 + 0.25 * (c_w2 + c3[:, 0, :])
        s_e = c_e1 + 0.25 * (c3[:, tj - 1, :] + c_e2)
        z_own = f_own + hdot(s_own * cext[0:elems], RF)
        f_rim = jnp.concatenate([f_halo[o_n:o_w], f_halo[o_w:o_w + ti], f_halo[o_e:o_e + ti]], axis=0)
        ok_rim = jnp.concatenate([valid[o_n:o_w], valid[o_w:o_w + ti], valid[o_e:o_e + ti]], axis=0)
        s_rim = jnp.concatenate([s_n, s_s, s_w, s_e], axis=0)
        z_rim = jnp.where(ok_rim, f_rim + hdot(s_rim * cext[elems:elems + h], RF), 0.0)
        return z_own, z_rim

    def operator(z, z_rim):
        nb = [
            jnp.concatenate([z_rim[0:tj], z[0:elems - tj]], axis=0),
            jnp.concatenate([z[tj:], z_rim[tj:2 * tj]], axis=0),
            left_of(z, z_rim[2 * tj:2 * tj + ti]),
            right_of(z, z_rim[2 * tj + ti:2 * tj + 2 * ti]),
        ]
        cols = []
        for f in range(4):
            cols.append((nb[f] * masks[2 * f]).astype(BF16))
            cols.append((nb[f] * masks[2 * f + 1]).astype(BF16))
        lifted = jnp.dot(jnp.concatenate(cols, axis=1), wts[...], preferred_element_type=F32)
        wbuf[...] = lifted.reshape(ti, tj, n)
        half = tj // 2
        for q in range(ti):
            a = z[q * tj:(q + 1) * tj]
            hi = a.astype(BF16)
            both = jnp.concatenate([hi, (a - hi.astype(F32)).astype(BF16)], axis=0)
            lhs = jnp.concatenate([both * keep[t] for t in range(half)], axis=1)
            rhs_w = jnp.concatenate(
                [dvm[q, 0:half].reshape(half * n, n), dvm[q, half:tj].reshape(half * n, n)], axis=1)
            prod = jnp.dot(lhs, rhs_w, preferred_element_type=F32)
            prod = prod[0:tj] + prod[tj:2 * tj]
            wbuf[q] += jnp.concatenate([prod[0:half, 0:n], prod[half:tj, n:2 * n]], axis=0)

    keep = [(lax.rem(iota((2 * tj, n), 0), tj // 2) == t).astype(F32).astype(BF16) for t in range(tj // 2)]
    coarse_rhs = hdot(rhs2, RE)
    line_wait(0, "recv")
    rim_wait(0, "recv")
    rim_wait(2, "recv")
    if steps:
        tell(0)

    cext[elems:elems + h] = chalo[...]
    z1, z1_rim = precondition(rhs2, jnp.where(valid, halos[0], 0.0), three_lines(0), coarse_rhs)
    for c in dcopies:
        c.wait()
    operator(z1, z1_rim)
    fill_sends(1, wbuf)
    start_all(rim_copies(1))
    sums[1, ny + gy] = packed_rowsum(wbuf[...])
    share_lines(1)
    w1 = wbuf[...].reshape(elems, n)
    for q in range(len(steps)):
        learn(q)
        if q + 1 < len(steps):
            tell(q + 1)
    own_n1 = total(rhs2 * rhs2)
    p_one = safe_div(total(rhs2 * w1), own_n1)
    gap = w1 - p_one * rhs2
    own_n2 = total(gap * gap)
    coarse_w = hdot(w1, RE)
    line_wait(1, "recv")
    rim_wait(1, "recv")

    z2, z2_rim = precondition(w1, jnp.where(valid, halos[1], 0.0), three_lines(1), coarse_w)
    operator(z2, z2_rim)
    w2 = wbuf[...].reshape(elems, n)
    p_two = safe_div(total(rhs2 * w2), own_n1)
    q_two = safe_div(total(gap * w2), own_n2)
    rest = w2 - p_two * rhs2 - q_two * gap
    msgs[me] = message([own_n1, p_one, own_n2, p_two, q_two, total(rest * rest)])
    broadcast()
    bc_wait("recv")
    Y = msgs[:, 0, :]
    l_n1, l_p, l_n2, l_a, l_b, l_n3 = [Y[:, q:q + 1] for q in range(6)]

    def over(x):
        return jnp.sum(x, axis=0, keepdims=True)
    len2 = over(l_n1)
    start_len = jnp.sqrt(len2)
    h11 = over(l_p * l_n1) / len2
    dev = l_p - h11
    gap2 = over(dev * dev * l_n1 + l_n2)
    gap_len = jnp.sqrt(gap2)
    h21 = gap_len / start_len
    e_one = l_a - h11 * l_p
    e_two = l_b - h11
    t12 = over(e_one * l_n1) / len2
    h12 = t12 * start_len / gap_len
    h22 = over(dev * e_one * l_n1 + e_two * l_n2) / gap2
    g_one = e_one - t12 - h22 * dev
    g_two = e_two - h22
    h32 = jnp.sqrt(over(g_one * g_one * l_n1 + g_two * g_two * l_n2 + l_n3)) / gap_len

    first = jnp.sqrt(h11 * h11 + h21 * h21)
    cos_one = h11 / first
    sin_one = h21 / first
    upper = cos_one * h12 + sin_one * h22
    lower = -sin_one * h12 + cos_one * h22
    second = jnp.sqrt(lower * lower + h32 * h32)
    cos_two = lower / second
    y2 = cos_two * (-sin_one * start_len) / second
    y1 = (cos_one * start_len - upper * y2) / first
    c2 = y2 / gap_len
    c1 = y1 / start_len - c2 * h11
    out[...] = (c1 * z1 + c2 * z2).reshape(ti, tj, n)
    hr, hc = iota((2, 3), 1), iota((2, 3), 0)
    hess_out[...] = jnp.where(
        hr == 0, jnp.where(hc == 0, h11, h12),
        jnp.where(hr == 1, jnp.where(hc == 0, h21, h22), jnp.where(hc == 0, 0.0, h32)))

    bc_wait("send")
    for g in range(2):
        line_wait(g, "send")
    for g in range(3):
        rim_wait(g, "send")


def hand_on(sol_in, hess_in, sol_out, hess_out):
    sol_out[...] = sol_in[...]
    hess_out[...] = hess_in[...]


def solution(mesh):
    nx, ny = mesh.shape["gx"], mesh.shape["gy"]

    def body(rhs, diag, lift, state, basis, cinv):
        ti, tj, n = rhs.shape
        kc = basis.shape[1]
        cflat = jnp.transpose(cinv, (0, 2, 3, 1)).reshape(ti, kc * kc, tj)
        sflat = jnp.transpose(state, (0, 2, 1))
        hrows = 2 * tj + 4 * ti + 32
        h = 2 * ti + 2 * tj
        vm = pl.BlockSpec(memory_space=pltpu.VMEM)
        hbm = pl.BlockSpec(memory_space=pltpu.HBM)
        sol, hess = pl.pallas_call(
            functools.partial(kernel, nx, ny, ti, tj, n, kc),
            out_shape=(jax.ShapeDtypeStruct((ti, tj, n), F32), jax.ShapeDtypeStruct((2, 3), F32)),
            in_specs=[hbm] * 6,
            out_specs=(vm, vm),
            scratch_shapes=[
                pltpu.VMEM((ti, tj, n), F32),
                pltpu.VMEM((4, n, n), BF16),
                pltpu.VMEM((ti, 4, tj), jnp.int32),
                pltpu.VMEM((kc, n), F32),
                pltpu.VMEM((ti, kc * kc, tj), F32),
                pltpu.VMEM((ti, tj, n, n), BF16),
                pltpu.VMEM((8 * n, n), BF16),
                pltpu.VMEM((8, ti * tj, n), F32),
                pltpu.VMEM((ti * tj + h, n), F32),
                pltpu.VMEM((ti, tj, n), F32),
                pltpu.VMEM((2, hrows, n), F32),
                pltpu.VMEM((2, hrows, n), F32),
                pltpu.VMEM((h, n), F32),
                pltpu.VMEM((h, n), F32),
                pltpu.VMEM((2, 3 * ny, 1, n), F32),
                pltpu.VMEM((nx * ny, 1, n), F32),
                pltpu.SemaphoreType.DMA((5,)),
                pltpu.SemaphoreType.DMA((ti,)),
                pltpu.SemaphoreType.DMA((3, 8)),
                pltpu.SemaphoreType.DMA((3, 8)),
                pltpu.SemaphoreType.DMA((2, 3)),
                pltpu.SemaphoreType.DMA((2, 3)),
                pltpu.SemaphoreType.DMA((1,)),
                pltpu.SemaphoreType.DMA((1,)),
                pltpu.SemaphoreType.REGULAR((max(1, nx.bit_length()),)),
            ],
            compiler_params=pltpu.CompilerParams(collective_id=0, has_side_effects=True,
                                                 vmem_limit_bytes=30000 * 1024),
        )(*[pltpu.with_memory_space_constraint(x, pltpu.HBM) for x in (rhs, diag, lift, sflat, basis.T, cflat)])
        sol, hess = pl.pallas_call(
            hand_on,
            out_shape=(jax.ShapeDtypeStruct(sol.shape, F32), jax.ShapeDtypeStruct(hess.shape, F32)),
            in_specs=[vm, vm],
            out_specs=(vm, vm),
            compiler_params=pltpu.CompilerParams(vmem_limit_bytes=30000 * 1024),
        )(sol, hess)
        return sol, hess.T

    in_specs = (P("gx", "gy", None), P("gx", "gy", None, None), P(), P("gx", "gy", None), P(),
                P("gx", "gy", None, None))
    return jax.shard_map(body, mesh=mesh, in_specs=in_specs, out_specs=(P("gx", "gy", None), P()), check_vma=False)
```

```python
import functools
import jax
import jax.numpy as jnp
from jax import lax
from jax.experimental import pallas as pl
from jax.experimental.pallas import tpu as pltpu
from jax.sharding import PartitionSpec as P

MESH = pl.DeviceIdType.MESH
F32 = jnp.float32
BF16 = jnp.bfloat16


def fdot(a, b):
    return jnp.dot(a, b, preferred_element_type=F32)


def over_first(a, b):
    return lax.dot_general(a, b, (((0,), (0,)), ((), ())), preferred_element_type=F32)


def cut(x):
    hi = x.astype(BF16)
    return hi, (x - hi.astype(F32)).astype(BF16)


def fine_dot(x, w):
    hi, lo = cut(x)
    return fdot(jnp.concatenate([hi, lo, hi], axis=1), w)


def one_hot(x):
    return x.astype(F32).astype(BF16)


def total(x):
    return jnp.sum(jnp.sum(x, axis=0, keepdims=True), axis=1, keepdims=True)


def safe_div(a, b):
    return jnp.where(b > 0, a / jnp.where(b > 0, b, 1.0), 0.0)


def iota(shape, dim):
    return lax.broadcasted_iota(jnp.int32, shape, dim)


def kernel(nx, ny, ti, tj, n, kc, rhs_h, diag, lift_h, state_h, basis_h, cinv_h, out, hess_out,
           rhs, lift, state, basis, cinv,
           dvm, wts, cwts, wmat, masks, packs, rims, cext, pbuf, zbuf, cbuf, fbuf, gbuf, wbuf, sends, halos, csend, chalo, sums, msgs,
           isem, dsem, ssem, rsem, lsend, lrecv, msend, mrecv, know):
    gx = lax.axis_index("gx")
    gy = lax.axis_index("gy")
    me = gx * ny + gy
    count = nx * ny
    elems = ti * tj
    kk = kc * kc

    loads = [pltpu.make_async_copy(a, b, isem.at[q]) for q, (a, b) in enumerate(
        ((rhs_h, rhs), (basis_h, basis), (cinv_h, cinv), (state_h, state), (lift_h, lift)))]
    for c in loads:
        c.start()
    dcopies = [pltpu.make_async_copy(diag.at[q], dvm.at[q], dsem.at[q]) for q in range(ti)]
    for c in dcopies:
        c.start()

    barrier = pltpu.get_barrier_semaphore()

    has_n, has_s, has_w, has_e = gx > 0, gx < nx - 1, gy > 0, gy < ny - 1
    n_i, s_i, w_i, e_i = [v.astype(jnp.int32) for v in (has_n, has_s, has_w, has_e)]
    near = [(has_n, -1, k) for k in range(ny)] + [(has_s, 1, k) for k in range(ny)] + [
        (None, 0, k) for k in range(1, ny)]
    near_count = ny - 1 + ny * (n_i + s_i)

    def when(ok, run):
        if ok is None:
            run()
        else:
            pl.when(ok)(run)

    sums[...] = jnp.zeros_like(sums)
    for ok, d, k in near:
        def hello(d=d, k=k):
            pl.semaphore_signal(barrier, inc=1, device_id=(gx + d, lax.rem(gy + k, ny)), device_id_type=MESH)
        when(ok, hello)

    steps = []
    r = 2
    while r < nx - 1:
        steps.append(r)
        r *= 2

    def tell(q):
        r = steps[q]
        for ok, d in ((gx >= r, -r), (gx + r < nx, r)):
            def one(d=d):
                pl.semaphore_signal(know.at[q], inc=1, device_id=(gx + d, gy), device_id_type=MESH)
            when(ok, one)

    def learn(q):
        r = steps[q]
        amount = (gx >= r).astype(jnp.int32) + (gx + r < nx).astype(jnp.int32)
        pl.semaphore_wait(know.at[q], amount)

    def line_copy(g, d, k):
        return pltpu.make_async_remote_copy(
            src_ref=sums.at[g, ny + gy], dst_ref=sums.at[g, (1 - d) * ny + gy],
            send_sem=lsend.at[g, d + 1], recv_sem=lrecv.at[g, 1 - d],
            device_id=(gx + d, lax.rem(gy + k, ny)), device_id_type=MESH)

    def share_lines(g):
        for ok, d, k in near:
            when(ok, lambda d=d, k=k: line_copy(g, d, k).start())

    def line_wait(g, which):
        for ok, d in ((has_n, -1), (has_s, 1), (None, 0)):
            def one(d=d):
                part = sums.at[g, pl.ds((d + 1) * ny, ny if d else ny - 1)]
                c = pltpu.make_async_remote_copy(
                    src_ref=part, dst_ref=part, send_sem=lsend.at[g, d + 1], recv_sem=lrecv.at[g, d + 1],
                    device_id=(gx, gy), device_id_type=MESH)
                if which == "send":
                    c.wait_send()
                else:
                    c.wait_recv()
            when(ok, one)

    h = 2 * ti + 2 * tj
    o_n, o_s, o_w, o_e = 0, tj, 2 * tj, 2 * tj + 2 * ti
    o_nw = 2 * tj + 4 * ti
    o_ne, o_sw, o_se = o_nw + 8, o_nw + 16, o_nw + 24
    hrows = o_nw + 32
    routes = [
        (has_n, (gx - 1, gy), o_n, o_s, tj),
        (has_s, (gx + 1, gy), o_s, o_n, tj),
        (has_w, (gx, gy - 1), o_w, o_e, 2 * ti),
        (has_e, (gx, gy + 1), o_e, o_w, 2 * ti),
        (jnp.logical_and(has_n, has_w), (gx - 1, gy - 1), o_nw, o_se, 8),
        (jnp.logical_and(has_n, has_e), (gx - 1, gy + 1), o_ne, o_sw, 8),
        (jnp.logical_and(has_s, has_w), (gx + 1, gy - 1), o_sw, o_ne, 8),
        (jnp.logical_and(has_s, has_e), (gx + 1, gy + 1), o_se, o_nw, 8),
    ]
    croutes = [
        (has_n, (gx - 1, gy), 0, tj, tj),
        (has_s, (gx + 1, gy), tj, 0, tj),
        (has_w, (gx, gy - 1), 2 * tj, 2 * tj + ti, ti),
        (has_e, (gx, gy + 1), 2 * tj + ti, 2 * tj, ti),
    ]
    opposite = [1, 0, 3, 2, 7, 6, 5, 4]

    def rim_copies(g):
        return [(ok, pltpu.make_async_remote_copy(
            src_ref=sends.at[g, pl.ds(src, rows)], dst_ref=halos.at[g, pl.ds(dst, rows)],
            send_sem=ssem.at[g, d], recv_sem=rsem.at[g, opposite[d]],
            device_id=dev, device_id_type=MESH)) for d, (ok, dev, src, dst, rows) in enumerate(routes)]

    def coarse_copies():
        return [(ok, pltpu.make_async_remote_copy(
            src_ref=csend.at[pl.ds(src, rows)], dst_ref=chalo.at[pl.ds(dst, rows)],
            send_sem=ssem.at[2, d], recv_sem=rsem.at[2, opposite[d]],
            device_id=dev, device_id_type=MESH)) for d, (ok, dev, src, dst, rows) in enumerate(croutes)]

    def rim_wait(g, which):
        table = routes if g < 2 else croutes
        for d, (ok, dev, src, dst, rows) in enumerate(table):
            @pl.when(ok)
            def _(d=d, dev=dev, src=src, rows=rows):
                if g < 2:
                    s, r = sends.at[g, pl.ds(src, rows)], halos.at[g, pl.ds(src, rows)]
                else:
                    s, r = csend.at[pl.ds(src, rows)], chalo.at[pl.ds(src, rows)]
                c = pltpu.make_async_remote_copy(
                    src_ref=s, dst_ref=r, send_sem=ssem.at[g, d], recv_sem=rsem.at[g, d],
                    device_id=dev, device_id_type=MESH)
                if which == "send":
                    c.wait_send()
                else:
                    c.wait_recv()

    def start_all(copies):
        for ok, c in copies:
            @pl.when(ok)
            def _(c=c):
                c.start()

    def broadcast():
        for dx in sorted(range(nx), key=lambda d: abs(d - nx // 2)):
            for dy in range(ny):
                if dx or dy:
                    pltpu.make_async_remote_copy(
                        src_ref=msgs.at[me], dst_ref=msgs.at[me], send_sem=msend.at[0], recv_sem=mrecv.at[0],
                        device_id=(lax.rem(gx + dx, nx), lax.rem(gy + dy, ny)), device_id_type=MESH).start()

    def bc_wait(which):
        part = msgs.at[pl.ds(0, count - 1)]
        c = pltpu.make_async_remote_copy(
            src_ref=part, dst_ref=part, send_sem=msend.at[0], recv_sem=mrecv.at[0],
            device_id=(gx, gy), device_id_type=MESH)
        if which == "send":
            c.wait_send()
        else:
            c.wait_recv()

    def fill_sends(g, ref):
        sends[g, o_n:o_n + tj] = ref[0]
        sends[g, o_s:o_s + tj] = ref[ti - 1]
        sends[g, o_w:o_w + ti] = ref[:, 0, :]
        sends[g, o_w + ti:o_w + 2 * ti] = ref[:, 1, :]
        sends[g, o_e:o_e + ti] = ref[:, tj - 1, :]
        sends[g, o_e + ti:o_e + 2 * ti] = ref[:, tj - 2, :]
        sends[g, o_nw:o_nw + 8] = jnp.broadcast_to(ref[0, 0:1, :], (8, n))
        sends[g, o_ne:o_ne + 8] = jnp.broadcast_to(ref[0, tj - 1:tj, :], (8, n))
        sends[g, o_sw:o_sw + 8] = jnp.broadcast_to(ref[ti - 1, 0:1, :], (8, n))
        sends[g, o_se:o_se + 8] = jnp.broadcast_to(ref[ti - 1, tj - 1:tj, :], (8, n))

    lane1 = iota((1, n), 1)

    def message(values):
        row = jnp.zeros((1, n), F32)
        for p, v in enumerate(values):
            row = jnp.where(lane1 == p, v, row)
        return row

    row_k = lax.rem(iota((kc, n), 1), kk) // kc == iota((kc, n), 0)
    row_l = lax.rem(iota((kc, n), 1), kc) == iota((kc, n), 0)
    pick = iota((ti, n), 1) // kc == iota((ti, n), 0)
    low = lane1 < kk
    loads[0].wait()
    loads[1].wait()
    Rh, Rl = cut(basis[...])

    def spreads(pattern):
        e = one_hot(pattern)
        return over_first(Rh, e).astype(BF16), over_first(Rl, e).astype(BF16)

    def stacked(hi, lo):
        return jnp.concatenate([hi, hi, lo], axis=0)
    RT = stacked(*spreads(row_l))
    rhs3 = rhs[...]
    rhs2 = rhs3.reshape(elems, n)

    def packed_rowsum(f3):
        rows = fine_dot(jnp.sum(f3, axis=1), RT)
        return jnp.sum(jnp.where(pick, rows, 0.0), axis=0, keepdims=True)

    fill_sends(0, rhs)
    sums[0, ny + gy] = packed_rowsum(rhs3)
    loads[2].wait()
    eye = one_hot(iota((tj, tj), 0) == iota((tj, tj), 1))
    chi, clo = cut(cinv[...])
    both = jnp.concatenate([chi, clo], axis=2)
    both = jnp.concatenate([both, both], axis=1).reshape(ti * n, 2 * tj)
    turned = lax.dot_general(jnp.concatenate([eye, eye], axis=1), both, (((1,), (1,)), ((), ())),
                             preferred_element_type=F32)
    for q in range(ti):
        cext[q * tj:(q + 1) * tj] = turned[:, q * n:(q + 1) * n]
    c3d = cext[0:elems].reshape(ti, tj, n)
    csend[0:tj] = c3d[0]
    csend[tj:2 * tj] = c3d[ti - 1]
    csend[2 * tj:2 * tj + ti] = c3d[:, 0, :]
    csend[2 * tj + ti:2 * tj + 2 * ti] = c3d[:, tj - 1, :]

    pl.semaphore_wait(barrier, near_count)
    start_all(rim_copies(0))
    share_lines(0)
    start_all(coarse_copies())

    RE = stacked(*spreads(row_k))
    row_le = one_hot(row_l)
    RFh, RFl = over_first(row_le, Rh).astype(BF16), over_first(row_le, Rl).astype(BF16)
    low_row = iota((n, n), 0) < kk
    RF = jnp.concatenate([RFh, jnp.where(low_row, RFl.astype(F32), 0.0).astype(BF16)], axis=0)
    G = one_hot(lax.rem(iota((n, n), 0), kc) == lax.rem(iota((n, n), 1), kk) // kc)
    G = jnp.concatenate([G, G], axis=0)
    Q = one_hot(lax.rem(iota((n, n), 0), kc) == lax.rem(iota((n, n), 1), kc))
    flip = one_hot(iota((n, n), 0) + iota((n, n), 1) == n - 1)
    RR = jnp.concatenate([RFh, RFl], axis=1)
    loads[4].wait()
    for f in range(4):
        straight = lift[f]
        turned = fdot(flip, straight).astype(BF16)
        wts[2 * f * n:(2 * f + 1) * n] = straight
        wts[(2 * f + 1) * n:(2 * f + 2) * n] = turned
        pair = jnp.concatenate([straight, turned], axis=1)
        prod = fdot(RR, jnp.concatenate([pair, pair], axis=0))
        cwts[f * n:(f + 1) * n] = jnp.where(low_row, prod[:, 0:n], prod[:, n:2 * n]).astype(BF16)
    loads[3].wait()
    own_j = lax.rem(iota((elems, tj), 0), tj) == iota((elems, tj), 1)
    ones = jnp.ones((tj, n), BF16)
    for f in range(4):
        rows = state[:, f, :].astype(F32)
        wide = jnp.broadcast_to(rows[:, None, :], (ti, tj, tj)).reshape(elems, tj)
        col = fdot(jnp.where(own_j, wide, 0.0).astype(BF16), ones)
        masks[2 * f] = one_hot(col == 1.0)
        masks[2 * f + 1] = one_hot(col == 2.0)
        packs[f] = (col == jnp.where(low, 1.0, 2.0)).astype(F32)
        if f >= 2:
            edge = col.reshape(ti, tj, n)[:, 0 if f == 2 else tj - 1, :]
            rims[2 * f - 4] = one_hot(edge == 1.0)
            rims[2 * f - 3] = one_hot(edge == 2.0)

    hrow = iota((hrows, 1), 0)
    valid = jnp.where(hrow < o_s, n_i, jnp.where(hrow < o_w, s_i, jnp.where(
        hrow < o_e, w_i, jnp.where(hrow < o_nw, e_i, jnp.where(
            hrow < o_ne, n_i * w_i, jnp.where(hrow < o_sw, n_i * e_i, jnp.where(
                hrow < o_se, s_i * w_i, s_i * e_i))))))) > 0
    ok_rim = jnp.concatenate([valid[o_n:o_w], valid[o_w:o_w + ti], valid[o_e:o_e + ti]], axis=0)

    jrow = lax.rem(iota((elems, 1), 0), tj)
    trow = iota((tj, 1), 0)
    inner = 1.0 + 0.25 * ((jrow > 0).astype(F32) + (jrow < tj - 1).astype(F32))

    def spread(col):
        return jnp.broadcast_to(col[:, None, :], (ti, tj, n)).reshape(elems, n)

    def left_of(x, edge):
        return jnp.where(jrow == 0, edge, pltpu.roll(x, 1, 0))

    def right_of(x, edge):
        return jnp.where(jrow == tj - 1, edge, pltpu.roll(x, elems - 1, 0))

    def line_sum(g, d):
        acc = sums[g, (d + 1) * ny]
        for q in range(1, ny):
            acc = acc + sums[g, (d + 1) * ny + q]
        return acc

    half = tj // 2
    keep = [one_hot(lax.rem(iota((2 * tj, n), 0), half) == t) for t in range(half)]
    none = jnp.zeros((kc, n), BF16)
    coarse_rows = jnp.concatenate([
        jnp.concatenate([Rh, none], axis=1), jnp.concatenate([none, Rh], axis=1)], axis=0)
    own_block = (iota((tj, n), 1) // kc == iota((tj, n), 0)).astype(F32)

    def local_lifts(x):
        b = x.astype(BF16)
        gap = jnp.zeros((tj, n), BF16)
        nb = [
            jnp.concatenate([gap, b[0:elems - tj]], axis=0),
            jnp.concatenate([b[tj:], gap], axis=0),
            left_of(x, 0.0).astype(BF16),
            right_of(x, 0.0).astype(BF16),
        ]
        cols = []
        for f in range(4):
            cols.append(nb[f] * masks[2 * f])
            cols.append(nb[f] * masks[2 * f + 1])
        wbuf[...] = fdot(jnp.concatenate(cols, axis=1), wts[...]).reshape(ti, tj, n)

    def local_blocks(x, first):
        for q in range(ti):
            if first:
                dcopies[q].wait()
            both = jnp.concatenate(cut(x[q * tj:(q + 1) * tj]), axis=0)
            rhs_w = jnp.concatenate(
                [dvm[q, 0:half].reshape(half * n, n), dvm[q, half:tj].reshape(half * n, n)], axis=1)
            if first:
                prod = None
                for t in range(0, half, 2):
                    lhs = jnp.concatenate([
                        jnp.concatenate([both * keep[t], both * keep[t + 1]], axis=1), coarse_rows], axis=0)
                    part = fdot(lhs, rhs_w[t * n:(t + 2) * n])
                    prod = part[0:2 * tj] if prod is None else prod + part[0:2 * tj]
                    for side in range(2):
                        at = (side * half + t) * kc
                        hi, lo = cut(part[2 * tj:, side * n:(side + 1) * n])
                        wmat[q, at:at + 2 * kc, 0:n] = hi
                        wmat[q, at:at + 2 * kc, n:2 * n] = lo
            else:
                prod = fdot(jnp.concatenate([both * keep[t] for t in range(half)], axis=1), rhs_w)
            prod = prod[0:tj] + prod[tj:2 * tj]
            wbuf[q] += jnp.concatenate([prod[0:half, 0:n], prod[half:tj, n:2 * n]], axis=0)

    def local_coarse(x):
        c = fine_dot(x, RE)
        cbuf[...] = c + 0.25 * (left_of(c, 0.0) + right_of(c, 0.0))
        c3 = c.reshape(ti, tj, n)
        return c3[:, 0, :], c3[:, tj - 1, :]

    def fix(g, own_w, own_e):
        p_c, p_n, p_s = line_sum(g, 0), line_sum(g, -1), line_sum(g, 1)
        f_halo = jnp.where(valid, halos[g], 0.0)
        stack = jnp.concatenate([
            jnp.where(pick, jnp.broadcast_to(p_c, (ti, n)), 0.0),
            jnp.broadcast_to(jnp.where(lane1 // kc == ti - 1, p_n, 0.0), (8, n)),
            jnp.broadcast_to(jnp.where(lane1 // kc == 0, p_s, 0.0), (8, n))], axis=0)
        mean = fdot(jnp.concatenate(cut(stack), axis=1), G) * (1.0 / (ny * tj))
        m_c, m_n, m_s = mean[0:ti], mean[ti:ti + 1], mean[ti + 8:ti + 9]
        m_halo = jnp.concatenate([
            jnp.broadcast_to(m_n, (tj, n)), jnp.broadcast_to(m_s, (tj, n)), m_c, m_c, m_c, m_c,
            jnp.broadcast_to(m_n, (16, n)), jnp.broadcast_to(m_s, (16, n))], axis=0)
        c_halo = jnp.where(valid, fine_dot(f_halo, RE) - m_halo, 0.0)
        c_w1, c_w2 = c_halo[o_w:o_w + ti], c_halo[o_w + ti:o_e]
        c_e1, c_e2 = c_halo[o_e:o_e + ti], c_halo[o_e + ti:o_nw]
        c_n, c_s = c_halo[o_n:o_n + tj], c_halo[o_s:o_s + tj]

        def row_smooth(x, lo, hi):
            left = jnp.where(trow == 0, lo, pltpu.roll(x, 1, 0))
            right = jnp.where(trow == tj - 1, hi, pltpu.roll(x, tj - 1, 0))
            return x + 0.25 * (left + right)
        s_n = row_smooth(c_n, c_halo[o_nw:o_nw + 1], c_halo[o_ne:o_ne + 1])
        s_s = row_smooth(c_s, c_halo[o_sw:o_sw + 1], c_halo[o_se:o_se + 1])
        s_w = c_w1 + 0.25 * (c_w2 + own_w - m_c)
        s_e = c_e1 + 0.25 * (own_e - m_c + c_e2)
        s_own = cbuf[...] - inner * spread(m_c)
        s_own = s_own + jnp.where(jrow == 0, spread(0.25 * c_w1), 0.0) + jnp.where(
            jrow == tj - 1, spread(0.25 * c_e1), 0.0)
        p = s_own * cext[0:elems]
        pbuf[g] = p
        s_rim = jnp.concatenate([s_n, s_s, s_w, s_e], axis=0)
        p_rim = jnp.where(ok_rim, s_rim * cext[elems:elems + h], 0.0)

        hi, lo = cut(p)
        coef = fdot(jnp.where(low, hi.astype(F32), lo.astype(F32)).astype(BF16), Q)
        nb = [
            jnp.concatenate([p_rim[0:tj], p[0:elems - tj]], axis=0),
            jnp.concatenate([p[tj:], p_rim[tj:2 * tj]], axis=0),
            left_of(p, spread(p_rim[2 * tj:2 * tj + ti])),
            right_of(p, spread(p_rim[2 * tj + ti:2 * tj + 2 * ti])),
        ]
        cols = [(nb[f] * packs[f]).astype(BF16) for f in range(4)]
        lifted = fdot(jnp.concatenate(cols, axis=1), cwts[...])

        def rim_lift(f, at, one, two):
            b = f_halo[at:at + 16].astype(BF16)
            return fdot(jnp.concatenate([b * one, b * two], axis=1), wts[2 * f * n:(2 * f + 2) * n])
        last = elems - tj
        north = rim_lift(0, o_n, masks[0, 0:tj], masks[1, 0:tj])
        south = rim_lift(1, o_s, masks[2, last:elems], masks[3, last:elems])
        west = rim_lift(2, o_w, rims[0], rims[1])
        east = rim_lift(3, o_e, rims[2], rims[3])
        for q in range(ti):
            at = slice(q * tj, (q + 1) * tj)
            x = jnp.concatenate(cut(coef[at] * own_block), axis=1)
            w = wmat[q]
            y = fdot(x, jnp.concatenate([w, w], axis=0))
            y = y[:, 0:n] + y[:, n:2 * n] + lifted[at]
            if q == 0:
                y = y + north
            if q == ti - 1:
                y = y + south
            side = jnp.where(trow == 0, west[q:q + 1], jnp.where(trow == tj - 1, east[q:q + 1], 0.0))
            wbuf[q] += y + side

    def full(g, x):
        hi, lo = cut(pbuf[g])
        mixed = jnp.where(low, hi.astype(F32), lo.astype(F32)).astype(BF16)
        zbuf[g] = x + fdot(jnp.concatenate([mixed, hi], axis=1), RF)

    edges = local_coarse(rhs2)
    local_lifts(rhs2)
    local_blocks(rhs2, True)
    line_wait(0, "recv")
    rim_wait(0, "recv")
    rim_wait(2, "recv")
    if steps:
        tell(0)

    cext[elems:elems + h] = chalo[...]
    fix(0, *edges)
    fill_sends(1, wbuf)
    start_all(rim_copies(1))
    sums[1, ny + gy] = packed_rowsum(wbuf[...])
    share_lines(1)
    w1 = wbuf[...].reshape(elems, n)
    fbuf[...] = w1
    for q in range(len(steps)):
        learn(q)
        if q + 1 < len(steps):
            tell(q + 1)
    edges = local_coarse(w1)
    local_lifts(w1)
    local_blocks(w1, False)
    own_n1 = total(rhs2 * rhs2)
    p_one = safe_div(total(rhs2 * w1), own_n1)
    gap = w1 - p_one * rhs2
    gbuf[...] = gap
    own_n2 = total(gap * gap)
    line_wait(1, "recv")
    rim_wait(1, "recv")

    fix(1, *edges)
    w2 = wbuf[...].reshape(elems, n)
    rhs2, gap = rhs[...].reshape(elems, n), gbuf[...]
    p_two = safe_div(total(rhs2 * w2), own_n1)
    q_two = safe_div(total(gap * w2), own_n2)
    rest = w2 - p_two * rhs2 - q_two * gap
    msgs[me] = message([own_n1, p_one, own_n2, p_two, q_two, total(rest * rest)])
    broadcast()
    full(0, rhs2)
    full(1, fbuf[...])
    bc_wait("recv")
    Y = msgs[:, 0, :]
    l_n1, l_p, l_n2, l_a, l_b, l_n3 = [Y[:, q:q + 1] for q in range(6)]

    def over(x):
        return jnp.sum(x, axis=0, keepdims=True)
    len2 = over(l_n1)
    start_len = jnp.sqrt(len2)
    h11 = over(l_p * l_n1) / len2
    dev = l_p - h11
    gap2 = over(dev * dev * l_n1 + l_n2)
    gap_len = jnp.sqrt(gap2)
    h21 = gap_len / start_len
    e_one = l_a - h11 * l_p
    e_two = l_b - h11
    t12 = over(e_one * l_n1) / len2
    h12 = t12 * start_len / gap_len
    h22 = over(dev * e_one * l_n1 + e_two * l_n2) / gap2
    g_one = e_one - t12 - h22 * dev
    g_two = e_two - h22
    h32 = jnp.sqrt(over(g_one * g_one * l_n1 + g_two * g_two * l_n2 + l_n3)) / gap_len

    first = jnp.sqrt(h11 * h11 + h21 * h21)
    cos_one = h11 / first
    sin_one = h21 / first
    upper = cos_one * h12 + sin_one * h22
    lower = -sin_one * h12 + cos_one * h22
    second = jnp.sqrt(lower * lower + h32 * h32)
    cos_two = lower / second
    y2 = cos_two * (-sin_one * start_len) / second
    y1 = (cos_one * start_len - upper * y2) / first
    c2 = y2 / gap_len
    c1 = y1 / start_len - c2 * h11
    out[...] = (c1 * zbuf[0] + c2 * zbuf[1]).reshape(ti, tj, n)
    hr, hc = iota((2, 3), 1), iota((2, 3), 0)
    hess_out[...] = jnp.where(
        hr == 0, jnp.where(hc == 0, h11, h12),
        jnp.where(hr == 1, jnp.where(hc == 0, h21, h22), jnp.where(hc == 0, 0.0, h32)))

    bc_wait("send")
    for g in range(2):
        line_wait(g, "send")
    for g in range(3):
        rim_wait(g, "send")


def hand_on(sol_in, hess_in, sol_out, hess_out):
    sol_out[...] = sol_in[...]
    hess_out[...] = hess_in[...]


def solution(mesh):
    nx, ny = mesh.shape["gx"], mesh.shape["gy"]

    def body(rhs, diag, lift, state, basis, cinv):
        ti, tj, n = rhs.shape
        kc = basis.shape[1]
        cflat = jnp.transpose(cinv, (0, 2, 3, 1)).reshape(ti, kc * kc, tj)
        sflat = jnp.transpose(state, (0, 2, 1))
        hrows = 2 * tj + 4 * ti + 32
        h = 2 * ti + 2 * tj
        vm = pl.BlockSpec(memory_space=pltpu.VMEM)
        hbm = pl.BlockSpec(memory_space=pltpu.HBM)
        sol, hess = pl.pallas_call(
            functools.partial(kernel, nx, ny, ti, tj, n, kc),
            out_shape=(jax.ShapeDtypeStruct((ti, tj, n), F32), jax.ShapeDtypeStruct((2, 3), F32)),
            in_specs=[hbm] * 6,
            out_specs=(vm, vm),
            scratch_shapes=[
                pltpu.VMEM((ti, tj, n), F32),
                pltpu.VMEM((4, n, n), BF16),
                pltpu.VMEM((ti, 4, tj), jnp.int32),
                pltpu.VMEM((kc, n), F32),
                pltpu.VMEM((ti, kc * kc, tj), F32),
                pltpu.VMEM((ti, tj, n, n), BF16),
                pltpu.VMEM((8 * n, n), BF16),
                pltpu.VMEM((4 * n, n), BF16),
                pltpu.VMEM((ti, tj * kc, 2 * n), BF16),
                pltpu.VMEM((8, ti * tj, n), BF16),
                pltpu.VMEM((4, ti * tj, n), F32),
                pltpu.VMEM((4, ti, n), BF16),
                pltpu.VMEM((ti * tj + h, n), F32),
                pltpu.VMEM((2, ti * tj, n), F32),
                pltpu.VMEM((2, ti * tj, n), F32),
                pltpu.VMEM((ti * tj, n), F32),
                pltpu.VMEM((ti * tj, n), F32),
                pltpu.VMEM((ti * tj, n), F32),
                pltpu.VMEM((ti, tj, n), F32),
                pltpu.VMEM((2, hrows, n), F32),
                pltpu.VMEM((2, hrows, n), F32),
                pltpu.VMEM((h, n), F32),
                pltpu.VMEM((h, n), F32),
                pltpu.VMEM((2, 3 * ny, 1, n), F32),
                pltpu.VMEM((nx * ny, 1, n), F32),
                pltpu.SemaphoreType.DMA((5,)),
                pltpu.SemaphoreType.DMA((ti,)),
                pltpu.SemaphoreType.DMA((3, 8)),
                pltpu.SemaphoreType.DMA((3, 8)),
                pltpu.SemaphoreType.DMA((2, 3)),
                pltpu.SemaphoreType.DMA((2, 3)),
                pltpu.SemaphoreType.DMA((1,)),
                pltpu.SemaphoreType.DMA((1,)),
                pltpu.SemaphoreType.REGULAR((max(1, nx.bit_length()),)),
            ],
            compiler_params=pltpu.CompilerParams(collective_id=0, has_side_effects=True,
                                                 vmem_limit_bytes=30000 * 1024),
        )(*[pltpu.with_memory_space_constraint(x, pltpu.HBM) for x in (rhs, diag, lift, sflat, basis.T, cflat)])
        sol, hess = pl.pallas_call(
            hand_on,
            out_shape=(jax.ShapeDtypeStruct(sol.shape, F32), jax.ShapeDtypeStruct(hess.shape, F32)),
            in_specs=[vm, vm],
            out_specs=(vm, vm),
            compiler_params=pltpu.CompilerParams(vmem_limit_bytes=30000 * 1024),
        )(sol, hess)
        return sol, hess.T

    in_specs = (P("gx", "gy", None), P("gx", "gy", None, None), P(), P("gx", "gy", None), P(),
                P("gx", "gy", None, None))
    return jax.shard_map(body, mesh=mesh, in_specs=in_specs, out_specs=(P("gx", "gy", None), P()), check_vma=False)
```

```python
import functools
import jax
import jax.numpy as jnp
from jax import lax
from jax.experimental import pallas as pl
from jax.experimental.pallas import tpu as pltpu
from jax.sharding import PartitionSpec as P

MESH = pl.DeviceIdType.MESH
F32 = jnp.float32
BF16 = jnp.bfloat16


def fdot(a, b):
    return jnp.dot(a, b, preferred_element_type=F32)


def over_first(a, b):
    return lax.dot_general(a, b, (((0,), (0,)), ((), ())), preferred_element_type=F32)


def cut(x):
    hi = x.astype(BF16)
    return hi, (x - hi.astype(F32)).astype(BF16)


def fine_dot(x, w):
    hi, lo = cut(x)
    return fdot(jnp.concatenate([hi, lo, hi], axis=1), w)


def exact_dot(x, w):
    m = x.shape[0]
    y = fdot(jnp.concatenate(cut(x), axis=0), w)
    return y[0:m] + y[m:2 * m]


def small_dot(x, w):
    m, n = x.shape[0], w.shape[1] // 2
    y = fdot(jnp.concatenate(cut(x), axis=0), w)
    return y[0:m, 0:n] + y[m:2 * m, 0:n] + y[0:m, n:2 * n]


def one_hot(x):
    return x.astype(F32).astype(BF16)


def total(x):
    return jnp.sum(jnp.sum(x, axis=0, keepdims=True), axis=1, keepdims=True)


def safe_div(a, b):
    return jnp.where(b > 0, a / jnp.where(b > 0, b, 1.0), 0.0)


def iota(shape, dim):
    return lax.broadcasted_iota(jnp.int32, shape, dim)


def kernel(nx, ny, ti, tj, n, kc, rhs_h, diag, lift_h, state_h, basis_h, cinv_h, out, hess_out,
           rhs, lift, state, basis, cinv,
           dvm, wts, cwts, wmat, masks, packs, rims, cext, pbuf, zbuf, cbuf, fbuf, gbuf, wbuf, sends, halos, csend, chalo, sums, msgs,
           isem, dsem, ssem, rsem, lsend, lrecv, msend, mrecv, know):
    gx = lax.axis_index("gx")
    gy = lax.axis_index("gy")
    me = gx * ny + gy
    count = nx * ny
    elems = ti * tj
    kk = kc * kc

    barrier = pltpu.get_barrier_semaphore()

    has_n, has_s, has_w, has_e = gx > 0, gx < nx - 1, gy > 0, gy < ny - 1
    n_i, s_i, w_i, e_i = [v.astype(jnp.int32) for v in (has_n, has_s, has_w, has_e)]
    near = [(has_s, 1, k) for k in range(ny)] + [(None, 0, k) for k in range(1, ny)] + [
        (has_n, -1, k) for k in range(ny)]
    near_count = ny - 1 + ny * (n_i + s_i)

    def when(ok, run):
        if ok is None:
            run()
        else:
            pl.when(ok)(run)

    sums[...] = jnp.zeros_like(sums)
    halos[...] = jnp.zeros_like(halos)
    chalo[...] = jnp.zeros_like(chalo)
    for ok, d, k in near:
        def hello(d=d, k=k):
            pl.semaphore_signal(barrier, inc=1, device_id=(gx + d, lax.rem(gy + k, ny)), device_id_type=MESH)
        when(ok, hello)

    loads = [pltpu.make_async_copy(a, b, isem.at[q]) for q, (a, b) in enumerate(
        ((rhs_h, rhs), (basis_h, basis), (cinv_h, cinv), (state_h, state), (lift_h, lift)))]
    for c in loads:
        c.start()
    group = max(1, ti // 4)
    dcopies = [pltpu.make_async_copy(diag.at[pl.ds(q, group)], dvm.at[pl.ds(q, group)], dsem.at[q // group])
               for q in range(0, ti, group)]
    dcopies[0].start()

    steps = []
    r = 2
    while r < nx - 1:
        steps.append(r)
        r *= 2

    def tell(q):
        r = steps[q]
        for ok, d in ((gx >= r, -r), (gx + r < nx, r)):
            def one(d=d):
                pl.semaphore_signal(know.at[q], inc=1, device_id=(gx + d, gy), device_id_type=MESH)
            when(ok, one)

    def learn(q):
        r = steps[q]
        amount = (gx >= r).astype(jnp.int32) + (gx + r < nx).astype(jnp.int32)
        pl.semaphore_wait(know.at[q], amount)

    def line_copy(g, d, k):
        return pltpu.make_async_remote_copy(
            src_ref=sums.at[g, ny + gy], dst_ref=sums.at[g, (1 - d) * ny + gy],
            send_sem=lsend.at[g, d + 1], recv_sem=lrecv.at[g, 1 - d],
            device_id=(gx + d, lax.rem(gy + k, ny)), device_id_type=MESH)

    def share_lines(g):
        for ok, d, k in near:
            when(ok, lambda d=d, k=k: line_copy(g, d, k).start())

    def line_wait(g, which):
        for ok, d in ((has_n, -1), (has_s, 1), (None, 0)):
            def one(d=d):
                part = sums.at[g, pl.ds((d + 1) * ny, ny if d else ny - 1)]
                c = pltpu.make_async_remote_copy(
                    src_ref=part, dst_ref=part, send_sem=lsend.at[g, d + 1], recv_sem=lrecv.at[g, d + 1],
                    device_id=(gx, gy), device_id_type=MESH)
                if which == "send":
                    c.wait_send()
                else:
                    c.wait_recv()
            when(ok, one)

    h = 2 * ti + 2 * tj
    croutes = [
        (has_n, (gx - 1, gy), 0, tj, tj),
        (has_s, (gx + 1, gy), tj, 0, tj),
        (has_w, (gx, gy - 1), 2 * tj, 2 * tj + ti, ti),
        (has_e, (gx, gy + 1), 2 * tj + ti, 2 * tj, ti),
    ]
    opposite = [1, 0, 3, 2]

    def rim_copies(g):
        return [(ok, pltpu.make_async_remote_copy(
            src_ref=sends.at[g, pl.ds(src, rows)], dst_ref=halos.at[g, pl.ds(dst, rows)],
            send_sem=ssem.at[g, d], recv_sem=rsem.at[g, opposite[d]],
            device_id=dev, device_id_type=MESH)) for d, (ok, dev, src, dst, rows) in enumerate(croutes)]

    def coarse_copies():
        return [(ok, pltpu.make_async_remote_copy(
            src_ref=csend.at[pl.ds(src, rows)], dst_ref=chalo.at[pl.ds(dst, rows)],
            send_sem=ssem.at[2, d], recv_sem=rsem.at[2, opposite[d]],
            device_id=dev, device_id_type=MESH)) for d, (ok, dev, src, dst, rows) in enumerate(croutes)]

    def rim_wait(g, which):
        for d, (ok, dev, src, dst, rows) in enumerate(croutes):
            @pl.when(ok)
            def _(d=d, dev=dev, src=src, rows=rows):
                if g < 2:
                    s, r = sends.at[g, pl.ds(src, rows)], halos.at[g, pl.ds(src, rows)]
                else:
                    s, r = csend.at[pl.ds(src, rows)], chalo.at[pl.ds(src, rows)]
                c = pltpu.make_async_remote_copy(
                    src_ref=s, dst_ref=r, send_sem=ssem.at[g, d], recv_sem=rsem.at[g, d],
                    device_id=dev, device_id_type=MESH)
                if which == "send":
                    c.wait_send()
                else:
                    c.wait_recv()

    def start_all(copies):
        for ok, c in copies:
            @pl.when(ok)
            def _(c=c):
                c.start()

    def broadcast():
        for tx, ty in sorted(((x, y) for x in range(nx) for y in range(ny)), key=lambda t: t[0] // 2 + t[1] // 2 + t[1] % 2):
            @pl.when(jnp.logical_or(gx != tx, gy != ty))
            def _(tx=tx, ty=ty):
                pltpu.make_async_remote_copy(
                    src_ref=msgs.at[me], dst_ref=msgs.at[me], send_sem=msend.at[0], recv_sem=mrecv.at[0],
                    device_id=(tx, ty), device_id_type=MESH).start()

    def bc_wait(which):
        part = msgs.at[pl.ds(0, count - 1)]
        c = pltpu.make_async_remote_copy(
            src_ref=part, dst_ref=part, send_sem=msend.at[0], recv_sem=mrecv.at[0],
            device_id=(gx, gy), device_id_type=MESH)
        if which == "send":
            c.wait_send()
        else:
            c.wait_recv()

    def fill_sends(g, ref):
        sends[g, 0:tj] = ref[0].astype(BF16)
        sends[g, tj:2 * tj] = ref[ti - 1].astype(BF16)
        sends[g, 2 * tj:2 * tj + ti] = ref[:, 0, :].astype(BF16)
        sends[g, 2 * tj + ti:h] = ref[:, tj - 1, :].astype(BF16)

    lane1 = iota((1, n), 1)

    def message(values):
        row = jnp.zeros((1, n), F32)
        for p, v in enumerate(values):
            row = jnp.where(lane1 == p, v, row)
        return row

    row_k = lax.rem(iota((kc, n), 1), kk) // kc == iota((kc, n), 0)
    row_l = lax.rem(iota((kc, n), 1), kc) == iota((kc, n), 0)
    pick = iota((ti, n), 1) // kc == iota((ti, n), 0)
    pick_j = iota((tj, n), 1) // kc == iota((tj, n), 0)
    low = lane1 < kk
    loads[0].wait()
    loads[1].wait()
    Rh, Rl = cut(basis[...])

    def spreads(pattern):
        e = one_hot(pattern)
        return over_first(Rh, e).astype(BF16), over_first(Rl, e).astype(BF16)

    def stacked(hi, lo):
        return jnp.concatenate([hi, hi, lo], axis=0)
    RT = jnp.concatenate(spreads(row_l), axis=1)
    rhs3 = rhs[...]
    rhs2 = rhs3.reshape(elems, n)

    def fill_sums(g, ref):
        rows = jnp.concatenate([
            jnp.sum(ref[...], axis=1), ref[:, 0, :], ref[:, 1, :], ref[:, tj - 1, :], ref[:, tj - 2, :],
            ref[0], ref[ti - 1]], axis=0)
        rows = small_dot(rows, RT)
        for q in range(7):
            at, lanes, size = (q * ti, pick, ti) if q < 5 else (5 * ti + (q - 5) * tj, pick_j, tj)
            sums[g, ny + gy, q:q + 1] = jnp.sum(jnp.where(lanes, rows[at:at + size], 0.0), axis=0, keepdims=True)

    fill_sends(0, rhs)
    fill_sums(0, rhs)
    loads[2].wait()
    eye = one_hot(iota((tj, tj), 0) == iota((tj, tj), 1))
    chi, clo = cut(cinv[...])
    both = jnp.concatenate([chi, clo], axis=2)
    both = jnp.concatenate([both, both], axis=1).reshape(ti * n, 2 * tj)
    turned = lax.dot_general(jnp.concatenate([eye, eye], axis=1), both, (((1,), (1,)), ((), ())),
                             preferred_element_type=F32)
    for q in range(ti):
        cext[q * tj:(q + 1) * tj] = turned[:, q * n:(q + 1) * n]
    c3d = cext[0:elems].reshape(ti, tj, n)
    csend[0:tj] = c3d[0]
    csend[tj:2 * tj] = c3d[ti - 1]
    csend[2 * tj:2 * tj + ti] = c3d[:, 0, :]
    csend[2 * tj + ti:2 * tj + 2 * ti] = c3d[:, tj - 1, :]

    pl.semaphore_wait(barrier, near_count)
    start_all(rim_copies(0))
    share_lines(0)
    start_all(coarse_copies())

    for c in dcopies[1:]:
        c.start()
    RE = stacked(*spreads(row_k))
    row_le = one_hot(row_l)
    RFh, RFl = over_first(row_le, Rh).astype(BF16), over_first(row_le, Rl).astype(BF16)
    low_row = iota((n, n), 0) < kk
    RF = jnp.concatenate([RFh, jnp.where(low_row, RFl.astype(F32), 0.0).astype(BF16)], axis=0)
    G = one_hot(lax.rem(iota((n, n), 0), kc) == lax.rem(iota((n, n), 1), kk) // kc)
    Q = one_hot(lax.rem(iota((n, n), 0), kc) == lax.rem(iota((n, n), 1), kc))
    flip = one_hot(iota((n, n), 0) + iota((n, n), 1) == n - 1)
    RR = jnp.concatenate([RFh, RFl], axis=1)
    loads[4].wait()
    for f in range(4):
        straight = lift[f]
        turned = fdot(flip, straight).astype(BF16)
        wts[2 * f * n:(2 * f + 1) * n] = straight
        wts[(2 * f + 1) * n:(2 * f + 2) * n] = turned
        pair = jnp.concatenate([straight, turned], axis=1)
        prod = fdot(RR, jnp.concatenate([pair, pair], axis=0))
        cwts[f * n:(f + 1) * n] = jnp.where(low_row, prod[:, 0:n], prod[:, n:2 * n]).astype(BF16)
    loads[3].wait()
    own_j = lax.rem(iota((elems, tj), 0), tj) == iota((elems, tj), 1)
    ones = jnp.ones((tj, n), BF16)
    for f in range(4):
        rows = state[:, f, :].astype(F32)
        wide = jnp.broadcast_to(rows[:, None, :], (ti, tj, tj)).reshape(elems, tj)
        col = fdot(jnp.where(own_j, wide, 0.0).astype(BF16), ones)
        masks[2 * f] = one_hot(col == 1.0)
        masks[2 * f + 1] = one_hot(col == 2.0)
        packs[f] = (col == jnp.where(low, 1.0, 2.0)).astype(F32)
        if f >= 2:
            edge = col.reshape(ti, tj, n)[:, 0 if f == 2 else tj - 1, :]
            rims[2 * f - 4] = one_hot(edge == 1.0)
            rims[2 * f - 3] = one_hot(edge == 2.0)

    jrow = lax.rem(iota((elems, 1), 0), tj)
    trow = iota((tj, 1), 0)
    scale = 1.0 / (ny * tj)
    inner = 1.0 + 0.25 * ((jrow > 0).astype(F32) + (jrow < tj - 1).astype(F32))

    def spread(col):
        return jnp.broadcast_to(col[:, None, :], (ti, tj, n)).reshape(elems, n)

    def left_of(x, edge):
        return jnp.where(jrow == 0, edge, pltpu.roll(x, 1, 0))

    def right_of(x, edge):
        return jnp.where(jrow == tj - 1, edge, pltpu.roll(x, elems - 1, 0))

    def line_sum(g, d):
        acc = sums[g, (d + 1) * ny, 0:1]
        for q in range(1, ny):
            acc = acc + sums[g, (d + 1) * ny + q, 0:1]
        return acc

    def part_of(g, dx, dy, row):
        at = (dx + 1) * ny + jnp.clip(gy + dy, 0, ny - 1)
        return sums[g, at, row:row + 1]

    half = tj // 2
    keep = [one_hot(lax.rem(iota((2 * tj, n), 0), half) == t) for t in range(half)]
    none = jnp.zeros((kc, n), BF16)
    coarse_rows = jnp.concatenate([
        jnp.concatenate([Rh, none], axis=1), jnp.concatenate([none, Rh], axis=1)], axis=0)
    own_block = (iota((tj, n), 1) // kc == iota((tj, n), 0)).astype(F32)

    def local_lifts(x):
        b = x.astype(BF16)
        gap = jnp.zeros((tj, n), BF16)
        nb = [
            jnp.concatenate([gap, b[0:elems - tj]], axis=0),
            jnp.concatenate([b[tj:], gap], axis=0),
            left_of(x, 0.0).astype(BF16),
            right_of(x, 0.0).astype(BF16),
        ]
        cols = []
        for f in range(4):
            cols.append(nb[f] * masks[2 * f])
            cols.append(nb[f] * masks[2 * f + 1])
        wbuf[...] = fdot(jnp.concatenate(cols, axis=1), wts[...]).reshape(ti, tj, n)

    def local_blocks(x, first):
        for q in range(ti):
            if first and q % group == 0:
                dcopies[q // group].wait()
            both = jnp.concatenate(cut(x[q * tj:(q + 1) * tj]), axis=0)
            rhs_w = jnp.concatenate(
                [dvm[q, 0:half].reshape(half * n, n), dvm[q, half:tj].reshape(half * n, n)], axis=1)
            if first:
                prod = None
                for t in range(0, half, 2):
                    lhs = jnp.concatenate([
                        jnp.concatenate([both * keep[t], both * keep[t + 1]], axis=1), coarse_rows], axis=0)
                    part = fdot(lhs, rhs_w[t * n:(t + 2) * n])
                    prod = part[0:2 * tj] if prod is None else prod + part[0:2 * tj]
                    for side in range(2):
                        at = (side * half + t) * kc
                        hi, lo = cut(part[2 * tj:, side * n:(side + 1) * n])
                        wmat[q, at:at + 2 * kc, 0:n] = hi
                        wmat[q, at:at + 2 * kc, n:2 * n] = lo
            else:
                prod = fdot(jnp.concatenate([both * keep[t] for t in range(half)], axis=1), rhs_w)
            prod = prod[0:tj] + prod[tj:2 * tj]
            wbuf[q] += jnp.concatenate([prod[0:half, 0:n], prod[half:tj, n:2 * n]], axis=0)

    def local_coarse(x):
        c = fine_dot(x, RE)
        cbuf[...] = c + 0.25 * (left_of(c, 0.0) + right_of(c, 0.0))
        c3 = c.reshape(ti, tj, n)
        return c3[:, 0, :], c3[:, tj - 1, :]

    def fix(g, own_w, own_e):
        group_of = lane1 // kc

        def lanes(x, mask):
            return jnp.where(mask, jnp.broadcast_to(x, mask.shape), 0.0)
        single = [
            (line_sum(g, -1), ti - 1), (line_sum(g, 1), 0),
            (part_of(g, -1, -1, 6), tj - 1), (part_of(g, -1, 1, 6), 0),
            (part_of(g, 1, -1, 5), tj - 1), (part_of(g, 1, 1, 5), 0)]
        srow = iota((8, n), 0)
        singles = jnp.zeros((8, n), F32)
        for q, (x, at) in enumerate(single):
            singles = jnp.where(jnp.logical_and(srow == q, group_of == at), jnp.broadcast_to(x, (8, n)), singles)
        stack = jnp.concatenate([
            lanes(line_sum(g, 0) * scale, pick),
            lanes(part_of(g, 0, -1, 3), pick), lanes(part_of(g, 0, -1, 4), pick),
            lanes(part_of(g, 0, 1, 1), pick), lanes(part_of(g, 0, 1, 2), pick),
            lanes(part_of(g, -1, 0, 6), pick_j), lanes(part_of(g, 1, 0, 5), pick_j), singles], axis=0)
        wide = exact_dot(stack, G)
        m_c, c_w1, c_w2, c_e1, c_e2 = [wide[q * ti:(q + 1) * ti] for q in range(5)]
        c_n, c_s = wide[5 * ti:5 * ti + tj], wide[5 * ti + tj:5 * ti + 2 * tj]
        one = wide[5 * ti + 2 * tj:]
        m_n, m_s = one[0:1] * scale, one[1:2] * scale
        c_nw, c_ne, c_sw, c_se = [one[q:q + 1] for q in range(2, 6)]
        w_f, e_f = w_i.astype(F32), e_i.astype(F32)
        c_w1, c_w2 = (c_w1 - m_c) * w_f, c_w2 - m_c
        c_e1, c_e2 = (c_e1 - m_c) * e_f, c_e2 - m_c
        c_n, c_s = c_n - m_n, c_s - m_s
        c_nw, c_sw = (c_nw - m_n) * w_f, (c_sw - m_s) * w_f
        c_ne, c_se = (c_ne - m_n) * e_f, (c_se - m_s) * e_f

        def row_smooth(x, lo, hi):
            left = jnp.where(trow == 0, lo, pltpu.roll(x, 1, 0))
            right = jnp.where(trow == tj - 1, hi, pltpu.roll(x, tj - 1, 0))
            return x + 0.25 * (left + right)
        s_n, s_s = row_smooth(c_n, c_nw, c_ne), row_smooth(c_s, c_sw, c_se)
        s_w = c_w1 + 0.25 * (c_w2 + own_w - m_c)
        s_e = c_e1 + 0.25 * (own_e - m_c + c_e2)
        s_own = cbuf[...] - inner * spread(m_c)
        s_own = s_own + jnp.where(jrow == 0, spread(0.25 * c_w1), 0.0) + jnp.where(
            jrow == tj - 1, spread(0.25 * c_e1), 0.0)
        p = s_own * cext[0:elems]
        pbuf[g] = p
        s_rim = jnp.concatenate([s_n, s_s, s_w, s_e], axis=0)
        p_rim = s_rim * cext[elems:elems + h]

        hi, lo = cut(p)
        coef = fdot(jnp.where(low, hi.astype(F32), lo.astype(F32)).astype(BF16), Q)
        nb = [
            jnp.concatenate([p_rim[0:tj], p[0:elems - tj]], axis=0),
            jnp.concatenate([p[tj:], p_rim[tj:2 * tj]], axis=0),
            left_of(p, spread(p_rim[2 * tj:2 * tj + ti])),
            right_of(p, spread(p_rim[2 * tj + ti:2 * tj + 2 * ti])),
        ]
        cols = [(nb[f] * packs[f]).astype(BF16) for f in range(4)]
        lifted = fdot(jnp.concatenate(cols, axis=1), cwts[...])

        def rim_lift(f, at, one, two):
            b = halos[g, at:at + one.shape[0]]
            return fdot(jnp.concatenate([b * one, b * two], axis=1), wts[2 * f * n:(2 * f + 2) * n])
        last = elems - tj
        north = rim_lift(0, 0, masks[0, 0:tj], masks[1, 0:tj])
        south = rim_lift(1, tj, masks[2, last:elems], masks[3, last:elems])
        west = rim_lift(2, 2 * tj, rims[0], rims[1])
        east = rim_lift(3, 2 * tj + ti, rims[2], rims[3])
        for q in range(ti):
            at = slice(q * tj, (q + 1) * tj)
            y = small_dot(coef[at] * own_block, wmat[q]) + lifted[at]
            if q == 0:
                y = y + north
            if q == ti - 1:
                y = y + south
            side = jnp.where(trow == 0, west[q:q + 1], jnp.where(trow == tj - 1, east[q:q + 1], 0.0))
            wbuf[q] += y + side

    def full(g, x):
        hi, lo = cut(pbuf[g])
        mixed = jnp.where(low, hi.astype(F32), lo.astype(F32)).astype(BF16)
        zbuf[g] = x + fdot(jnp.concatenate([mixed, hi], axis=1), RF)

    edges = local_coarse(rhs2)
    local_lifts(rhs2)
    local_blocks(rhs2, True)
    line_wait(0, "recv")
    rim_wait(0, "recv")
    rim_wait(2, "recv")
    if steps:
        tell(0)

    cext[elems:elems + h] = chalo[...]
    fix(0, *edges)
    fill_sends(1, wbuf)
    start_all(rim_copies(1))
    fill_sums(1, wbuf)
    share_lines(1)
    w1 = wbuf[...].reshape(elems, n)
    fbuf[...] = w1
    for q in range(len(steps)):
        learn(q)
        if q + 1 < len(steps):
            tell(q + 1)
    edges = local_coarse(w1)
    local_lifts(w1)
    local_blocks(w1, False)
    own_n1 = total(rhs2 * rhs2)
    p_one = safe_div(total(rhs2 * w1), own_n1)
    gap = w1 - p_one * rhs2
    gbuf[...] = gap
    own_n2 = total(gap * gap)
    line_wait(1, "recv")
    rim_wait(1, "recv")

    fix(1, *edges)
    w2 = wbuf[...].reshape(elems, n)
    rhs2, gap = rhs[...].reshape(elems, n), gbuf[...]
    p_two = safe_div(total(rhs2 * w2), own_n1)
    q_two = safe_div(total(gap * w2), own_n2)
    rest = w2 - p_two * rhs2 - q_two * gap
    msgs[me] = message([own_n1, p_one, own_n2, p_two, q_two, total(rest * rest)])
    broadcast()
    full(0, rhs2)
    full(1, fbuf[...])
    for g in range(2):
        line_wait(g, "send")
    for g in range(3):
        rim_wait(g, "send")
    bc_wait("send")
    bc_wait("recv")
    Y = msgs[:, 0, :]
    l_n1, l_p, l_n2, l_a, l_b, l_n3 = [Y] + [pltpu.roll(Y, n - q, 1) for q in range(1, 6)]

    def over(x):
        return jnp.sum(x, axis=0, keepdims=True)
    per_len2 = 1.0 / over(l_n1)
    h11 = over(l_p * l_n1) * per_len2
    dev = l_p - h11
    gap2 = over(dev * dev * l_n1 + l_n2)
    per_gap2 = 1.0 / gap2
    ratio = gap2 * per_len2
    e_one = l_a - h11 * l_p
    e_two = l_b - h11
    t12 = over(e_one * l_n1) * per_len2
    h22 = over(dev * e_one * l_n1 + e_two * l_n2) * per_gap2
    g_one = e_one - t12 - h22 * dev
    g_two = e_two - h22
    last2 = over(g_one * g_one * l_n1 + g_two * g_two * l_n2 + l_n3) * per_gap2
    first2 = h11 * h11 + ratio
    lower = h11 * h22 - t12
    c2 = -lower / (lower * lower + last2 * first2)
    c1 = (h11 - c2 * (h11 * t12 + ratio * h22)) / first2 - c2 * h11
    h21 = jnp.sqrt(ratio)
    h12, h32 = t12 / h21, jnp.sqrt(last2)
    c1, c2, h11, h12, h21, h22, h32 = [v[:, 0:1] for v in (c1, c2, h11, h12, h21, h22, h32)]
    out[...] = (c1 * zbuf[0] + c2 * zbuf[1]).reshape(ti, tj, n)
    hr, hc = iota((2, 3), 1), iota((2, 3), 0)
    hess_out[...] = jnp.where(
        hr == 0, jnp.where(hc == 0, h11, h12),
        jnp.where(hr == 1, jnp.where(hc == 0, h21, h22), jnp.where(hc == 0, 0.0, h32)))


def hand_on(sol_in, hess_in, sol_out, hess_out):
    sol_out[...] = sol_in[...]
    hess_out[...] = hess_in[...]


def solution(mesh):
    nx, ny = mesh.shape["gx"], mesh.shape["gy"]

    def body(rhs, diag, lift, state, basis, cinv):
        ti, tj, n = rhs.shape
        kc = basis.shape[1]
        cflat = jnp.transpose(cinv, (0, 2, 3, 1)).reshape(ti, kc * kc, tj)
        sflat = jnp.transpose(state, (0, 2, 1))
        h = 2 * ti + 2 * tj
        vm = pl.BlockSpec(memory_space=pltpu.VMEM)
        hbm = pl.BlockSpec(memory_space=pltpu.HBM)
        sol, hess = pl.pallas_call(
            functools.partial(kernel, nx, ny, ti, tj, n, kc),
            out_shape=(jax.ShapeDtypeStruct((ti, tj, n), F32), jax.ShapeDtypeStruct((2, 3), F32)),
            in_specs=[hbm] * 6,
            out_specs=(vm, vm),
            scratch_shapes=[
                pltpu.VMEM((ti, tj, n), F32),
                pltpu.VMEM((4, n, n), BF16),
                pltpu.VMEM((ti, 4, tj), jnp.int32),
                pltpu.VMEM((kc, n), F32),
                pltpu.VMEM((ti, kc * kc, tj), F32),
                pltpu.VMEM((ti, tj, n, n), BF16),
                pltpu.VMEM((8 * n, n), BF16),
                pltpu.VMEM((4 * n, n), BF16),
                pltpu.VMEM((ti, tj * kc, 2 * n), BF16),
                pltpu.VMEM((8, ti * tj, n), BF16),
                pltpu.VMEM((4, ti * tj, n), F32),
                pltpu.VMEM((4, ti, n), BF16),
                pltpu.VMEM((ti * tj + h, n), F32),
                pltpu.VMEM((2, ti * tj, n), F32),
                pltpu.VMEM((2, ti * tj, n), F32),
                pltpu.VMEM((ti * tj, n), F32),
                pltpu.VMEM((ti * tj, n), F32),
                pltpu.VMEM((ti * tj, n), F32),
                pltpu.VMEM((ti, tj, n), F32),
                pltpu.VMEM((2, h, n), BF16),
                pltpu.VMEM((2, h, n), BF16),
                pltpu.VMEM((h, n), F32),
                pltpu.VMEM((h, n), F32),
                pltpu.VMEM((2, 3 * ny, 8, n), F32),
                pltpu.VMEM((nx * ny, 1, n), F32),
                pltpu.SemaphoreType.DMA((5,)),
                pltpu.SemaphoreType.DMA((-(-ti // max(1, ti // 4)),)),
                pltpu.SemaphoreType.DMA((3, 4)),
                pltpu.SemaphoreType.DMA((3, 4)),
                pltpu.SemaphoreType.DMA((2, 3)),
                pltpu.SemaphoreType.DMA((2, 3)),
                pltpu.SemaphoreType.DMA((1,)),
                pltpu.SemaphoreType.DMA((1,)),
                pltpu.SemaphoreType.REGULAR((max(1, (nx - 2).bit_length() - 1),)),
            ],
            compiler_params=pltpu.CompilerParams(collective_id=0, has_side_effects=True,
                                                 vmem_limit_bytes=30000 * 1024),
        )(*[pltpu.with_memory_space_constraint(x, pltpu.HBM) for x in (rhs, diag, lift, sflat, basis.T, cflat)])
        sol, hess = pl.pallas_call(
            hand_on,
            out_shape=(jax.ShapeDtypeStruct(sol.shape, F32), jax.ShapeDtypeStruct(hess.shape, F32)),
            in_specs=[vm, vm],
            out_specs=(vm, vm),
            compiler_params=pltpu.CompilerParams(vmem_limit_bytes=30000 * 1024),
        )(sol, hess)
        return sol, hess.T

    in_specs = (P("gx", "gy", None), P("gx", "gy", None, None), P(), P("gx", "gy", None), P(),
                P("gx", "gy", None, None))
    return jax.shard_map(body, mesh=mesh, in_specs=in_specs, out_specs=(P("gx", "gy", None), P()), check_vma=False)
```

```python
import functools
import jax
import jax.numpy as jnp
from jax import lax
from jax.experimental import pallas as pl
from jax.experimental.pallas import tpu as pltpu
from jax.sharding import PartitionSpec as P

MESH = pl.DeviceIdType.MESH
F32 = jnp.float32
BF16 = jnp.bfloat16


def fdot(a, b):
    return jnp.dot(a, b, preferred_element_type=F32)


def over_first(a, b):
    return lax.dot_general(a, b, (((0,), (0,)), ((), ())), preferred_element_type=F32)


def cut(x):
    hi = x.astype(BF16)
    return hi, (x - hi.astype(F32)).astype(BF16)


def fine_dot(x, w):
    hi, lo = cut(x)
    return fdot(jnp.concatenate([hi, lo, hi], axis=1), w)


def exact_dot(x, w):
    m = x.shape[0]
    y = fdot(jnp.concatenate(cut(x), axis=0), w)
    return y[0:m] + y[m:2 * m]


def small_dot(x, w):
    m, n = x.shape[0], w.shape[1] // 2
    y = fdot(jnp.concatenate(cut(x), axis=0), w)
    return y[0:m, 0:n] + y[m:2 * m, 0:n] + y[0:m, n:2 * n]


def one_hot(x):
    return x.astype(F32).astype(BF16)


def total(x):
    return jnp.sum(jnp.sum(x, axis=0, keepdims=True), axis=1, keepdims=True)


def safe_div(a, b):
    return jnp.where(b > 0, a / jnp.where(b > 0, b, 1.0), 0.0)


def iota(shape, dim):
    return lax.broadcasted_iota(jnp.int32, shape, dim)


def kernel(nx, ny, ti, tj, n, kc, rhs_h, diag, lift_h, state_h, basis_h, cinv_h, out, hess_out,
           rhs, lift, state, basis, cinv,
           dvm, wts, cwts, wmat, masks, packs, rims, cext, pbuf, zbuf, cbuf, fbuf, gbuf, wbuf, sends, halos, csend, chalo, sums, msgs,
           isem, dsem, ssem, rsem, lsend, lrecv, msend, mrecv, know):
    gx = lax.axis_index("gx")
    gy = lax.axis_index("gy")
    me = gx * ny + gy
    count = nx * ny
    elems = ti * tj
    kk = kc * kc

    barrier = pltpu.get_barrier_semaphore()

    has_n, has_s, has_w, has_e = gx > 0, gx < nx - 1, gy > 0, gy < ny - 1
    n_i, s_i, w_i, e_i = [v.astype(jnp.int32) for v in (has_n, has_s, has_w, has_e)]
    turns = list(range(1, ny))
    near = [(has_s, 1, k) for k in turns[::-1] + [0]] + [(None, 0, k) for k in turns[::-1]] + [
        (has_n, -1, k) for k in turns[::-1] + [0]]
    near_count = ny - 1 + ny * (n_i + s_i)

    def when(ok, run):
        if ok is None:
            run()
        else:
            pl.when(ok)(run)

    sums[...] = jnp.zeros_like(sums)
    halos[...] = jnp.zeros_like(halos)
    chalo[...] = jnp.zeros_like(chalo)
    for ok, d, k in [(has_n, -1, k) for k in turns + [0]] + near[:2 * ny - 1]:
        def hello(d=d, k=k):
            pl.semaphore_signal(barrier, inc=1, device_id=(gx + d, lax.rem(gy + k, ny)), device_id_type=MESH)
        when(ok, hello)

    loads = [pltpu.make_async_copy(a, b, isem.at[q]) for q, (a, b) in enumerate(
        ((rhs_h, rhs), (basis_h, basis), (cinv_h, cinv), (state_h, state), (lift_h, lift)))]
    for c in loads:
        c.start()
    group = max(1, ti // 4)
    dcopies = [pltpu.make_async_copy(diag.at[pl.ds(q, group)], dvm.at[pl.ds(q, group)], dsem.at[q // group])
               for q in range(0, ti, group)]
    dcopies[0].start()
    dcopies[1].start()

    steps = []
    r = 2
    while r < nx - 1:
        steps.append(r)
        r *= 2

    def tell(q):
        r = steps[q]
        for ok, d in ((gx >= r, -r), (gx + r < nx, r)):
            def one(d=d):
                pl.semaphore_signal(know.at[q], inc=1, device_id=(gx + d, gy), device_id_type=MESH)
            when(ok, one)

    def learn(q):
        r = steps[q]
        amount = (gx >= r).astype(jnp.int32) + (gx + r < nx).astype(jnp.int32)
        pl.semaphore_wait(know.at[q], amount)

    def line_copy(g, d, k):
        return pltpu.make_async_remote_copy(
            src_ref=sums.at[g, ny + gy], dst_ref=sums.at[g, (1 - d) * ny + gy],
            send_sem=lsend.at[g, d + 1], recv_sem=lrecv.at[g, 1 - d],
            device_id=(gx + d, lax.rem(gy + k, ny)), device_id_type=MESH)

    def share_lines(g):
        for ok, d, k in near:
            when(ok, lambda d=d, k=k: line_copy(g, d, k).start())

    def line_wait(g, which):
        for ok, d in ((has_n, -1), (has_s, 1), (None, 0)):
            def one(d=d):
                part = sums.at[g, pl.ds((d + 1) * ny, ny if d else ny - 1)]
                c = pltpu.make_async_remote_copy(
                    src_ref=part, dst_ref=part, send_sem=lsend.at[g, d + 1], recv_sem=lrecv.at[g, d + 1],
                    device_id=(gx, gy), device_id_type=MESH)
                if which == "send":
                    c.wait_send()
                else:
                    c.wait_recv()
            when(ok, one)

    h = 2 * ti + 2 * tj
    croutes = [
        (has_n, (gx - 1, gy), 0, tj, tj),
        (has_s, (gx + 1, gy), tj, 0, tj),
        (has_w, (gx, gy - 1), 2 * tj, 2 * tj + ti, ti),
        (has_e, (gx, gy + 1), 2 * tj + ti, 2 * tj, ti),
    ]
    opposite = [1, 0, 3, 2]

    def rim_copies(g):
        return [(ok, pltpu.make_async_remote_copy(
            src_ref=sends.at[g, pl.ds(src, rows)], dst_ref=halos.at[g, pl.ds(dst, rows)],
            send_sem=ssem.at[g, d], recv_sem=rsem.at[g, opposite[d]],
            device_id=dev, device_id_type=MESH)) for d, (ok, dev, src, dst, rows) in enumerate(croutes)]

    def coarse_copies():
        return [(ok, pltpu.make_async_remote_copy(
            src_ref=csend.at[pl.ds(src, rows)], dst_ref=chalo.at[pl.ds(dst, rows)],
            send_sem=ssem.at[2, d], recv_sem=rsem.at[2, opposite[d]],
            device_id=dev, device_id_type=MESH)) for d, (ok, dev, src, dst, rows) in enumerate(croutes)]

    def rim_wait(g, which):
        for d, (ok, dev, src, dst, rows) in enumerate(croutes):
            @pl.when(ok)
            def _(d=d, dev=dev, src=src, rows=rows):
                if g < 2:
                    s, r = sends.at[g, pl.ds(src, rows)], halos.at[g, pl.ds(src, rows)]
                else:
                    s, r = csend.at[pl.ds(src, rows)], chalo.at[pl.ds(src, rows)]
                c = pltpu.make_async_remote_copy(
                    src_ref=s, dst_ref=r, send_sem=ssem.at[g, d], recv_sem=rsem.at[g, d],
                    device_id=dev, device_id_type=MESH)
                if which == "send":
                    c.wait_send()
                else:
                    c.wait_recv()

    def start_all(copies):
        for ok, c in copies:
            @pl.when(ok)
            def _(c=c):
                c.start()

    def broadcast():
        for tx, ty in sorted(((x, y) for x in range(nx) for y in range(ny)), key=lambda t: t[0] // 2 + t[1] // 2 + t[1] % 2):
            @pl.when(jnp.logical_or(gx != tx, gy != ty))
            def _(tx=tx, ty=ty):
                pltpu.make_async_remote_copy(
                    src_ref=msgs.at[me], dst_ref=msgs.at[me], send_sem=msend.at[0], recv_sem=mrecv.at[0],
                    device_id=(tx, ty), device_id_type=MESH).start()

    def bc_wait(which):
        part = msgs.at[pl.ds(0, count - 1)]
        c = pltpu.make_async_remote_copy(
            src_ref=part, dst_ref=part, send_sem=msend.at[0], recv_sem=mrecv.at[0],
            device_id=(gx, gy), device_id_type=MESH)
        if which == "send":
            c.wait_send()
        else:
            c.wait_recv()

    def fill_sends(g, ref):
        sends[g, 0:tj] = ref[0].astype(BF16)
        sends[g, tj:2 * tj] = ref[ti - 1].astype(BF16)
        sends[g, 2 * tj:2 * tj + ti] = ref[:, 0, :].astype(BF16)
        sends[g, 2 * tj + ti:h] = ref[:, tj - 1, :].astype(BF16)

    lane1 = iota((1, n), 1)

    def message(values):
        row = jnp.zeros((1, n), F32)
        for p, v in enumerate(values):
            row = jnp.where(lane1 == p, v, row)
        return row

    row_k = lax.rem(iota((kc, n), 1), kk) // kc == iota((kc, n), 0)
    row_l = lax.rem(iota((kc, n), 1), kc) == iota((kc, n), 0)
    pick = iota((ti, n), 1) // kc == iota((ti, n), 0)
    pick_j = iota((tj, n), 1) // kc == iota((tj, n), 0)
    low = lane1 < kk
    loads[0].wait()
    loads[1].wait()
    Rh, Rl = cut(basis[...])

    def spreads(pattern):
        e = one_hot(pattern)
        return over_first(Rh, e).astype(BF16), over_first(Rl, e).astype(BF16)

    def stacked(hi, lo):
        return jnp.concatenate([hi, hi, lo], axis=0)
    RT = jnp.concatenate(spreads(row_l), axis=1)
    rhs3 = rhs[...]
    rhs2 = rhs3.reshape(elems, n)

    def fill_sums(g, ref):
        rows = jnp.concatenate([
            jnp.sum(ref[...], axis=1), ref[:, 0, :], ref[:, 1, :], ref[:, tj - 1, :], ref[:, tj - 2, :],
            ref[0], ref[ti - 1]], axis=0)
        rows = small_dot(rows, RT)
        for q in range(7):
            at, lanes, size = (q * ti, pick, ti) if q < 5 else (5 * ti + (q - 5) * tj, pick_j, tj)
            sums[g, ny + gy, q:q + 1] = jnp.sum(jnp.where(lanes, rows[at:at + size], 0.0), axis=0, keepdims=True)

    fill_sends(0, rhs)
    fill_sums(0, rhs)
    loads[2].wait()
    eye = one_hot(iota((tj, tj), 0) == iota((tj, tj), 1))
    chi, clo = cut(cinv[...])
    both = jnp.concatenate([chi, clo], axis=2)
    both = jnp.concatenate([both, both], axis=1).reshape(ti * n, 2 * tj)
    turned = lax.dot_general(jnp.concatenate([eye, eye], axis=1), both, (((1,), (1,)), ((), ())),
                             preferred_element_type=F32)
    for q in range(ti):
        cext[q * tj:(q + 1) * tj] = turned[:, q * n:(q + 1) * n]
    c3d = cext[0:elems].reshape(ti, tj, n)
    csend[0:tj] = c3d[0]
    csend[tj:2 * tj] = c3d[ti - 1]
    csend[2 * tj:2 * tj + ti] = c3d[:, 0, :]
    csend[2 * tj + ti:2 * tj + 2 * ti] = c3d[:, tj - 1, :]

    pl.semaphore_wait(barrier, near_count)
    share_lines(0)
    start_all(rim_copies(0))
    start_all(coarse_copies())

    for c in dcopies[2:]:
        c.start()
    RE = stacked(*spreads(row_k))
    row_le = one_hot(row_l)
    RFh, RFl = over_first(row_le, Rh).astype(BF16), over_first(row_le, Rl).astype(BF16)
    low_row = iota((n, n), 0) < kk
    RF = jnp.concatenate([RFh, jnp.where(low_row, RFl.astype(F32), 0.0).astype(BF16)], axis=0)
    G = one_hot(lax.rem(iota((n, n), 0), kc) == lax.rem(iota((n, n), 1), kk) // kc)
    Q = one_hot(jnp.logical_and(low_row, lax.rem(iota((n, n), 0), kc) == lax.rem(iota((n, n), 1), kc)))
    Q = jnp.concatenate([Q, Q], axis=0)
    flip = one_hot(iota((n, n), 0) + iota((n, n), 1) == n - 1)
    RR = jnp.concatenate([RFh, RFl], axis=1)
    loads[4].wait()
    for f in range(4):
        straight = lift[f]
        turned = fdot(flip, straight).astype(BF16)
        wts[2 * f * n:(2 * f + 1) * n] = straight
        wts[(2 * f + 1) * n:(2 * f + 2) * n] = turned
        pair = jnp.concatenate([straight, turned], axis=1)
        prod = fdot(RR, jnp.concatenate([pair, pair], axis=0))
        cwts[f * n:(f + 1) * n] = jnp.where(low_row, prod[:, 0:n], prod[:, n:2 * n]).astype(BF16)
    loads[3].wait()
    own_j = lax.rem(iota((elems, tj), 0), tj) == iota((elems, tj), 1)
    ones = jnp.ones((tj, n), BF16)
    for f in range(4):
        rows = state[:, f, :].astype(F32)
        wide = jnp.broadcast_to(rows[:, None, :], (ti, tj, tj)).reshape(elems, tj)
        col = fdot(jnp.where(own_j, wide, 0.0).astype(BF16), ones)
        masks[2 * f] = one_hot(col == 1.0)
        masks[2 * f + 1] = one_hot(col == 2.0)
        packs[f] = one_hot(col == jnp.where(low, 1.0, 2.0))
        if f >= 2:
            edge = col.reshape(ti, tj, n)[:, 0 if f == 2 else tj - 1, :]
            rims[2 * f - 4] = one_hot(edge == 1.0)
            rims[2 * f - 3] = one_hot(edge == 2.0)

    jrow = lax.rem(iota((elems, 1), 0), tj)
    trow = iota((tj, 1), 0)
    scale = 1.0 / (ny * tj)
    irow = iota((1, 8, 1), 1)
    inner_parts = [1.0 + 0.25 * ((irow + q * 8 > 0).astype(F32) + (irow + q * 8 < tj - 1).astype(F32))
                   for q in range(tj // 8)]

    def spread(col):
        return jnp.broadcast_to(col[:, None, :], (ti, tj, n)).reshape(elems, n)

    def left_of(x, edge):
        return jnp.where(jrow == 0, edge, pltpu.roll(x, 1, 0))

    def right_of(x, edge):
        return jnp.where(jrow == tj - 1, edge, pltpu.roll(x, elems - 1, 0))

    def line_sum(g, d):
        acc = sums[g, (d + 1) * ny, 0:1]
        for q in range(1, ny):
            acc = acc + sums[g, (d + 1) * ny + q, 0:1]
        return acc

    def part_of(g, dx, dy, row):
        at = (dx + 1) * ny + jnp.clip(gy + dy, 0, ny - 1)
        return sums[g, at, row:row + 1]

    half = tj // 2
    keep = [one_hot(lax.rem(iota((2 * tj, n), 0), half) == t) for t in range(half)]
    none = jnp.zeros((kc, n), BF16)
    coarse_rows = jnp.concatenate([
        jnp.concatenate([Rh, none], axis=1), jnp.concatenate([none, Rh], axis=1)], axis=0)
    own_block = one_hot(iota((tj, n), 1) // kc == iota((tj, n), 0))

    def local_lifts(x):
        b = x.astype(BF16)
        gap = jnp.zeros((tj, n), BF16)
        nb = [
            jnp.concatenate([gap, b[0:elems - tj]], axis=0),
            jnp.concatenate([b[tj:], gap], axis=0),
            left_of(x, 0.0).astype(BF16),
            right_of(x, 0.0).astype(BF16),
        ]
        cols = []
        for f in range(4):
            cols.append(nb[f] * masks[2 * f])
            cols.append(nb[f] * masks[2 * f + 1])
        wbuf[...] = fdot(jnp.concatenate(cols, axis=1), wts[...]).reshape(ti, tj, n)

    def local_blocks(x, first):
        for q in range(ti):
            if first and q % group == 0:
                dcopies[q // group].wait()
            both = jnp.concatenate(cut(x[q * tj:(q + 1) * tj]), axis=0)
            rhs_w = jnp.concatenate(
                [dvm[q, 0:half].reshape(half * n, n), dvm[q, half:tj].reshape(half * n, n)], axis=1)
            if first:
                prod = None
                for t in range(0, half, 2):
                    lhs = jnp.concatenate([
                        jnp.concatenate([both * keep[t], both * keep[t + 1]], axis=1), coarse_rows], axis=0)
                    part = fdot(lhs, rhs_w[t * n:(t + 2) * n])
                    prod = part[0:2 * tj] if prod is None else prod + part[0:2 * tj]
                    for side in range(2):
                        at = (side * half + t) * kc
                        hi, lo = cut(part[2 * tj:, side * n:(side + 1) * n])
                        wmat[q, at:at + 2 * kc, 0:n] = hi
                        wmat[q, at:at + 2 * kc, n:2 * n] = lo
            else:
                prod = fdot(jnp.concatenate([both * keep[t] for t in range(half)], axis=1), rhs_w)
            prod = prod[0:tj] + prod[tj:2 * tj]
            wbuf[q] += jnp.concatenate([prod[0:half, 0:n], prod[half:tj, n:2 * n]], axis=0)

    def local_coarse(x):
        c = fine_dot(x, RE)
        cbuf[...] = c + 0.25 * (left_of(c, 0.0) + right_of(c, 0.0))
        c3 = c.reshape(ti, tj, n)
        return c3[:, 0, :], c3[:, tj - 1, :]

    def fix(g, own_w, own_e):
        group_of = lane1 // kc

        def lanes(x, mask):
            return jnp.where(mask, jnp.broadcast_to(x, mask.shape), 0.0)
        single = [
            (line_sum(g, -1), ti - 1), (line_sum(g, 1), 0),
            (part_of(g, -1, -1, 6), tj - 1), (part_of(g, -1, 1, 6), 0),
            (part_of(g, 1, -1, 5), tj - 1), (part_of(g, 1, 1, 5), 0)]
        srow = iota((8, n), 0)
        singles = jnp.zeros((8, n), F32)
        for q, (x, at) in enumerate(single):
            singles = jnp.where(jnp.logical_and(srow == q, group_of == at), jnp.broadcast_to(x, (8, n)), singles)
        stack = jnp.concatenate([
            lanes(line_sum(g, 0) * scale, pick),
            lanes(part_of(g, 0, -1, 3), pick), lanes(part_of(g, 0, -1, 4), pick),
            lanes(part_of(g, 0, 1, 1), pick), lanes(part_of(g, 0, 1, 2), pick),
            lanes(part_of(g, -1, 0, 6), pick_j), lanes(part_of(g, 1, 0, 5), pick_j), singles], axis=0)
        wide = exact_dot(stack, G)
        def rim_lift(f, at, one, two):
            b = halos[g, at:at + one.shape[0]]
            return fdot(jnp.concatenate([b * one, b * two], axis=1), wts[2 * f * n:(2 * f + 2) * n])
        last = elems - tj
        north = rim_lift(0, 0, masks[0, 0:tj], masks[1, 0:tj])
        south = rim_lift(1, tj, masks[2, last:elems], masks[3, last:elems])
        west = rim_lift(2, 2 * tj, rims[0], rims[1])
        east = rim_lift(3, 2 * tj + ti, rims[2], rims[3])
        m_c, c_w1, c_w2, c_e1, c_e2 = [wide[q * ti:(q + 1) * ti] for q in range(5)]
        c_n, c_s = wide[5 * ti:5 * ti + tj], wide[5 * ti + tj:5 * ti + 2 * tj]
        one = wide[5 * ti + 2 * tj:]
        m_n, m_s = one[0:1] * scale, one[1:2] * scale
        c_nw, c_ne, c_sw, c_se = [one[q:q + 1] for q in range(2, 6)]
        w_f, e_f = w_i.astype(F32), e_i.astype(F32)
        c_w1, c_w2 = (c_w1 - m_c) * w_f, c_w2 - m_c
        c_e1, c_e2 = (c_e1 - m_c) * e_f, c_e2 - m_c
        c_n, c_s = c_n - m_n, c_s - m_s
        c_nw, c_sw = (c_nw - m_n) * w_f, (c_sw - m_s) * w_f
        c_ne, c_se = (c_ne - m_n) * e_f, (c_se - m_s) * e_f

        def row_smooth(x, lo, hi):
            left = jnp.where(trow == 0, lo, pltpu.roll(x, 1, 0))
            right = jnp.where(trow == tj - 1, hi, pltpu.roll(x, tj - 1, 0))
            return x + 0.25 * (left + right)
        s_n, s_s = row_smooth(c_n, c_nw, c_ne), row_smooth(c_s, c_sw, c_se)
        s_w = c_w1 + 0.25 * (c_w2 + own_w - m_c)
        s_e = c_e1 + 0.25 * (own_e - m_c + c_e2)
        sub = iota((1, 8, 1), 1)
        parts = tj // 8

        def groups(x):
            return [x.reshape(ti, parts, 8, n)[:, q] for q in range(parts)]

        def whole(xs):
            return jnp.concatenate([x[:, None] for x in xs], axis=1).reshape(elems, n)

        def tall(x):
            return jnp.broadcast_to(x[:, None, :], (ti, 8, n))
        m_t, w_t, e_t = tall(m_c), tall(c_w1), tall(c_e1)
        first_w = jnp.where(sub == 0, 0.25, 0.0)
        last_e = jnp.where(sub == 7, 0.25, 0.0)
        p_parts = []
        for q, (c, k) in enumerate(zip(groups(cbuf[...]), groups(cext[0:elems]))):
            x = c - inner_parts[q] * m_t
            if q == 0:
                x = x + first_w * w_t
            if q == parts - 1:
                x = x + last_e * e_t
            p_parts.append(x * k)
        s_rim = jnp.concatenate([s_n, s_s, s_w, s_e], axis=0)
        p_rim = s_rim * cext[elems:elems + h]
        p = whole(p_parts)
        pbuf[g] = p
        hi, lo = cut(p)
        coef = fdot(jnp.concatenate([hi, lo], axis=1), Q)
        rim_w, rim_e = tall(p_rim[2 * tj:2 * tj + ti]), tall(p_rim[2 * tj + ti:2 * tj + 2 * ti])
        down = [pltpu.roll(x, 1, 1) for x in p_parts]
        up = [pltpu.roll(x, 7, 1) for x in p_parts]
        left = [jnp.where(sub == 0, rim_w if q == 0 else down[q - 1], down[q]) for q in range(parts)]
        right = [jnp.where(sub == 7, rim_e if q == parts - 1 else up[q + 1], up[q]) for q in range(parts)]
        rim_h = p_rim[0:2 * tj].astype(BF16)
        nb = [
            jnp.concatenate([rim_h[0:tj], hi[0:elems - tj]], axis=0),
            jnp.concatenate([hi[tj:], rim_h[tj:2 * tj]], axis=0),
            whole(left).astype(BF16),
            whole(right).astype(BF16),
        ]
        lifted = fdot(jnp.concatenate([nb[f] * packs[f] for f in range(4)], axis=1), cwts[...])
        c_hi, c_lo = cut(coef)
        base = []
        for q in range(ti):
            side = jnp.where(trow == 0, west[q:q + 1], jnp.where(trow == tj - 1, east[q:q + 1], 0.0))
            x = wbuf[q] + lifted[q * tj:(q + 1) * tj] + side
            base.append(x + north if q == 0 else x + south if q == ti - 1 else x)
        for q in range(ti):
            at = slice(q * tj, (q + 1) * tj)
            y = fdot(jnp.concatenate([c_hi[at] * own_block, c_lo[at] * own_block], axis=0), wmat[q])
            wbuf[q] = base[q] + y[0:tj, 0:n] + (y[tj:2 * tj, 0:n] + y[0:tj, n:2 * n])

    def full(g, x):
        hi, lo = cut(pbuf[g])
        mixed = jnp.where(low, hi.astype(F32), lo.astype(F32)).astype(BF16)
        zbuf[g] = x + fdot(jnp.concatenate([mixed, hi], axis=1), RF)

    edges = local_coarse(rhs2)
    local_lifts(rhs2)
    local_blocks(rhs2, True)
    line_wait(0, "recv")
    rim_wait(0, "recv")
    rim_wait(2, "recv")
    if steps:
        tell(0)

    cext[elems:elems + h] = chalo[...]
    fix(0, *edges)
    fill_sends(1, wbuf)
    start_all(rim_copies(1))
    fill_sums(1, wbuf)
    share_lines(1)
    w1 = wbuf[...].reshape(elems, n)
    fbuf[...] = w1
    for q in range(len(steps)):
        learn(q)
        if q + 1 < len(steps):
            tell(q + 1)
    edges = local_coarse(w1)
    local_lifts(w1)
    local_blocks(w1, False)
    own_n1 = total(rhs2 * rhs2)
    p_one = safe_div(total(rhs2 * w1), own_n1)
    gap = w1 - p_one * rhs2
    gbuf[...] = gap
    own_n2 = total(gap * gap)
    line_wait(1, "recv")
    rim_wait(1, "recv")

    fix(1, *edges)
    w2 = wbuf[...].reshape(elems, n)
    rhs2, gap = rhs[...].reshape(elems, n), gbuf[...]
    p_two = safe_div(total(rhs2 * w2), own_n1)
    q_two = safe_div(total(gap * w2), own_n2)
    rest = w2 - p_two * rhs2 - q_two * gap
    msgs[me] = message([own_n1, p_one, own_n2, p_two, q_two, total(rest * rest)])
    broadcast()
    full(0, rhs2)
    full(1, fbuf[...])
    for g in range(2):
        line_wait(g, "send")
    for g in range(3):
        rim_wait(g, "send")
    bc_wait("send")
    bc_wait("recv")
    Y = msgs[:, 0, :]
    l_n1, l_p, l_n2, l_a, l_b, l_n3 = [Y] + [pltpu.roll(Y, n - q, 1) for q in range(1, 6)]

    def over(x):
        return jnp.sum(x, axis=0, keepdims=True)
    per_len2 = 1.0 / over(l_n1)
    h11 = over(l_p * l_n1) * per_len2
    dev = l_p - h11
    gap2 = over(dev * dev * l_n1 + l_n2)
    per_gap2 = 1.0 / gap2
    ratio = gap2 * per_len2
    e_one = l_a - h11 * l_p
    e_two = l_b - h11
    t12 = over(e_one * l_n1) * per_len2
    h22 = over(dev * e_one * l_n1 + e_two * l_n2) * per_gap2
    g_one = e_one - t12 - h22 * dev
    g_two = e_two - h22
    last2 = over(g_one * g_one * l_n1 + g_two * g_two * l_n2 + l_n3) * per_gap2
    first2 = h11 * h11 + ratio
    lower = h11 * h22 - t12
    c2 = -lower / (lower * lower + last2 * first2)
    c1 = (h11 - c2 * (h11 * t12 + ratio * h22)) / first2 - c2 * h11
    h21 = jnp.sqrt(ratio)
    h12, h32 = t12 / h21, jnp.sqrt(last2)
    c1, c2, h11, h12, h21, h22, h32 = [v[:, 0:1] for v in (c1, c2, h11, h12, h21, h22, h32)]
    out[...] = (c1 * zbuf[0] + c2 * zbuf[1]).reshape(ti, tj, n)
    hr, hc = iota((2, 3), 1), iota((2, 3), 0)
    hess_out[...] = jnp.where(
        hr == 0, jnp.where(hc == 0, h11, h12),
        jnp.where(hr == 1, jnp.where(hc == 0, h21, h22), jnp.where(hc == 0, 0.0, h32)))


def hand_on(sol_in, hess_in, sol_out, hess_out):
    sol_out[...] = sol_in[...]
    hess_out[...] = hess_in[...]


def solution(mesh):
    nx, ny = mesh.shape["gx"], mesh.shape["gy"]

    def body(rhs, diag, lift, state, basis, cinv):
        ti, tj, n = rhs.shape
        kc = basis.shape[1]
        cflat = jnp.transpose(cinv, (0, 2, 3, 1)).reshape(ti, kc * kc, tj)
        sflat = jnp.transpose(state, (0, 2, 1))
        h = 2 * ti + 2 * tj
        vm = pl.BlockSpec(memory_space=pltpu.VMEM)
        hbm = pl.BlockSpec(memory_space=pltpu.HBM)
        sol, hess = pl.pallas_call(
            functools.partial(kernel, nx, ny, ti, tj, n, kc),
            out_shape=(jax.ShapeDtypeStruct((ti, tj, n), F32), jax.ShapeDtypeStruct((2, 3), F32)),
            in_specs=[hbm] * 6,
            out_specs=(vm, vm),
            scratch_shapes=[
                pltpu.VMEM((ti, tj, n), F32),
                pltpu.VMEM((4, n, n), BF16),
                pltpu.VMEM((ti, 4, tj), jnp.int32),
                pltpu.VMEM((kc, n), F32),
                pltpu.VMEM((ti, kc * kc, tj), F32),
                pltpu.VMEM((ti, tj, n, n), BF16),
                pltpu.VMEM((8 * n, n), BF16),
                pltpu.VMEM((4 * n, n), BF16),
                pltpu.VMEM((ti, tj * kc, 2 * n), BF16),
                pltpu.VMEM((8, ti * tj, n), BF16),
                pltpu.VMEM((4, ti * tj, n), BF16),
                pltpu.VMEM((4, ti, n), BF16),
                pltpu.VMEM((ti * tj + h, n), F32),
                pltpu.VMEM((2, ti * tj, n), F32),
                pltpu.VMEM((2, ti * tj, n), F32),
                pltpu.VMEM((ti * tj, n), F32),
                pltpu.VMEM((ti * tj, n), F32),
                pltpu.VMEM((ti * tj, n), F32),
                pltpu.VMEM((ti, tj, n), F32),
                pltpu.VMEM((2, h, n), BF16),
                pltpu.VMEM((2, h, n), BF16),
                pltpu.VMEM((h, n), F32),
                pltpu.VMEM((h, n), F32),
                pltpu.VMEM((2, 3 * ny, 8, n), F32),
                pltpu.VMEM((nx * ny, 1, n), F32),
                pltpu.SemaphoreType.DMA((5,)),
                pltpu.SemaphoreType.DMA((-(-ti // max(1, ti // 4)),)),
                pltpu.SemaphoreType.DMA((3, 4)),
                pltpu.SemaphoreType.DMA((3, 4)),
                pltpu.SemaphoreType.DMA((2, 3)),
                pltpu.SemaphoreType.DMA((2, 3)),
                pltpu.SemaphoreType.DMA((1,)),
                pltpu.SemaphoreType.DMA((1,)),
                pltpu.SemaphoreType.REGULAR((max(1, (nx - 2).bit_length() - 1),)),
            ],
            compiler_params=pltpu.CompilerParams(collective_id=0, has_side_effects=True,
                                                 vmem_limit_bytes=30000 * 1024),
        )(*[pltpu.with_memory_space_constraint(x, pltpu.HBM) for x in (rhs, diag, lift, sflat, basis.T, cflat)])
        sol, hess = pl.pallas_call(
            hand_on,
            out_shape=(jax.ShapeDtypeStruct(sol.shape, F32), jax.ShapeDtypeStruct(hess.shape, F32)),
            in_specs=[vm, vm],
            out_specs=(vm, vm),
            compiler_params=pltpu.CompilerParams(vmem_limit_bytes=30000 * 1024),
        )(sol, hess)
        return sol, hess.T

    in_specs = (P("gx", "gy", None), P("gx", "gy", None, None), P(), P("gx", "gy", None), P(),
                P("gx", "gy", None, None))
    return jax.shard_map(body, mesh=mesh, in_specs=in_specs, out_specs=(P("gx", "gy", None), P()), check_vma=False)
```

```python
import functools
import jax
import jax.numpy as jnp
from jax import lax
from jax.experimental import pallas as pl
from jax.experimental.pallas import tpu as pltpu
from jax.sharding import PartitionSpec as P

MESH = pl.DeviceIdType.MESH
F32 = jnp.float32
BF16 = jnp.bfloat16


def fdot(a, b):
    return jnp.dot(a, b, preferred_element_type=F32)


def over_first(a, b):
    return lax.dot_general(a, b, (((0,), (0,)), ((), ())), preferred_element_type=F32)


def cut(x):
    hi = x.astype(BF16)
    return hi, (x - hi.astype(F32)).astype(BF16)


def fine_dot(x, w):
    hi, lo = cut(x)
    return fdot(jnp.concatenate([hi, lo, hi], axis=1), w)


def exact_dot(x, w):
    m = x.shape[0]
    y = fdot(jnp.concatenate(cut(x), axis=0), w)
    return y[0:m] + y[m:2 * m]


def small_dot(x, w):
    m, n = x.shape[0], w.shape[1] // 2
    y = fdot(jnp.concatenate(cut(x), axis=0), w)
    return y[0:m, 0:n] + y[m:2 * m, 0:n] + y[0:m, n:2 * n]


def one_hot(x):
    return x.astype(F32).astype(BF16)


def total(x):
    return jnp.sum(jnp.sum(x, axis=0, keepdims=True), axis=1, keepdims=True)


def safe_div(a, b):
    return jnp.where(b > 0, a / jnp.where(b > 0, b, 1.0), 0.0)


def iota(shape, dim):
    return lax.broadcasted_iota(jnp.int32, shape, dim)


def kernel(nx, ny, ti, tj, n, kc, rhs_h, diag, lift_h, state_h, basis_h, cinv_h, out, hess_out,
           rhs, lift, state, basis, cinv,
           dvm, wts, cwts, wmat, masks, packs, rims, cext, pbuf, zbuf, cbuf, fbuf, gbuf, wbuf, sends, halos, csend, chalo, sums, msgs,
           isem, dsem, ssem, rsem, lsend, lrecv, msend, mrecv, know):
    gx = lax.axis_index("gx")
    gy = lax.axis_index("gy")
    me = gx * ny + gy
    count = nx * ny
    elems = ti * tj
    kk = kc * kc

    barrier = pltpu.get_barrier_semaphore()

    has_n, has_s, has_w, has_e = gx > 0, gx < nx - 1, gy > 0, gy < ny - 1
    n_i, s_i, w_i, e_i = [v.astype(jnp.int32) for v in (has_n, has_s, has_w, has_e)]
    turns = list(range(1, ny))
    near = [(has_s, 1, k) for k in turns[::-1] + [0]] + [(None, 0, k) for k in turns[::-1]] + [
        (has_n, -1, k) for k in turns[::-1] + [0]]
    near_count = ny - 1 + ny * (n_i + s_i)

    def when(ok, run):
        if ok is None:
            run()
        else:
            pl.when(ok)(run)

    sums[...] = jnp.zeros_like(sums)
    halos[...] = jnp.zeros_like(halos)
    chalo[...] = jnp.zeros_like(chalo)
    for ok, d, k in [(has_n, -1, k) for k in turns + [0]] + near[:2 * ny - 1]:
        def hello(d=d, k=k):
            pl.semaphore_signal(barrier, inc=1, device_id=(gx + d, lax.rem(gy + k, ny)), device_id_type=MESH)
        when(ok, hello)

    loads = [pltpu.make_async_copy(a, b, isem.at[q]) for q, (a, b) in enumerate(
        ((rhs_h, rhs), (basis_h, basis), (cinv_h, cinv), (state_h, state), (lift_h, lift)))]
    for c in loads:
        c.start()
    group = max(1, ti // 4)
    dcopies = [pltpu.make_async_copy(diag.at[pl.ds(q, group)], dvm.at[pl.ds(q, group)], dsem.at[q // group])
               for q in range(0, ti, group)]
    dcopies[0].start()
    dcopies[1].start()

    steps = []
    r = 2
    while r < nx - 1:
        steps.append(r)
        r *= 2

    def tell(q):
        r = steps[q]
        for ok, d in ((gx >= r, -r), (gx + r < nx, r)):
            def one(d=d):
                pl.semaphore_signal(know.at[q], inc=1, device_id=(gx + d, gy), device_id_type=MESH)
            when(ok, one)

    def learn(q):
        r = steps[q]
        amount = (gx >= r).astype(jnp.int32) + (gx + r < nx).astype(jnp.int32)
        pl.semaphore_wait(know.at[q], amount)

    def line_copy(g, d, k):
        return pltpu.make_async_remote_copy(
            src_ref=sums.at[g, ny + gy], dst_ref=sums.at[g, (1 - d) * ny + gy],
            send_sem=lsend.at[g], recv_sem=lrecv.at[g],
            device_id=(gx + d, lax.rem(gy + k, ny)), device_id_type=MESH)

    def share_lines(g):
        for ok, d, k in near:
            when(ok, lambda d=d, k=k: line_copy(g, d, k).start())

    def line_wait(g, which):
        for lines in range(3):
            messages = ny * (lines + 1) - 1
            if messages:
                @pl.when(n_i + s_i == lines)
                def _(messages=messages):
                    part = sums.at[g, pl.ds(0, messages)]
                    c = pltpu.make_async_remote_copy(
                        src_ref=part, dst_ref=part, send_sem=lsend.at[g], recv_sem=lrecv.at[g],
                        device_id=(gx, gy), device_id_type=MESH)
                    if which == "send":
                        c.wait_send()
                    else:
                        c.wait_recv()

    h = 2 * ti + 2 * tj
    croutes = [
        (has_n, (gx - 1, gy), 0, tj, tj),
        (has_s, (gx + 1, gy), tj, 0, tj),
        (has_w, (gx, gy - 1), 2 * tj, 2 * tj + ti, ti),
        (has_e, (gx, gy + 1), 2 * tj + ti, 2 * tj, ti),
    ]
    opposite = [1, 0, 3, 2]

    def rim_copies(g):
        return [(ok, pltpu.make_async_remote_copy(
            src_ref=sends.at[g, pl.ds(src, rows)], dst_ref=halos.at[g, pl.ds(dst, rows)],
            send_sem=ssem.at[g, d], recv_sem=rsem.at[g, opposite[d]],
            device_id=dev, device_id_type=MESH)) for d, (ok, dev, src, dst, rows) in enumerate(croutes)]

    def coarse_copies():
        return [(ok, pltpu.make_async_remote_copy(
            src_ref=csend.at[pl.ds(src, rows)], dst_ref=chalo.at[pl.ds(dst, rows)],
            send_sem=ssem.at[2, d], recv_sem=rsem.at[2, opposite[d]],
            device_id=dev, device_id_type=MESH)) for d, (ok, dev, src, dst, rows) in enumerate(croutes)]

    def rim_wait(g, which):
        for d, (ok, dev, src, dst, rows) in enumerate(croutes):
            @pl.when(ok)
            def _(d=d, dev=dev, src=src, rows=rows):
                if g < 2:
                    s, r = sends.at[g, pl.ds(src, rows)], halos.at[g, pl.ds(src, rows)]
                else:
                    s, r = csend.at[pl.ds(src, rows)], chalo.at[pl.ds(src, rows)]
                c = pltpu.make_async_remote_copy(
                    src_ref=s, dst_ref=r, send_sem=ssem.at[g, d], recv_sem=rsem.at[g, d],
                    device_id=dev, device_id_type=MESH)
                if which == "send":
                    c.wait_send()
                else:
                    c.wait_recv()

    def start_all(copies):
        for ok, c in copies:
            @pl.when(ok)
            def _(c=c):
                c.start()

    def broadcast():
        for tx, ty in sorted(((x, y) for x in range(nx) for y in range(ny)), key=lambda t: t[0] // 2 + t[1] // 2 + t[1] % 2):
            @pl.when(jnp.logical_or(gx != tx, gy != ty))
            def _(tx=tx, ty=ty):
                pltpu.make_async_remote_copy(
                    src_ref=msgs.at[me], dst_ref=msgs.at[me], send_sem=msend.at[0], recv_sem=mrecv.at[0],
                    device_id=(tx, ty), device_id_type=MESH).start()

    def bc_wait(which):
        part = msgs.at[pl.ds(0, count - 1)]
        c = pltpu.make_async_remote_copy(
            src_ref=part, dst_ref=part, send_sem=msend.at[0], recv_sem=mrecv.at[0],
            device_id=(gx, gy), device_id_type=MESH)
        if which == "send":
            c.wait_send()
        else:
            c.wait_recv()

    def fill_sends(g, ref):
        sends[g, 0:tj] = ref[0].astype(BF16)
        sends[g, tj:2 * tj] = ref[ti - 1].astype(BF16)
        sends[g, 2 * tj:2 * tj + ti] = ref[:, 0, :].astype(BF16)
        sends[g, 2 * tj + ti:h] = ref[:, tj - 1, :].astype(BF16)

    lane1 = iota((1, n), 1)

    def message(values):
        row = jnp.zeros((1, n), F32)
        for p, v in enumerate(values):
            row = jnp.where(lane1 == p, v, row)
        return row

    row_k = lax.rem(iota((kc, n), 1), kk) // kc == iota((kc, n), 0)
    row_l = lax.rem(iota((kc, n), 1), kc) == iota((kc, n), 0)
    pick = iota((ti, n), 1) // kc == iota((ti, n), 0)
    pick_j = iota((tj, n), 1) // kc == iota((tj, n), 0)
    low = lane1 < kk
    loads[0].wait()
    loads[1].wait()
    Rh, Rl = cut(basis[...])

    def spreads(pattern):
        e = one_hot(pattern)
        return over_first(Rh, e).astype(BF16), over_first(Rl, e).astype(BF16)

    def stacked(hi, lo):
        return jnp.concatenate([hi, hi, lo], axis=0)
    RT = jnp.concatenate(spreads(row_l), axis=1)
    rhs3 = rhs[...]
    rhs2 = rhs3.reshape(elems, n)

    def fill_sums(g, ref):
        rows = jnp.concatenate([
            jnp.sum(ref[...], axis=1), ref[:, 0, :], ref[:, 1, :], ref[:, tj - 1, :], ref[:, tj - 2, :],
            ref[0], ref[ti - 1]], axis=0)
        rows = small_dot(rows, RT)
        for q in range(7):
            at, lanes, size = (q * ti, pick, ti) if q < 5 else (5 * ti + (q - 5) * tj, pick_j, tj)
            sums[g, ny + gy, q:q + 1] = jnp.sum(jnp.where(lanes, rows[at:at + size], 0.0), axis=0, keepdims=True)

    fill_sends(0, rhs)
    fill_sums(0, rhs)
    loads[2].wait()
    eye = one_hot(iota((tj, tj), 0) == iota((tj, tj), 1))
    chi, clo = cut(cinv[...])
    both = jnp.concatenate([chi, clo], axis=2)
    both = jnp.concatenate([both, both], axis=1).reshape(ti * n, 2 * tj)
    turned = lax.dot_general(jnp.concatenate([eye, eye], axis=1), both, (((1,), (1,)), ((), ())),
                             preferred_element_type=F32)
    for q in range(ti):
        cext[q * tj:(q + 1) * tj] = turned[:, q * n:(q + 1) * n]
    c3d = cext[0:elems].reshape(ti, tj, n)
    csend[0:tj] = c3d[0]
    csend[tj:2 * tj] = c3d[ti - 1]
    csend[2 * tj:2 * tj + ti] = c3d[:, 0, :]
    csend[2 * tj + ti:2 * tj + 2 * ti] = c3d[:, tj - 1, :]

    pl.semaphore_wait(barrier, near_count)
    share_lines(0)
    start_all(rim_copies(0))
    start_all(coarse_copies())

    for c in dcopies[2:]:
        c.start()
    RE = stacked(*spreads(row_k))
    row_le = one_hot(row_l)
    RFh, RFl = over_first(row_le, Rh).astype(BF16), over_first(row_le, Rl).astype(BF16)
    low_row = iota((n, n), 0) < kk
    RF = jnp.concatenate([RFh, jnp.where(low_row, RFl.astype(F32), 0.0).astype(BF16)], axis=0)
    G = one_hot(lax.rem(iota((n, n), 0), kc) == lax.rem(iota((n, n), 1), kk) // kc)
    Q = one_hot(jnp.logical_and(low_row, lax.rem(iota((n, n), 0), kc) == lax.rem(iota((n, n), 1), kc)))
    Q = jnp.concatenate([Q, Q], axis=0)
    flip = one_hot(iota((n, n), 0) + iota((n, n), 1) == n - 1)
    RR = jnp.concatenate([RFh, RFl], axis=1)
    loads[4].wait()
    for f in range(4):
        straight = lift[f]
        turned = fdot(flip, straight).astype(BF16)
        wts[2 * f * n:(2 * f + 1) * n] = straight
        wts[(2 * f + 1) * n:(2 * f + 2) * n] = turned
        pair = jnp.concatenate([straight, turned], axis=1)
        prod = fdot(RR, jnp.concatenate([pair, pair], axis=0))
        cwts[f * n:(f + 1) * n] = jnp.where(low_row, prod[:, 0:n], prod[:, n:2 * n]).astype(BF16)
    loads[3].wait()
    own_j = lax.rem(iota((elems, tj), 0), tj) == iota((elems, tj), 1)
    ones = jnp.ones((tj, n), BF16)
    for f in range(4):
        rows = state[:, f, :].astype(F32)
        wide = jnp.broadcast_to(rows[:, None, :], (ti, tj, tj)).reshape(elems, tj)
        col = fdot(jnp.where(own_j, wide, 0.0).astype(BF16), ones)
        masks[2 * f] = one_hot(col == 1.0)
        masks[2 * f + 1] = one_hot(col == 2.0)
        packs[f] = one_hot(col == jnp.where(low, 1.0, 2.0))
        if f >= 2:
            edge = col.reshape(ti, tj, n)[:, 0 if f == 2 else tj - 1, :]
            rims[2 * f - 4] = one_hot(edge == 1.0)
            rims[2 * f - 3] = one_hot(edge == 2.0)

    jrow = lax.rem(iota((elems, 1), 0), tj)
    trow = iota((tj, 1), 0)
    scale = 1.0 / (ny * tj)
    irow = iota((1, 8, 1), 1)
    inner_parts = [1.0 + 0.25 * ((irow + q * 8 > 0).astype(F32) + (irow + q * 8 < tj - 1).astype(F32))
                   for q in range(tj // 8)]

    def spread(col):
        return jnp.broadcast_to(col[:, None, :], (ti, tj, n)).reshape(elems, n)

    def left_of(x, edge):
        return jnp.where(jrow == 0, edge, pltpu.roll(x, 1, 0))

    def right_of(x, edge):
        return jnp.where(jrow == tj - 1, edge, pltpu.roll(x, elems - 1, 0))

    def line_sum(g, d):
        acc = sums[g, (d + 1) * ny, 0:1]
        for q in range(1, ny):
            acc = acc + sums[g, (d + 1) * ny + q, 0:1]
        return acc

    def part_of(g, dx, dy, row):
        at = (dx + 1) * ny + jnp.clip(gy + dy, 0, ny - 1)
        return sums[g, at, row:row + 1]

    half = tj // 2
    keep = [one_hot(lax.rem(iota((2 * tj, n), 0), half) == t) for t in range(half)]
    none = jnp.zeros((kc, n), BF16)
    coarse_rows = jnp.concatenate([
        jnp.concatenate([Rh, none], axis=1), jnp.concatenate([none, Rh], axis=1)], axis=0)
    own_block = one_hot(iota((tj, n), 1) // kc == iota((tj, n), 0))

    def local_lifts(x):
        b = x.astype(BF16)
        gap = jnp.zeros((tj, n), BF16)
        nb = [
            jnp.concatenate([gap, b[0:elems - tj]], axis=0),
            jnp.concatenate([b[tj:], gap], axis=0),
            left_of(x, 0.0).astype(BF16),
            right_of(x, 0.0).astype(BF16),
        ]
        cols = []
        for f in range(4):
            cols.append(nb[f] * masks[2 * f])
            cols.append(nb[f] * masks[2 * f + 1])
        wbuf[...] = fdot(jnp.concatenate(cols, axis=1), wts[...]).reshape(ti, tj, n)

    def local_blocks(x, first):
        for q in range(ti):
            if first and q % group == 0:
                dcopies[q // group].wait()
            both = jnp.concatenate(cut(x[q * tj:(q + 1) * tj]), axis=0)
            rhs_w = jnp.concatenate(
                [dvm[q, 0:half].reshape(half * n, n), dvm[q, half:tj].reshape(half * n, n)], axis=1)
            if first:
                prod = None
                for t in range(0, half, 2):
                    lhs = jnp.concatenate([
                        jnp.concatenate([both * keep[t], both * keep[t + 1]], axis=1), coarse_rows], axis=0)
                    part = fdot(lhs, rhs_w[t * n:(t + 2) * n])
                    prod = part[0:2 * tj] if prod is None else prod + part[0:2 * tj]
                    for side in range(2):
                        at = (side * half + t) * kc
                        hi, lo = cut(part[2 * tj:, side * n:(side + 1) * n])
                        wmat[q, at:at + 2 * kc, 0:n] = hi
                        wmat[q, at:at + 2 * kc, n:2 * n] = lo
            else:
                prod = fdot(jnp.concatenate([both * keep[t] for t in range(half)], axis=1), rhs_w)
            prod = prod[0:tj] + prod[tj:2 * tj]
            wbuf[q] += jnp.concatenate([prod[0:half, 0:n], prod[half:tj, n:2 * n]], axis=0)

    def local_coarse(x):
        c = fine_dot(x, RE)
        cbuf[...] = c + 0.25 * (left_of(c, 0.0) + right_of(c, 0.0))
        c3 = c.reshape(ti, tj, n)
        return c3[:, 0, :], c3[:, tj - 1, :]

    def fix(g, own_w, own_e):
        group_of = lane1 // kc

        def lanes(x, mask):
            return jnp.where(mask, jnp.broadcast_to(x, mask.shape), 0.0)
        single = [
            (line_sum(g, -1), ti - 1), (line_sum(g, 1), 0),
            (part_of(g, -1, -1, 6), tj - 1), (part_of(g, -1, 1, 6), 0),
            (part_of(g, 1, -1, 5), tj - 1), (part_of(g, 1, 1, 5), 0)]
        srow = iota((8, n), 0)
        singles = jnp.zeros((8, n), F32)
        for q, (x, at) in enumerate(single):
            singles = jnp.where(jnp.logical_and(srow == q, group_of == at), jnp.broadcast_to(x, (8, n)), singles)
        stack = jnp.concatenate([
            lanes(line_sum(g, 0) * scale, pick),
            lanes(part_of(g, 0, -1, 3), pick), lanes(part_of(g, 0, -1, 4), pick),
            lanes(part_of(g, 0, 1, 1), pick), lanes(part_of(g, 0, 1, 2), pick),
            lanes(part_of(g, -1, 0, 6), pick_j), lanes(part_of(g, 1, 0, 5), pick_j), singles], axis=0)
        wide = exact_dot(stack, G)
        def rim_lift(f, at, one, two):
            b = halos[g, at:at + one.shape[0]]
            return fdot(jnp.concatenate([b * one, b * two], axis=1), wts[2 * f * n:(2 * f + 2) * n])
        last = elems - tj
        north = rim_lift(0, 0, masks[0, 0:tj], masks[1, 0:tj])
        south = rim_lift(1, tj, masks[2, last:elems], masks[3, last:elems])
        west = rim_lift(2, 2 * tj, rims[0], rims[1])
        east = rim_lift(3, 2 * tj + ti, rims[2], rims[3])
        m_c, c_w1, c_w2, c_e1, c_e2 = [wide[q * ti:(q + 1) * ti] for q in range(5)]
        c_n, c_s = wide[5 * ti:5 * ti + tj], wide[5 * ti + tj:5 * ti + 2 * tj]
        one = wide[5 * ti + 2 * tj:]
        m_n, m_s = one[0:1] * scale, one[1:2] * scale
        c_nw, c_ne, c_sw, c_se = [one[q:q + 1] for q in range(2, 6)]
        w_f, e_f = w_i.astype(F32), e_i.astype(F32)
        c_w1, c_w2 = (c_w1 - m_c) * w_f, c_w2 - m_c
        c_e1, c_e2 = (c_e1 - m_c) * e_f, c_e2 - m_c
        c_n, c_s = c_n - m_n, c_s - m_s
        c_nw, c_sw = (c_nw - m_n) * w_f, (c_sw - m_s) * w_f
        c_ne, c_se = (c_ne - m_n) * e_f, (c_se - m_s) * e_f

        def row_smooth(x, lo, hi):
            left = jnp.where(trow == 0, lo, pltpu.roll(x, 1, 0))
            right = jnp.where(trow == tj - 1, hi, pltpu.roll(x, tj - 1, 0))
            return x + 0.25 * (left + right)
        s_n, s_s = row_smooth(c_n, c_nw, c_ne), row_smooth(c_s, c_sw, c_se)
        s_w = c_w1 + 0.25 * (c_w2 + own_w - m_c)
        s_e = c_e1 + 0.25 * (own_e - m_c + c_e2)
        sub = iota((1, 8, 1), 1)
        parts = tj // 8

        def groups(x):
            return [x.reshape(ti, parts, 8, n)[:, q] for q in range(parts)]

        def whole(xs):
            return jnp.concatenate([x[:, None] for x in xs], axis=1).reshape(elems, n)

        def tall(x):
            return jnp.broadcast_to(x[:, None, :], (ti, 8, n))
        m_t, w_t, e_t = tall(m_c), tall(c_w1), tall(c_e1)
        first_w = jnp.where(sub == 0, 0.25, 0.0)
        last_e = jnp.where(sub == 7, 0.25, 0.0)
        p_parts = []
        for q, (c, k) in enumerate(zip(groups(cbuf[...]), groups(cext[0:elems]))):
            x = c - inner_parts[q] * m_t
            if q == 0:
                x = x + first_w * w_t
            if q == parts - 1:
                x = x + last_e * e_t
            p_parts.append(x * k)
        s_rim = jnp.concatenate([s_n, s_s, s_w, s_e], axis=0)
        p_rim = s_rim * cext[elems:elems + h]
        p = whole(p_parts)
        pbuf[g] = p
        hi, lo = cut(p)
        coef = fdot(jnp.concatenate([hi, lo], axis=1), Q)
        rim_w, rim_e = tall(p_rim[2 * tj:2 * tj + ti]), tall(p_rim[2 * tj + ti:2 * tj + 2 * ti])
        down = [pltpu.roll(x, 1, 1) for x in p_parts]
        up = [pltpu.roll(x, 7, 1) for x in p_parts]
        left = [jnp.where(sub == 0, rim_w if q == 0 else down[q - 1], down[q]) for q in range(parts)]
        right = [jnp.where(sub == 7, rim_e if q == parts - 1 else up[q + 1], up[q]) for q in range(parts)]
        rim_h = p_rim[0:2 * tj].astype(BF16)
        nb = [
            jnp.concatenate([rim_h[0:tj], hi[0:elems - tj]], axis=0),
            jnp.concatenate([hi[tj:], rim_h[tj:2 * tj]], axis=0),
            whole(left).astype(BF16),
            whole(right).astype(BF16),
        ]
        lifted = fdot(jnp.concatenate([nb[f] * packs[f] for f in range(4)], axis=1), cwts[...])
        c_hi, c_lo = cut(coef)
        base = []
        for q in range(ti):
            side = jnp.where(trow == 0, west[q:q + 1], jnp.where(trow == tj - 1, east[q:q + 1], 0.0))
            x = wbuf[q] + lifted[q * tj:(q + 1) * tj] + side
            base.append(x + north if q == 0 else x + south if q == ti - 1 else x)
        for q in range(ti):
            at = slice(q * tj, (q + 1) * tj)
            y = fdot(jnp.concatenate([c_hi[at] * own_block, c_lo[at] * own_block], axis=0), wmat[q])
            wbuf[q] = base[q] + y[0:tj, 0:n] + (y[tj:2 * tj, 0:n] + y[0:tj, n:2 * n])

    def full(g, x):
        hi, lo = cut(pbuf[g])
        mixed = jnp.where(low, hi.astype(F32), lo.astype(F32)).astype(BF16)
        zbuf[g] = x + fdot(jnp.concatenate([mixed, hi], axis=1), RF)

    edges = local_coarse(rhs2)
    local_lifts(rhs2)
    local_blocks(rhs2, True)
    line_wait(0, "recv")
    rim_wait(0, "recv")
    rim_wait(2, "recv")
    if steps:
        tell(0)

    cext[elems:elems + h] = chalo[...]
    fix(0, *edges)
    fill_sends(1, wbuf)
    start_all(rim_copies(1))
    fill_sums(1, wbuf)
    share_lines(1)
    w1 = wbuf[...].reshape(elems, n)
    fbuf[...] = w1
    for q in range(len(steps)):
        learn(q)
        if q + 1 < len(steps):
            tell(q + 1)
    edges = local_coarse(w1)
    local_lifts(w1)
    local_blocks(w1, False)
    own_n1 = total(rhs2 * rhs2)
    p_one = safe_div(total(rhs2 * w1), own_n1)
    gap = w1 - p_one * rhs2
    gbuf[...] = gap
    own_n2 = total(gap * gap)
    line_wait(1, "recv")
    rim_wait(1, "recv")

    fix(1, *edges)
    w2 = wbuf[...].reshape(elems, n)
    rhs2, gap = rhs[...].reshape(elems, n), gbuf[...]
    on_rhs, on_gap, square = total(rhs2 * w2), total(gap * w2), total(w2 * w2)
    p_two, q_two = safe_div(on_rhs, own_n1), safe_div(on_gap, own_n2)
    rest = jnp.maximum(square - p_two * on_rhs - q_two * on_gap, 0.0)
    msgs[me] = message([own_n1, p_one, own_n2, p_two, q_two, rest])
    broadcast()
    full(0, rhs2)
    full(1, fbuf[...])
    for g in range(2):
        line_wait(g, "send")
    for g in range(3):
        rim_wait(g, "send")
    bc_wait("send")
    bc_wait("recv")
    Y = msgs[:, 0, :]
    l_n1, l_p, l_n2, l_a, l_b, l_n3 = [Y] + [pltpu.roll(Y, n - q, 1) for q in range(1, 6)]

    def over(x):
        return jnp.sum(x, axis=0, keepdims=True)
    per_len2 = 1.0 / over(l_n1)
    h11 = over(l_p * l_n1) * per_len2
    dev = l_p - h11
    gap2 = over(dev * dev * l_n1 + l_n2)
    per_gap2 = 1.0 / gap2
    ratio = gap2 * per_len2
    e_one = l_a - h11 * l_p
    e_two = l_b - h11
    t12 = over(e_one * l_n1) * per_len2
    h22 = over(dev * e_one * l_n1 + e_two * l_n2) * per_gap2
    g_one = e_one - t12 - h22 * dev
    g_two = e_two - h22
    last2 = over(g_one * g_one * l_n1 + g_two * g_two * l_n2 + l_n3) * per_gap2
    first2 = h11 * h11 + ratio
    lower = h11 * h22 - t12
    c2 = -lower / (lower * lower + last2 * first2)
    c1 = (h11 - c2 * (h11 * t12 + ratio * h22)) / first2 - c2 * h11
    h21 = jnp.sqrt(ratio)
    h12, h32 = t12 / h21, jnp.sqrt(last2)
    c1, c2, h11, h12, h21, h22, h32 = [v[:, 0:1] for v in (c1, c2, h11, h12, h21, h22, h32)]
    out[...] = (c1 * zbuf[0] + c2 * zbuf[1]).reshape(ti, tj, n)
    hr, hc = iota((2, 3), 1), iota((2, 3), 0)
    hess_out[...] = jnp.where(
        hr == 0, jnp.where(hc == 0, h11, h12),
        jnp.where(hr == 1, jnp.where(hc == 0, h21, h22), jnp.where(hc == 0, 0.0, h32)))


def hand_on(sol_in, hess_in, sol_out, hess_out, sem):
    copies = [pltpu.make_async_copy(sol_in, sol_out, sem.at[0]), pltpu.make_async_copy(hess_in, hess_out, sem.at[1])]
    for c in copies:
        c.start()
    for c in copies:
        c.wait()


def solution(mesh):
    nx, ny = mesh.shape["gx"], mesh.shape["gy"]

    def body(rhs, diag, lift, state, basis, cinv):
        ti, tj, n = rhs.shape
        kc = basis.shape[1]
        cflat = jnp.transpose(cinv, (0, 2, 3, 1)).reshape(ti, kc * kc, tj)
        sflat = jnp.transpose(state, (0, 2, 1))
        h = 2 * ti + 2 * tj
        vm = pl.BlockSpec(memory_space=pltpu.VMEM)
        hbm = pl.BlockSpec(memory_space=pltpu.HBM)
        sol, hess = pl.pallas_call(
            functools.partial(kernel, nx, ny, ti, tj, n, kc),
            out_shape=(jax.ShapeDtypeStruct((ti, tj, n), F32), jax.ShapeDtypeStruct((2, 3), F32)),
            in_specs=[hbm] * 6,
            out_specs=(vm, vm),
            scratch_shapes=[
                pltpu.VMEM((ti, tj, n), F32),
                pltpu.VMEM((4, n, n), BF16),
                pltpu.VMEM((ti, 4, tj), jnp.int32),
                pltpu.VMEM((kc, n), F32),
                pltpu.VMEM((ti, kc * kc, tj), F32),
                pltpu.VMEM((ti, tj, n, n), BF16),
                pltpu.VMEM((8 * n, n), BF16),
                pltpu.VMEM((4 * n, n), BF16),
                pltpu.VMEM((ti, tj * kc, 2 * n), BF16),
                pltpu.VMEM((8, ti * tj, n), BF16),
                pltpu.VMEM((4, ti * tj, n), BF16),
                pltpu.VMEM((4, ti, n), BF16),
                pltpu.VMEM((ti * tj + h, n), F32),
                pltpu.VMEM((2, ti * tj, n), F32),
                pltpu.VMEM((2, ti * tj, n), F32),
                pltpu.VMEM((ti * tj, n), F32),
                pltpu.VMEM((ti * tj, n), F32),
                pltpu.VMEM((ti * tj, n), F32),
                pltpu.VMEM((ti, tj, n), F32),
                pltpu.VMEM((2, h, n), BF16),
                pltpu.VMEM((2, h, n), BF16),
                pltpu.VMEM((h, n), F32),
                pltpu.VMEM((h, n), F32),
                pltpu.VMEM((2, 3 * ny, 8, n), F32),
                pltpu.VMEM((nx * ny, 1, n), F32),
                pltpu.SemaphoreType.DMA((5,)),
                pltpu.SemaphoreType.DMA((-(-ti // max(1, ti // 4)),)),
                pltpu.SemaphoreType.DMA((3, 4)),
                pltpu.SemaphoreType.DMA((3, 4)),
                pltpu.SemaphoreType.DMA((2,)),
                pltpu.SemaphoreType.DMA((2,)),
                pltpu.SemaphoreType.DMA((1,)),
                pltpu.SemaphoreType.DMA((1,)),
                pltpu.SemaphoreType.REGULAR((max(1, (nx - 2).bit_length() - 1),)),
            ],
            compiler_params=pltpu.CompilerParams(collective_id=0, has_side_effects=True,
                                                 vmem_limit_bytes=30000 * 1024),
        )(*[pltpu.with_memory_space_constraint(x, pltpu.HBM) for x in (rhs, diag, lift, sflat, basis.T, cflat)])
        sol, hess = pl.pallas_call(
            hand_on,
            out_shape=(jax.ShapeDtypeStruct(sol.shape, F32), jax.ShapeDtypeStruct(hess.shape, F32)),
            in_specs=[vm, vm],
            out_specs=(hbm, hbm),
            scratch_shapes=[pltpu.SemaphoreType.DMA((2,))],
            compiler_params=pltpu.CompilerParams(vmem_limit_bytes=30000 * 1024),
        )(sol, hess)
        return sol, hess.T

    in_specs = (P("gx", "gy", None), P("gx", "gy", None, None), P(), P("gx", "gy", None), P(),
                P("gx", "gy", None, None))
    return jax.shard_map(body, mesh=mesh, in_specs=in_specs, out_specs=(P("gx", "gy", None), P()), check_vma=False)
```

```python
import functools
import jax
import jax.numpy as jnp
from jax import lax
from jax.experimental import pallas as pl
from jax.experimental.pallas import tpu as pltpu
from jax.sharding import PartitionSpec as P

MESH = pl.DeviceIdType.MESH
F32 = jnp.float32
BF16 = jnp.bfloat16


def fdot(a, b):
    return jnp.dot(a, b, preferred_element_type=F32)


def over_first(a, b):
    return lax.dot_general(a, b, (((0,), (0,)), ((), ())), preferred_element_type=F32)


def cut(x):
    hi = x.astype(BF16)
    return hi, (x - hi.astype(F32)).astype(BF16)


def fine_dot(x, w):
    hi, lo = cut(x)
    return fdot(jnp.concatenate([hi, lo, hi], axis=1), w)


def exact_dot(x, w):
    m = x.shape[0]
    y = fdot(jnp.concatenate(cut(x), axis=0), w)
    return y[0:m] + y[m:2 * m]


def small_dot(x, w):
    m, n = x.shape[0], w.shape[1] // 2
    y = fdot(jnp.concatenate(cut(x), axis=0), w)
    return y[0:m, 0:n] + y[m:2 * m, 0:n] + y[0:m, n:2 * n]


def one_hot(x):
    return x.astype(F32).astype(BF16)


def total(x):
    return jnp.sum(jnp.sum(x, axis=0, keepdims=True), axis=1, keepdims=True)


def safe_div(a, b):
    return jnp.where(b > 0, a / jnp.where(b > 0, b, 1.0), 0.0)


def iota(shape, dim):
    return lax.broadcasted_iota(jnp.int32, shape, dim)


def kernel(nx, ny, ti, tj, n, kc, rhs_h, diag, lift_h, state_h, basis_h, cinv_h, out, hess_out,
           rhs, lift, state, basis, cinv,
           dvm, wts, cwts, wmat, masks, packs, rims, cext, pbuf, zbuf, cbuf, fbuf, gbuf, wbuf, sends, halos, csend, chalo, sums, msgs,
           isem, dsem, ssem, rsem, lsend, lrecv, msend, mrecv, know):
    gx = lax.axis_index("gx")
    gy = lax.axis_index("gy")
    me = gx * ny + gy
    count = nx * ny
    elems = ti * tj
    kk = kc * kc

    barrier = pltpu.get_barrier_semaphore()

    has_n, has_s, has_w, has_e = gx > 0, gx < nx - 1, gy > 0, gy < ny - 1
    n_i, s_i, w_i, e_i = [v.astype(jnp.int32) for v in (has_n, has_s, has_w, has_e)]
    turns = list(range(1, ny))
    near = [(has_s, 1, k) for k in turns[::-1] + [0]] + [(None, 0, k) for k in turns[::-1]] + [
        (has_n, -1, k) for k in turns[::-1] + [0]]
    near_count = ny - 1 + ny * (n_i + s_i)

    def when(ok, run):
        if ok is None:
            run()
        else:
            pl.when(ok)(run)

    for ok, d, k in [(has_n, -1, k) for k in turns + [0]] + near[:2 * ny - 1]:
        def hello(d=d, k=k):
            pl.semaphore_signal(barrier, inc=1, device_id=(gx + d, lax.rem(gy + k, ny)), device_id_type=MESH)
        when(ok, hello)

    h = 2 * ti + 2 * tj
    for ok, at, rows, line in ((has_n, 0, tj, 0), (has_s, tj, tj, 2), (has_w, 2 * tj, ti, None), (has_e, 2 * tj + ti, ti, None)):
        @pl.when(jnp.logical_not(ok))
        def _(at=at, rows=rows, line=line):
            halos[:, at:at + rows] = jnp.zeros((2, rows, n), BF16)
            chalo[at:at + rows] = jnp.zeros((rows, n), F32)
            if line is not None:
                sums[:, line * ny:(line + 1) * ny] = jnp.zeros((2, ny, 8, n), F32)

    loads = [pltpu.make_async_copy(a, b, isem.at[q]) for q, (a, b) in enumerate(
        ((rhs_h, rhs), (basis_h, basis), (cinv_h, cinv), (state_h, state), (lift_h, lift)))]
    for c in loads:
        c.start()
    group = max(1, ti // 4)
    dcopies = [pltpu.make_async_copy(diag.at[pl.ds(q, group)], dvm.at[pl.ds(q, group)], dsem.at[q // group])
               for q in range(0, ti, group)]
    dcopies[0].start()
    dcopies[1].start()

    steps = []
    r = 2
    while r < nx - 1:
        steps.append(r)
        r *= 2

    def tell(q):
        r = steps[q]
        for ok, d in ((gx >= r, -r), (gx + r < nx, r)):
            def one(d=d):
                pl.semaphore_signal(know.at[q], inc=1, device_id=(gx + d, gy), device_id_type=MESH)
            when(ok, one)

    def learn(q):
        r = steps[q]
        amount = (gx >= r).astype(jnp.int32) + (gx + r < nx).astype(jnp.int32)
        pl.semaphore_wait(know.at[q], amount)

    def line_copy(g, d, k):
        return pltpu.make_async_remote_copy(
            src_ref=sums.at[g, ny + gy], dst_ref=sums.at[g, (1 - d) * ny + gy],
            send_sem=lsend.at[g], recv_sem=lrecv.at[g],
            device_id=(gx + d, lax.rem(gy + k, ny)), device_id_type=MESH)

    def share_lines(g):
        for ok, d, k in near:
            when(ok, lambda d=d, k=k: line_copy(g, d, k).start())

    def line_wait(g, which):
        for lines in range(3):
            messages = ny * (lines + 1) - 1
            if messages:
                @pl.when(n_i + s_i == lines)
                def _(messages=messages):
                    part = sums.at[g, pl.ds(0, messages)]
                    c = pltpu.make_async_remote_copy(
                        src_ref=part, dst_ref=part, send_sem=lsend.at[g], recv_sem=lrecv.at[g],
                        device_id=(gx, gy), device_id_type=MESH)
                    if which == "send":
                        c.wait_send()
                    else:
                        c.wait_recv()

    h = 2 * ti + 2 * tj
    croutes = [
        (has_n, (gx - 1, gy), 0, tj, tj),
        (has_s, (gx + 1, gy), tj, 0, tj),
        (has_w, (gx, gy - 1), 2 * tj, 2 * tj + ti, ti),
        (has_e, (gx, gy + 1), 2 * tj + ti, 2 * tj, ti),
    ]
    opposite = [1, 0, 3, 2]

    def rim_copies(g):
        return [(ok, pltpu.make_async_remote_copy(
            src_ref=sends.at[g, pl.ds(src, rows)], dst_ref=halos.at[g, pl.ds(dst, rows)],
            send_sem=ssem.at[g], recv_sem=rsem.at[g, opposite[d]],
            device_id=dev, device_id_type=MESH)) for d, (ok, dev, src, dst, rows) in enumerate(croutes)]

    def coarse_copies():
        return [(ok, pltpu.make_async_remote_copy(
            src_ref=csend.at[pl.ds(src, rows)], dst_ref=chalo.at[pl.ds(dst, rows)],
            send_sem=ssem.at[2], recv_sem=rsem.at[2, opposite[d]],
            device_id=dev, device_id_type=MESH)) for d, (ok, dev, src, dst, rows) in enumerate(croutes)]

    def rim_part(g, src, rows):
        return halos.at[g, pl.ds(src, rows)] if g < 2 else chalo.at[pl.ds(src, rows)]

    def rim_wait(g, which):
        if which == "send":
            for a in range(3):
                for b in range(3):
                    if a or b:
                        @pl.when(jnp.logical_and(n_i + s_i == a, w_i + e_i == b))
                        def _(a=a, b=b):
                            part = rim_part(g, 0, a * tj + b * ti)
                            pltpu.make_async_remote_copy(
                                src_ref=part, dst_ref=part, send_sem=ssem.at[g], recv_sem=rsem.at[g, 0],
                                device_id=(gx, gy), device_id_type=MESH).wait_send()
            return
        for d, (ok, dev, src, dst, rows) in enumerate(croutes):
            @pl.when(ok)
            def _(d=d, dev=dev, src=src, rows=rows):
                part = rim_part(g, src, rows)
                pltpu.make_async_remote_copy(
                    src_ref=part, dst_ref=part, send_sem=ssem.at[g], recv_sem=rsem.at[g, d],
                    device_id=dev, device_id_type=MESH).wait_recv()

    def start_all(copies):
        for ok, c in copies:
            @pl.when(ok)
            def _(c=c):
                c.start()

    def broadcast():
        for tx, ty in sorted(((x, y) for x in range(nx) for y in range(ny)), key=lambda t: t[0] // 2 + t[1] // 2 + t[1] % 2):
            @pl.when(jnp.logical_or(gx != tx, gy != ty))
            def _(tx=tx, ty=ty):
                pltpu.make_async_remote_copy(
                    src_ref=msgs.at[me], dst_ref=msgs.at[me], send_sem=msend.at[0], recv_sem=mrecv.at[0],
                    device_id=(tx, ty), device_id_type=MESH).start()

    def bc_wait(which):
        part = msgs.at[pl.ds(0, count - 1)]
        c = pltpu.make_async_remote_copy(
            src_ref=part, dst_ref=part, send_sem=msend.at[0], recv_sem=mrecv.at[0],
            device_id=(gx, gy), device_id_type=MESH)
        if which == "send":
            c.wait_send()
        else:
            c.wait_recv()

    def fill_sends(g, ref):
        sends[g, 0:tj] = ref[0].astype(BF16)
        sends[g, tj:2 * tj] = ref[ti - 1].astype(BF16)
        sends[g, 2 * tj:2 * tj + ti] = ref[:, 0, :].astype(BF16)
        sends[g, 2 * tj + ti:h] = ref[:, tj - 1, :].astype(BF16)

    lane1 = iota((1, n), 1)

    def message(values):
        row = jnp.zeros((1, n), F32)
        for p, v in enumerate(values):
            row = jnp.where(lane1 == p, v, row)
        return row

    row_k = lax.rem(iota((kc, n), 1), kk) // kc == iota((kc, n), 0)
    row_l = lax.rem(iota((kc, n), 1), kc) == iota((kc, n), 0)
    pick = iota((ti, n), 1) // kc == iota((ti, n), 0)
    pick_j = iota((tj, n), 1) // kc == iota((tj, n), 0)
    low = lane1 < kk
    loads[0].wait()
    loads[1].wait()
    Rh, Rl = cut(basis[...])

    def spreads(pattern):
        e = one_hot(pattern)
        return over_first(Rh, e).astype(BF16), over_first(Rl, e).astype(BF16)

    def stacked(hi, lo):
        return jnp.concatenate([hi, hi, lo], axis=0)
    RT = jnp.concatenate(spreads(row_l), axis=1)
    rhs3 = rhs[...]
    rhs2 = rhs3.reshape(elems, n)

    def fill_sums(g, ref):
        rows = jnp.concatenate([
            jnp.sum(ref[...], axis=1), ref[:, 0, :], ref[:, 1, :], ref[:, tj - 1, :], ref[:, tj - 2, :],
            ref[0], ref[ti - 1]], axis=0)
        rows = small_dot(rows, RT)
        for q in range(7):
            at, lanes, size = (q * ti, pick, ti) if q < 5 else (5 * ti + (q - 5) * tj, pick_j, tj)
            sums[g, ny + gy, q:q + 1] = jnp.sum(jnp.where(lanes, rows[at:at + size], 0.0), axis=0, keepdims=True)

    fill_sends(0, rhs)
    fill_sums(0, rhs)
    loads[2].wait()
    eye = one_hot(iota((tj, tj), 0) == iota((tj, tj), 1))
    chi, clo = cut(cinv[...])
    both = jnp.concatenate([chi, clo], axis=2)
    both = jnp.concatenate([both, both], axis=1).reshape(ti * n, 2 * tj)
    turned = lax.dot_general(jnp.concatenate([eye, eye], axis=1), both, (((1,), (1,)), ((), ())),
                             preferred_element_type=F32)
    for q in range(ti):
        cext[q * tj:(q + 1) * tj] = turned[:, q * n:(q + 1) * n]
    c3d = cext[0:elems].reshape(ti, tj, n)
    csend[0:tj] = c3d[0]
    csend[tj:2 * tj] = c3d[ti - 1]
    csend[2 * tj:2 * tj + ti] = c3d[:, 0, :]
    csend[2 * tj + ti:2 * tj + 2 * ti] = c3d[:, tj - 1, :]

    pl.semaphore_wait(barrier, near_count)
    share_lines(0)
    start_all(rim_copies(0))
    start_all(coarse_copies())

    for c in dcopies[2:]:
        c.start()
    RE = stacked(*spreads(row_k))
    row_le = one_hot(row_l)
    RFh, RFl = over_first(row_le, Rh).astype(BF16), over_first(row_le, Rl).astype(BF16)
    low_row = iota((n, n), 0) < kk
    RF = jnp.concatenate([RFh, jnp.where(low_row, RFl.astype(F32), 0.0).astype(BF16)], axis=0)
    G = one_hot(lax.rem(iota((n, n), 0), kc) == lax.rem(iota((n, n), 1), kk) // kc)
    Q = one_hot(jnp.logical_and(low_row, lax.rem(iota((n, n), 0), kc) == lax.rem(iota((n, n), 1), kc)))
    Q = jnp.concatenate([Q, Q], axis=0)
    flip = one_hot(iota((n, n), 0) + iota((n, n), 1) == n - 1)
    RR = jnp.concatenate([RFh, RFl], axis=1)
    loads[4].wait()
    for f in range(4):
        straight = lift[f]
        turned = fdot(flip, straight).astype(BF16)
        wts[2 * f * n:(2 * f + 1) * n] = straight
        wts[(2 * f + 1) * n:(2 * f + 2) * n] = turned
        pair = jnp.concatenate([straight, turned], axis=1)
        prod = fdot(RR, jnp.concatenate([pair, pair], axis=0))
        cwts[f * n:(f + 1) * n] = jnp.where(low_row, prod[:, 0:n], prod[:, n:2 * n]).astype(BF16)
    loads[3].wait()
    own_j = lax.rem(iota((elems, tj), 0), tj) == iota((elems, tj), 1)
    ones = jnp.ones((tj, n), BF16)
    for f in range(4):
        rows = state[:, f, :].astype(F32)
        wide = jnp.broadcast_to(rows[:, None, :], (ti, tj, tj)).reshape(elems, tj)
        col = fdot(jnp.where(own_j, wide, 0.0).astype(BF16), ones)
        masks[2 * f] = one_hot(col == 1.0)
        masks[2 * f + 1] = one_hot(col == 2.0)
        packs[f] = one_hot(col == jnp.where(low, 1.0, 2.0))
        if f >= 2:
            edge = col.reshape(ti, tj, n)[:, 0 if f == 2 else tj - 1, :]
            rims[2 * f - 4] = one_hot(edge == 1.0)
            rims[2 * f - 3] = one_hot(edge == 2.0)

    jrow = lax.rem(iota((elems, 1), 0), tj)
    trow = iota((tj, 1), 0)
    scale = 1.0 / (ny * tj)
    irow = iota((1, 8, 1), 1)
    inner_parts = [1.0 + 0.25 * ((irow + q * 8 > 0).astype(F32) + (irow + q * 8 < tj - 1).astype(F32))
                   for q in range(tj // 8)]

    def spread(col):
        return jnp.broadcast_to(col[:, None, :], (ti, tj, n)).reshape(elems, n)

    def left_of(x, edge):
        return jnp.where(jrow == 0, edge, pltpu.roll(x, 1, 0))

    def right_of(x, edge):
        return jnp.where(jrow == tj - 1, edge, pltpu.roll(x, elems - 1, 0))

    def line_sum(g, d):
        acc = sums[g, (d + 1) * ny, 0:1]
        for q in range(1, ny):
            acc = acc + sums[g, (d + 1) * ny + q, 0:1]
        return acc

    def part_of(g, dx, dy, row):
        at = (dx + 1) * ny + jnp.clip(gy + dy, 0, ny - 1)
        return sums[g, at, row:row + 1]

    half = tj // 2
    keep = [one_hot(lax.rem(iota((2 * tj, n), 0), half) == t) for t in range(half)]
    none = jnp.zeros((kc, n), BF16)
    coarse_rows = jnp.concatenate([
        jnp.concatenate([Rh, none], axis=1), jnp.concatenate([none, Rh], axis=1)], axis=0)
    own_block = one_hot(iota((tj, n), 1) // kc == iota((tj, n), 0))

    def local_lifts(x):
        b = x.astype(BF16)
        gap = jnp.zeros((tj, n), BF16)
        nb = [
            jnp.concatenate([gap, b[0:elems - tj]], axis=0),
            jnp.concatenate([b[tj:], gap], axis=0),
            left_of(x, 0.0).astype(BF16),
            right_of(x, 0.0).astype(BF16),
        ]
        cols = []
        for f in range(4):
            cols.append(nb[f] * masks[2 * f])
            cols.append(nb[f] * masks[2 * f + 1])
        wbuf[...] = fdot(jnp.concatenate(cols, axis=1), wts[...]).reshape(ti, tj, n)

    def local_blocks(x, first):
        for q in range(ti):
            if first and q % group == 0:
                dcopies[q // group].wait()
            both = jnp.concatenate(cut(x[q * tj:(q + 1) * tj]), axis=0)
            rhs_w = jnp.concatenate(
                [dvm[q, 0:half].reshape(half * n, n), dvm[q, half:tj].reshape(half * n, n)], axis=1)
            if first:
                prod = None
                for t in range(0, half, 2):
                    lhs = jnp.concatenate([
                        jnp.concatenate([both * keep[t], both * keep[t + 1]], axis=1), coarse_rows], axis=0)
                    part = fdot(lhs, rhs_w[t * n:(t + 2) * n])
                    prod = part[0:2 * tj] if prod is None else prod + part[0:2 * tj]
                    for side in range(2):
                        at = (side * half + t) * kc
                        hi, lo = cut(part[2 * tj:, side * n:(side + 1) * n])
                        wmat[q, at:at + 2 * kc, 0:n] = hi
                        wmat[q, at:at + 2 * kc, n:2 * n] = lo
            else:
                prod = fdot(jnp.concatenate([both * keep[t] for t in range(half)], axis=1), rhs_w)
            prod = prod[0:tj] + prod[tj:2 * tj]
            wbuf[q] += jnp.concatenate([prod[0:half, 0:n], prod[half:tj, n:2 * n]], axis=0)

    def local_coarse(x):
        c = fine_dot(x, RE)
        cbuf[...] = c + 0.25 * (left_of(c, 0.0) + right_of(c, 0.0))
        c3 = c.reshape(ti, tj, n)
        return c3[:, 0, :], c3[:, tj - 1, :]

    def fix_rims(g):
        def rim_lift(f, at, one, two):
            b = halos[g, at:at + one.shape[0]]
            return fdot(jnp.concatenate([b * one, b * two], axis=1), wts[2 * f * n:(2 * f + 2) * n])
        last = elems - tj
        north = rim_lift(0, 0, masks[0, 0:tj], masks[1, 0:tj])
        south = rim_lift(1, tj, masks[2, last:elems], masks[3, last:elems])
        west = rim_lift(2, 2 * tj, rims[0], rims[1])
        east = rim_lift(3, 2 * tj + ti, rims[2], rims[3])
        for q in range(ti):
            side = jnp.where(trow == 0, west[q:q + 1], jnp.where(trow == tj - 1, east[q:q + 1], 0.0))
            if q == 0:
                side = side + north
            if q == ti - 1:
                side = side + south
            wbuf[q] += side

    def fix(g, own_w, own_e):
        group_of = lane1 // kc

        def lanes(x, mask):
            return jnp.where(mask, jnp.broadcast_to(x, mask.shape), 0.0)
        single = [
            (line_sum(g, -1), ti - 1), (line_sum(g, 1), 0),
            (part_of(g, -1, -1, 6), tj - 1), (part_of(g, -1, 1, 6), 0),
            (part_of(g, 1, -1, 5), tj - 1), (part_of(g, 1, 1, 5), 0)]
        srow = iota((8, n), 0)
        singles = jnp.zeros((8, n), F32)
        for q, (x, at) in enumerate(single):
            singles = jnp.where(jnp.logical_and(srow == q, group_of == at), jnp.broadcast_to(x, (8, n)), singles)
        stack = jnp.concatenate([
            lanes(line_sum(g, 0) * scale, pick),
            lanes(part_of(g, 0, -1, 3), pick), lanes(part_of(g, 0, -1, 4), pick),
            lanes(part_of(g, 0, 1, 1), pick), lanes(part_of(g, 0, 1, 2), pick),
            lanes(part_of(g, -1, 0, 6), pick_j), lanes(part_of(g, 1, 0, 5), pick_j), singles], axis=0)
        wide = exact_dot(stack, G)
        m_c, c_w1, c_w2, c_e1, c_e2 = [wide[q * ti:(q + 1) * ti] for q in range(5)]
        c_n, c_s = wide[5 * ti:5 * ti + tj], wide[5 * ti + tj:5 * ti + 2 * tj]
        one = wide[5 * ti + 2 * tj:]
        m_n, m_s = one[0:1] * scale, one[1:2] * scale
        c_nw, c_ne, c_sw, c_se = [one[q:q + 1] for q in range(2, 6)]
        w_f, e_f = w_i.astype(F32), e_i.astype(F32)
        c_w1, c_w2 = (c_w1 - m_c) * w_f, c_w2 - m_c
        c_e1, c_e2 = (c_e1 - m_c) * e_f, c_e2 - m_c
        c_n, c_s = c_n - m_n, c_s - m_s
        c_nw, c_sw = (c_nw - m_n) * w_f, (c_sw - m_s) * w_f
        c_ne, c_se = (c_ne - m_n) * e_f, (c_se - m_s) * e_f

        def row_smooth(x, lo, hi):
            left = jnp.where(trow == 0, lo, pltpu.roll(x, 1, 0))
            right = jnp.where(trow == tj - 1, hi, pltpu.roll(x, tj - 1, 0))
            return x + 0.25 * (left + right)
        s_n, s_s = row_smooth(c_n, c_nw, c_ne), row_smooth(c_s, c_sw, c_se)
        s_w = c_w1 + 0.25 * (c_w2 + own_w - m_c)
        s_e = c_e1 + 0.25 * (own_e - m_c + c_e2)
        sub = iota((1, 8, 1), 1)
        parts = tj // 8

        def groups(x):
            return [x.reshape(ti, parts, 8, n)[:, q] for q in range(parts)]

        def whole(xs):
            return jnp.concatenate([x[:, None] for x in xs], axis=1).reshape(elems, n)

        def tall(x):
            return jnp.broadcast_to(x[:, None, :], (ti, 8, n))
        m_t, w_t, e_t = tall(m_c), tall(c_w1), tall(c_e1)
        first_w = jnp.where(sub == 0, 0.25, 0.0)
        last_e = jnp.where(sub == 7, 0.25, 0.0)
        p_parts = []
        for q, (c, k) in enumerate(zip(groups(cbuf[...]), groups(cext[0:elems]))):
            x = c - inner_parts[q] * m_t
            if q == 0:
                x = x + first_w * w_t
            if q == parts - 1:
                x = x + last_e * e_t
            p_parts.append(x * k)
        s_rim = jnp.concatenate([s_n, s_s, s_w, s_e], axis=0)
        p_rim = s_rim * cext[elems:elems + h]
        p = whole(p_parts)
        pbuf[g] = p
        hi, lo = cut(p)
        coef = fdot(jnp.concatenate([hi, lo], axis=1), Q)
        rim_w, rim_e = tall(p_rim[2 * tj:2 * tj + ti]), tall(p_rim[2 * tj + ti:2 * tj + 2 * ti])
        down = [pltpu.roll(x, 1, 1) for x in p_parts]
        up = [pltpu.roll(x, 7, 1) for x in p_parts]
        left = [jnp.where(sub == 0, rim_w if q == 0 else down[q - 1], down[q]) for q in range(parts)]
        right = [jnp.where(sub == 7, rim_e if q == parts - 1 else up[q + 1], up[q]) for q in range(parts)]
        rim_h = p_rim[0:2 * tj].astype(BF16)
        nb = [
            jnp.concatenate([rim_h[0:tj], hi[0:elems - tj]], axis=0),
            jnp.concatenate([hi[tj:], rim_h[tj:2 * tj]], axis=0),
            whole(left).astype(BF16),
            whole(right).astype(BF16),
        ]
        lifted = fdot(jnp.concatenate([nb[f] * packs[f] for f in range(4)], axis=1), cwts[...])
        c_hi, c_lo = cut(coef)
        base = [wbuf[q] + lifted[q * tj:(q + 1) * tj] for q in range(ti)]
        for q in range(ti):
            at = slice(q * tj, (q + 1) * tj)
            y = fdot(jnp.concatenate([c_hi[at] * own_block, c_lo[at] * own_block], axis=0), wmat[q])
            wbuf[q] = base[q] + y[0:tj, 0:n] + (y[tj:2 * tj, 0:n] + y[0:tj, n:2 * n])

    def full(g, x):
        hi, lo = cut(pbuf[g])
        mixed = jnp.where(low, hi.astype(F32), lo.astype(F32)).astype(BF16)
        zbuf[g] = x + fdot(jnp.concatenate([mixed, hi], axis=1), RF)

    edges = local_coarse(rhs2)
    local_lifts(rhs2)
    local_blocks(rhs2, True)
    rim_wait(0, "recv")
    fix_rims(0)
    line_wait(0, "recv")
    rim_wait(2, "recv")
    if steps:
        tell(0)

    cext[elems:elems + h] = chalo[...]
    fix(0, *edges)
    fill_sends(1, wbuf)
    start_all(rim_copies(1))
    fill_sums(1, wbuf)
    share_lines(1)
    w1 = wbuf[...].reshape(elems, n)
    fbuf[...] = w1
    for q in range(len(steps)):
        learn(q)
        if q + 1 < len(steps):
            tell(q + 1)
    edges = local_coarse(w1)
    local_lifts(w1)
    local_blocks(w1, False)
    own_n1 = total(rhs2 * rhs2)
    p_one = safe_div(total(rhs2 * w1), own_n1)
    gap = w1 - p_one * rhs2
    gbuf[...] = gap
    own_n2 = total(gap * gap)
    rim_wait(1, "recv")
    fix_rims(1)
    line_wait(1, "recv")

    fix(1, *edges)
    w2 = wbuf[...].reshape(elems, n)
    rhs2, gap = rhs[...].reshape(elems, n), gbuf[...]
    on_rhs, on_gap, square = total(rhs2 * w2), total(gap * w2), total(w2 * w2)
    p_two, q_two = safe_div(on_rhs, own_n1), safe_div(on_gap, own_n2)
    rest = jnp.maximum(square - p_two * on_rhs - q_two * on_gap, 0.0)
    msgs[me] = message([own_n1, p_one, own_n2, p_two, q_two, rest])
    broadcast()
    full(0, rhs2)
    full(1, fbuf[...])
    for g in range(2):
        line_wait(g, "send")
    for g in range(3):
        rim_wait(g, "send")
    bc_wait("send")
    bc_wait("recv")
    Y = msgs[:, 0, :]
    l_n1, l_p, l_n2, l_a, l_b, l_n3 = [Y] + [pltpu.roll(Y, n - q, 1) for q in range(1, 6)]

    def over(x):
        return jnp.sum(x, axis=0, keepdims=True)
    per_len2 = 1.0 / over(l_n1)
    h11 = over(l_p * l_n1) * per_len2
    dev = l_p - h11
    gap2 = over(dev * dev * l_n1 + l_n2)
    per_gap2 = 1.0 / gap2
    ratio = gap2 * per_len2
    e_one = l_a - h11 * l_p
    e_two = l_b - h11
    t12 = over(e_one * l_n1) * per_len2
    h22 = over(dev * e_one * l_n1 + e_two * l_n2) * per_gap2
    g_one = e_one - t12 - h22 * dev
    g_two = e_two - h22
    last2 = over(g_one * g_one * l_n1 + g_two * g_two * l_n2 + l_n3) * per_gap2
    first2 = h11 * h11 + ratio
    lower = h11 * h22 - t12
    c2 = -lower / (lower * lower + last2 * first2)
    c1 = (h11 - c2 * (h11 * t12 + ratio * h22)) / first2 - c2 * h11
    h21 = jnp.sqrt(ratio)
    h12, h32 = t12 / h21, jnp.sqrt(last2)
    c1, c2, h11, h12, h21, h22, h32 = [v[:, 0:1] for v in (c1, c2, h11, h12, h21, h22, h32)]
    out[...] = (c1 * zbuf[0] + c2 * zbuf[1]).reshape(ti, tj, n)
    hr, hc = iota((2, 3), 1), iota((2, 3), 0)
    hess_out[...] = jnp.where(
        hr == 0, jnp.where(hc == 0, h11, h12),
        jnp.where(hr == 1, jnp.where(hc == 0, h21, h22), jnp.where(hc == 0, 0.0, h32)))


def hand_on(sol_in, hess_in, sol_out, hess_out, sem):
    copies = [pltpu.make_async_copy(sol_in, sol_out, sem.at[0]), pltpu.make_async_copy(hess_in, hess_out, sem.at[1])]
    for c in copies:
        c.start()
    for c in copies:
        c.wait()


def solution(mesh):
    nx, ny = mesh.shape["gx"], mesh.shape["gy"]

    def body(rhs, diag, lift, state, basis, cinv):
        ti, tj, n = rhs.shape
        kc = basis.shape[1]
        cflat = jnp.transpose(cinv, (0, 2, 3, 1)).reshape(ti, kc * kc, tj)
        sflat = jnp.transpose(state, (0, 2, 1))
        h = 2 * ti + 2 * tj
        vm = pl.BlockSpec(memory_space=pltpu.VMEM)
        hbm = pl.BlockSpec(memory_space=pltpu.HBM)
        sol, hess = pl.pallas_call(
            functools.partial(kernel, nx, ny, ti, tj, n, kc),
            out_shape=(jax.ShapeDtypeStruct((ti, tj, n), F32), jax.ShapeDtypeStruct((2, 3), F32)),
            in_specs=[hbm] * 6,
            out_specs=(vm, vm),
            scratch_shapes=[
                pltpu.VMEM((ti, tj, n), F32),
                pltpu.VMEM((4, n, n), BF16),
                pltpu.VMEM((ti, 4, tj), jnp.int32),
                pltpu.VMEM((kc, n), F32),
                pltpu.VMEM((ti, kc * kc, tj), F32),
                pltpu.VMEM((ti, tj, n, n), BF16),
                pltpu.VMEM((8 * n, n), BF16),
                pltpu.VMEM((4 * n, n), BF16),
                pltpu.VMEM((ti, tj * kc, 2 * n), BF16),
                pltpu.VMEM((8, ti * tj, n), BF16),
                pltpu.VMEM((4, ti * tj, n), BF16),
                pltpu.VMEM((4, ti, n), BF16),
                pltpu.VMEM((ti * tj + h, n), F32),
                pltpu.VMEM((2, ti * tj, n), F32),
                pltpu.VMEM((2, ti * tj, n), F32),
                pltpu.VMEM((ti * tj, n), F32),
                pltpu.VMEM((ti * tj, n), F32),
                pltpu.VMEM((ti * tj, n), F32),
                pltpu.VMEM((ti, tj, n), F32),
                pltpu.VMEM((2, h, n), BF16),
                pltpu.VMEM((2, h, n), BF16),
                pltpu.VMEM((h, n), F32),
                pltpu.VMEM((h, n), F32),
                pltpu.VMEM((2, 3 * ny, 8, n), F32),
                pltpu.VMEM((nx * ny, 1, n), F32),
                pltpu.SemaphoreType.DMA((5,)),
                pltpu.SemaphoreType.DMA((-(-ti // max(1, ti // 4)),)),
                pltpu.SemaphoreType.DMA((3,)),
                pltpu.SemaphoreType.DMA((3, 4)),
                pltpu.SemaphoreType.DMA((2,)),
                pltpu.SemaphoreType.DMA((2,)),
                pltpu.SemaphoreType.DMA((1,)),
                pltpu.SemaphoreType.DMA((1,)),
                pltpu.SemaphoreType.REGULAR((max(1, (nx - 2).bit_length() - 1),)),
            ],
            compiler_params=pltpu.CompilerParams(collective_id=0, has_side_effects=True,
                                                 vmem_limit_bytes=30000 * 1024),
        )(*[pltpu.with_memory_space_constraint(x, pltpu.HBM) for x in (rhs, diag, lift, sflat, basis.T, cflat)])
        sol, hess = pl.pallas_call(
            hand_on,
            out_shape=(jax.ShapeDtypeStruct(sol.shape, F32), jax.ShapeDtypeStruct(hess.shape, F32)),
            in_specs=[vm, vm],
            out_specs=(hbm, hbm),
            scratch_shapes=[pltpu.SemaphoreType.DMA((2,))],
            compiler_params=pltpu.CompilerParams(vmem_limit_bytes=30000 * 1024),
        )(sol, hess)
        return sol, hess.T

    in_specs = (P("gx", "gy", None), P("gx", "gy", None, None), P(), P("gx", "gy", None), P(),
                P("gx", "gy", None, None))
    return jax.shard_map(body, mesh=mesh, in_specs=in_specs, out_specs=(P("gx", "gy", None), P()), check_vma=False)
```

```python
import functools
import jax
import jax.numpy as jnp
from jax import lax
from jax.experimental import pallas as pl
from jax.experimental.pallas import tpu as pltpu
from jax.sharding import PartitionSpec as P

MESH = pl.DeviceIdType.MESH
F32 = jnp.float32
BF16 = jnp.bfloat16


def fdot(a, b):
    return jnp.dot(a, b, preferred_element_type=F32)


def over_first(a, b):
    return lax.dot_general(a, b, (((0,), (0,)), ((), ())), preferred_element_type=F32)


def cut(x):
    hi = x.astype(BF16)
    return hi, (x - hi.astype(F32)).astype(BF16)


def fine_dot(x, w):
    hi, lo = cut(x)
    return fdot(jnp.concatenate([hi, lo, hi], axis=1), w)


def exact_dot(x, w):
    m = x.shape[0]
    y = fdot(jnp.concatenate(cut(x), axis=0), w)
    return y[0:m] + y[m:2 * m]


def small_dot(x, w):
    m, n = x.shape[0], w.shape[1] // 2
    y = fdot(jnp.concatenate(cut(x), axis=0), w)
    return y[0:m, 0:n] + y[m:2 * m, 0:n] + y[0:m, n:2 * n]


def one_hot(x):
    return x.astype(F32).astype(BF16)


def total(x):
    return jnp.sum(jnp.sum(x, axis=0, keepdims=True), axis=1, keepdims=True)


def safe_div(a, b):
    return jnp.where(b > 0, a / jnp.where(b > 0, b, 1.0), 0.0)


def iota(shape, dim):
    return lax.broadcasted_iota(jnp.int32, shape, dim)


def kernel(nx, ny, ti, tj, n, kc, rhs_h, diag, lift_h, state_h, basis_h, cinv_h, out, hess_out,
           rhs, lift, state, basis, cinv,
           dvm, wts, cwts, wmat, masks, packs, rims, cext, pbuf, zbuf, cbuf, fbuf, gbuf, wbuf, sends, halos, csend, chalo, sums, msgs,
           isem, dsem, ssem, rsem, lsend, lrecv, msend, mrecv, know):
    gx = lax.axis_index("gx")
    gy = lax.axis_index("gy")
    me = gx * ny + gy
    count = nx * ny
    elems = ti * tj
    kk = kc * kc

    barrier = pltpu.get_barrier_semaphore()

    has_n, has_s, has_w, has_e = gx > 0, gx < nx - 1, gy > 0, gy < ny - 1
    n_i, s_i, w_i, e_i = [v.astype(jnp.int32) for v in (has_n, has_s, has_w, has_e)]
    turns = list(range(1, ny))
    near = [(has_s, 1, k) for k in turns[::-1] + [0]] + [(None, 0, k) for k in turns[::-1]] + [
        (has_n, -1, k) for k in turns[::-1] + [0]]
    near_count = ny - 1 + ny * (n_i + s_i)

    def when(ok, run):
        if ok is None:
            run()
        else:
            pl.when(ok)(run)

    for ok, d, k in [(has_n, -1, k) for k in turns + [0]] + near[:2 * ny - 1]:
        def hello(d=d, k=k):
            pl.semaphore_signal(barrier, inc=1, device_id=(gx + d, lax.rem(gy + k, ny)), device_id_type=MESH)
        when(ok, hello)

    h = 2 * ti + 2 * tj
    for ok, at, rows, line in ((has_n, 0, tj, 0), (has_s, tj, tj, 2), (has_w, 2 * tj, ti, None), (has_e, 2 * tj + ti, ti, None)):
        @pl.when(jnp.logical_not(ok))
        def _(at=at, rows=rows, line=line):
            halos[:, at:at + rows] = jnp.zeros((2, rows, n), BF16)
            chalo[at:at + rows] = jnp.zeros((rows, n), F32)
            if line is not None:
                sums[:, line * ny:(line + 1) * ny] = jnp.zeros((2, ny, 8, n), F32)

    loads = [pltpu.make_async_copy(a, b, isem.at[q]) for q, (a, b) in enumerate(
        ((rhs_h, rhs), (basis_h, basis), (cinv_h, cinv), (state_h, state), (lift_h, lift)))]
    for c in loads:
        c.start()
    group = max(1, ti // 4)
    dcopies = [pltpu.make_async_copy(diag.at[pl.ds(q, group)], dvm.at[pl.ds(q, group)], dsem.at[q // group])
               for q in range(0, ti, group)]
    dcopies[0].start()
    dcopies[1].start()

    steps = []
    r = 2
    while r < nx - 1:
        steps.append(r)
        r *= 2

    def tell(q):
        r = steps[q]
        for ok, d in ((gx >= r, -r), (gx + r < nx, r)):
            def one(d=d):
                pl.semaphore_signal(know.at[q], inc=1, device_id=(gx + d, gy), device_id_type=MESH)
            when(ok, one)

    def learn(q):
        r = steps[q]
        amount = (gx >= r).astype(jnp.int32) + (gx + r < nx).astype(jnp.int32)
        pl.semaphore_wait(know.at[q], amount)

    def line_copy(g, d, k):
        return pltpu.make_async_remote_copy(
            src_ref=sums.at[g, ny + gy], dst_ref=sums.at[g, (1 - d) * ny + gy],
            send_sem=lsend.at[g], recv_sem=lrecv.at[g],
            device_id=(gx + d, lax.rem(gy + k, ny)), device_id_type=MESH)

    def share_lines(g):
        for ok, d, k in near:
            when(ok, lambda d=d, k=k: line_copy(g, d, k).start())

    def line_wait(g, which):
        for lines in range(3):
            messages = ny * (lines + 1) - 1
            if messages:
                @pl.when(n_i + s_i == lines)
                def _(messages=messages):
                    part = sums.at[g, pl.ds(0, messages)]
                    c = pltpu.make_async_remote_copy(
                        src_ref=part, dst_ref=part, send_sem=lsend.at[g], recv_sem=lrecv.at[g],
                        device_id=(gx, gy), device_id_type=MESH)
                    if which == "send":
                        c.wait_send()
                    else:
                        c.wait_recv()

    h = 2 * ti + 2 * tj
    croutes = [
        (has_n, (gx - 1, gy), 0, tj, tj),
        (has_s, (gx + 1, gy), tj, 0, tj),
        (has_w, (gx, gy - 1), 2 * tj, 2 * tj + ti, ti),
        (has_e, (gx, gy + 1), 2 * tj + ti, 2 * tj, ti),
    ]
    opposite = [1, 0, 3, 2]

    def rim_copies(g):
        return [(ok, pltpu.make_async_remote_copy(
            src_ref=sends.at[g, pl.ds(src, rows)], dst_ref=halos.at[g, pl.ds(dst, rows)],
            send_sem=ssem.at[g], recv_sem=rsem.at[g, opposite[d]],
            device_id=dev, device_id_type=MESH)) for d, (ok, dev, src, dst, rows) in enumerate(croutes)]

    def coarse_copies():
        return [(ok, pltpu.make_async_remote_copy(
            src_ref=csend.at[pl.ds(src, rows)], dst_ref=chalo.at[pl.ds(dst, rows)],
            send_sem=ssem.at[2], recv_sem=rsem.at[2, opposite[d]],
            device_id=dev, device_id_type=MESH)) for d, (ok, dev, src, dst, rows) in enumerate(croutes)]

    def rim_part(g, src, rows):
        return halos.at[g, pl.ds(src, rows)] if g < 2 else chalo.at[pl.ds(src, rows)]

    def rim_wait(g, which):
        if which == "send":
            for a in range(3):
                for b in range(3):
                    if a or b:
                        @pl.when(jnp.logical_and(n_i + s_i == a, w_i + e_i == b))
                        def _(a=a, b=b):
                            part = rim_part(g, 0, a * tj + b * ti)
                            pltpu.make_async_remote_copy(
                                src_ref=part, dst_ref=part, send_sem=ssem.at[g], recv_sem=rsem.at[g, 0],
                                device_id=(gx, gy), device_id_type=MESH).wait_send()
            return
        for d, (ok, dev, src, dst, rows) in enumerate(croutes):
            @pl.when(ok)
            def _(d=d, dev=dev, src=src, rows=rows):
                part = rim_part(g, src, rows)
                pltpu.make_async_remote_copy(
                    src_ref=part, dst_ref=part, send_sem=ssem.at[g], recv_sem=rsem.at[g, d],
                    device_id=dev, device_id_type=MESH).wait_recv()

    def start_all(copies):
        for ok, c in copies:
            @pl.when(ok)
            def _(c=c):
                c.start()

    def broadcast():
        for tx, ty in sorted(((x, y) for x in range(nx) for y in range(ny)), key=lambda t: t[0] // 2 + t[1] // 2 + t[1] % 2):
            @pl.when(jnp.logical_or(gx != tx, gy != ty))
            def _(tx=tx, ty=ty):
                pltpu.make_async_remote_copy(
                    src_ref=msgs.at[me], dst_ref=msgs.at[me], send_sem=msend.at[0], recv_sem=mrecv.at[0],
                    device_id=(tx, ty), device_id_type=MESH).start()

    def bc_wait(which):
        part = msgs.at[pl.ds(0, count - 1)]
        c = pltpu.make_async_remote_copy(
            src_ref=part, dst_ref=part, send_sem=msend.at[0], recv_sem=mrecv.at[0],
            device_id=(gx, gy), device_id_type=MESH)
        if which == "send":
            c.wait_send()
        else:
            c.wait_recv()

    def fill_sends(g, ref):
        sends[g, 0:tj] = ref[0].astype(BF16)
        sends[g, tj:2 * tj] = ref[ti - 1].astype(BF16)
        sends[g, 2 * tj:2 * tj + ti] = ref[:, 0, :].astype(BF16)
        sends[g, 2 * tj + ti:h] = ref[:, tj - 1, :].astype(BF16)

    lane1 = iota((1, n), 1)

    def message(values):
        row = jnp.zeros((1, n), F32)
        for p, v in enumerate(values):
            row = jnp.where(lane1 == p, v, row)
        return row

    row_k = lax.rem(iota((kc, n), 1), kk) // kc == iota((kc, n), 0)
    row_l = lax.rem(iota((kc, n), 1), kc) == iota((kc, n), 0)
    pick = iota((ti, n), 1) // kc == iota((ti, n), 0)
    pick_j = iota((tj, n), 1) // kc == iota((tj, n), 0)
    low = lane1 < kk
    loads[0].wait()
    loads[1].wait()
    Rh, Rl = cut(basis[...])

    def spreads(pattern):
        e = one_hot(pattern)
        return over_first(Rh, e).astype(BF16), over_first(Rl, e).astype(BF16)

    def stacked(hi, lo):
        return jnp.concatenate([hi, hi, lo], axis=0)
    RT = jnp.concatenate(spreads(row_l), axis=1)
    rhs3 = rhs[...]
    rhs2 = rhs3.reshape(elems, n)

    def fill_sums(g, ref):
        rows = jnp.concatenate([
            jnp.sum(ref[...], axis=1), ref[:, 0, :], ref[:, 1, :], ref[:, tj - 1, :], ref[:, tj - 2, :],
            ref[0], ref[ti - 1]], axis=0)
        rows = small_dot(rows, RT)
        for q in range(7):
            at, lanes, size = (q * ti, pick, ti) if q < 5 else (5 * ti + (q - 5) * tj, pick_j, tj)
            sums[g, ny + gy, q:q + 1] = jnp.sum(jnp.where(lanes, rows[at:at + size], 0.0), axis=0, keepdims=True)

    fill_sends(0, rhs)
    fill_sums(0, rhs)
    loads[2].wait()
    eye = one_hot(iota((tj, tj), 0) == iota((tj, tj), 1))
    chi, clo = cut(cinv[...])
    both = jnp.concatenate([chi, clo], axis=2)
    both = jnp.concatenate([both, both], axis=1).reshape(ti * n, 2 * tj)
    turned = lax.dot_general(jnp.concatenate([eye, eye], axis=1), both, (((1,), (1,)), ((), ())),
                             preferred_element_type=F32)
    for q in range(ti):
        cext[q * tj:(q + 1) * tj] = turned[:, q * n:(q + 1) * n]
    c3d = cext[0:elems].reshape(ti, tj, n)
    csend[0:tj] = c3d[0]
    csend[tj:2 * tj] = c3d[ti - 1]
    csend[2 * tj:2 * tj + ti] = c3d[:, 0, :]
    csend[2 * tj + ti:2 * tj + 2 * ti] = c3d[:, tj - 1, :]

    pl.semaphore_wait(barrier, near_count)
    start_all(rim_copies(0))
    share_lines(0)
    start_all(coarse_copies())

    for c in dcopies[2:]:
        c.start()
    RE = stacked(*spreads(row_k))
    row_le = one_hot(row_l)
    RFh, RFl = over_first(row_le, Rh).astype(BF16), over_first(row_le, Rl).astype(BF16)
    low_row = iota((n, n), 0) < kk
    RF = jnp.concatenate([RFh, jnp.where(low_row, RFl.astype(F32), 0.0).astype(BF16)], axis=0)
    G = one_hot(lax.rem(iota((n, n), 0), kc) == lax.rem(iota((n, n), 1), kk) // kc)
    Q = one_hot(jnp.logical_and(low_row, lax.rem(iota((n, n), 0), kc) == lax.rem(iota((n, n), 1), kc)))
    Q = jnp.concatenate([Q, Q], axis=0)
    flip = one_hot(iota((n, n), 0) + iota((n, n), 1) == n - 1)
    RR = jnp.concatenate([RFh, RFl], axis=1)
    loads[4].wait()
    for f in range(4):
        straight = lift[f]
        turned = fdot(flip, straight).astype(BF16)
        wts[2 * f * n:(2 * f + 1) * n] = straight
        wts[(2 * f + 1) * n:(2 * f + 2) * n] = turned
        pair = jnp.concatenate([straight, turned], axis=1)
        prod = fdot(RR, jnp.concatenate([pair, pair], axis=0))
        cwts[f * n:(f + 1) * n] = jnp.where(low_row, prod[:, 0:n], prod[:, n:2 * n]).astype(BF16)
    loads[3].wait()
    own_j = lax.rem(iota((elems, tj), 0), tj) == iota((elems, tj), 1)
    ones = jnp.ones((tj, n), BF16)
    for f in range(4):
        rows = state[:, f, :].astype(F32)
        wide = jnp.broadcast_to(rows[:, None, :], (ti, tj, tj)).reshape(elems, tj)
        col = fdot(jnp.where(own_j, wide, 0.0).astype(BF16), ones)
        masks[2 * f] = one_hot(col == 1.0)
        masks[2 * f + 1] = one_hot(col == 2.0)
        packs[f] = one_hot(col == jnp.where(low, 1.0, 2.0))
        if f >= 2:
            edge = col.reshape(ti, tj, n)[:, 0 if f == 2 else tj - 1, :]
            rims[2 * f - 4] = one_hot(edge == 1.0)
            rims[2 * f - 3] = one_hot(edge == 2.0)

    jrow = lax.rem(iota((elems, 1), 0), tj)
    trow = iota((tj, 1), 0)
    scale = 1.0 / (ny * tj)
    irow = iota((1, 8, 1), 1)
    inner_parts = [1.0 + 0.25 * ((irow + q * 8 > 0).astype(F32) + (irow + q * 8 < tj - 1).astype(F32))
                   for q in range(tj // 8)]

    def spread(col):
        return jnp.broadcast_to(col[:, None, :], (ti, tj, n)).reshape(elems, n)

    def left_of(x, edge):
        return jnp.where(jrow == 0, edge, pltpu.roll(x, 1, 0))

    def right_of(x, edge):
        return jnp.where(jrow == tj - 1, edge, pltpu.roll(x, elems - 1, 0))

    def line_sum(g, d):
        acc = sums[g, (d + 1) * ny, 0:1]
        for q in range(1, ny):
            acc = acc + sums[g, (d + 1) * ny + q, 0:1]
        return acc

    def part_of(g, dx, dy, row):
        at = (dx + 1) * ny + jnp.clip(gy + dy, 0, ny - 1)
        return sums[g, at, row:row + 1]

    half = tj // 2
    keep = [one_hot(lax.rem(iota((2 * tj, n), 0), half) == t) for t in range(half)]
    none = jnp.zeros((kc, n), BF16)
    coarse_rows = jnp.concatenate([
        jnp.concatenate([Rh, none], axis=1), jnp.concatenate([none, Rh], axis=1)], axis=0)
    own_block = one_hot(iota((tj, n), 1) // kc == iota((tj, n), 0))

    def local_lifts(x):
        b = x.astype(BF16)
        gap = jnp.zeros((tj, n), BF16)
        nb = [
            jnp.concatenate([gap, b[0:elems - tj]], axis=0),
            jnp.concatenate([b[tj:], gap], axis=0),
            left_of(x, 0.0).astype(BF16),
            right_of(x, 0.0).astype(BF16),
        ]
        cols = []
        for f in range(4):
            cols.append(nb[f] * masks[2 * f])
            cols.append(nb[f] * masks[2 * f + 1])
        wbuf[...] = fdot(jnp.concatenate(cols, axis=1), wts[...]).reshape(ti, tj, n)

    def local_blocks(x, first):
        for q in range(ti):
            if first and q % group == 0:
                dcopies[q // group].wait()
            both = jnp.concatenate(cut(x[q * tj:(q + 1) * tj]), axis=0)
            rhs_w = jnp.concatenate(
                [dvm[q, 0:half].reshape(half * n, n), dvm[q, half:tj].reshape(half * n, n)], axis=1)
            if first:
                prod = None
                for t in range(0, half, 2):
                    lhs = jnp.concatenate([
                        jnp.concatenate([both * keep[t], both * keep[t + 1]], axis=1), coarse_rows], axis=0)
                    part = fdot(lhs, rhs_w[t * n:(t + 2) * n])
                    prod = part[0:2 * tj] if prod is None else prod + part[0:2 * tj]
                    for side in range(2):
                        at = (side * half + t) * kc
                        hi, lo = cut(part[2 * tj:, side * n:(side + 1) * n])
                        wmat[q, at:at + 2 * kc, 0:n] = hi
                        wmat[q, at:at + 2 * kc, n:2 * n] = lo
            else:
                prod = fdot(jnp.concatenate([both * keep[t] for t in range(half)], axis=1), rhs_w)
            prod = prod[0:tj] + prod[tj:2 * tj]
            wbuf[q] += jnp.concatenate([prod[0:half, 0:n], prod[half:tj, n:2 * n]], axis=0)

    def local_coarse(x):
        c = fine_dot(x, RE)
        cbuf[...] = c + 0.25 * (left_of(c, 0.0) + right_of(c, 0.0))
        c3 = c.reshape(ti, tj, n)
        return c3[:, 0, :], c3[:, tj - 1, :]

    def fix_rims(g):
        def rim_lift(f, at, one, two):
            b = halos[g, at:at + one.shape[0]]
            return fdot(jnp.concatenate([b * one, b * two], axis=1), wts[2 * f * n:(2 * f + 2) * n])
        last = elems - tj
        north = rim_lift(0, 0, masks[0, 0:tj], masks[1, 0:tj])
        south = rim_lift(1, tj, masks[2, last:elems], masks[3, last:elems])
        west = rim_lift(2, 2 * tj, rims[0], rims[1])
        east = rim_lift(3, 2 * tj + ti, rims[2], rims[3])
        for q in range(ti):
            side = jnp.where(trow == 0, west[q:q + 1], jnp.where(trow == tj - 1, east[q:q + 1], 0.0))
            if q == 0:
                side = side + north
            if q == ti - 1:
                side = side + south
            wbuf[q] += side

    def fix(g, own_w, own_e):
        group_of = lane1 // kc

        def lanes(x, mask):
            return jnp.where(mask, jnp.broadcast_to(x, mask.shape), 0.0)
        single = [
            (line_sum(g, -1), ti - 1), (line_sum(g, 1), 0),
            (part_of(g, -1, -1, 6), tj - 1), (part_of(g, -1, 1, 6), 0),
            (part_of(g, 1, -1, 5), tj - 1), (part_of(g, 1, 1, 5), 0)]
        srow = iota((8, n), 0)
        singles = jnp.zeros((8, n), F32)
        for q, (x, at) in enumerate(single):
            singles = jnp.where(jnp.logical_and(srow == q, group_of == at), jnp.broadcast_to(x, (8, n)), singles)
        stack = jnp.concatenate([
            lanes(line_sum(g, 0) * scale, pick),
            lanes(part_of(g, 0, -1, 3), pick), lanes(part_of(g, 0, -1, 4), pick),
            lanes(part_of(g, 0, 1, 1), pick), lanes(part_of(g, 0, 1, 2), pick),
            lanes(part_of(g, -1, 0, 6), pick_j), lanes(part_of(g, 1, 0, 5), pick_j), singles], axis=0)
        wide = exact_dot(stack, G)
        m_c, c_w1, c_w2, c_e1, c_e2 = [wide[q * ti:(q + 1) * ti] for q in range(5)]
        c_n, c_s = wide[5 * ti:5 * ti + tj], wide[5 * ti + tj:5 * ti + 2 * tj]
        one = wide[5 * ti + 2 * tj:]
        m_n, m_s = one[0:1] * scale, one[1:2] * scale
        c_nw, c_ne, c_sw, c_se = [one[q:q + 1] for q in range(2, 6)]
        w_f, e_f = w_i.astype(F32), e_i.astype(F32)
        c_w1, c_w2 = (c_w1 - m_c) * w_f, c_w2 - m_c
        c_e1, c_e2 = (c_e1 - m_c) * e_f, c_e2 - m_c
        c_n, c_s = c_n - m_n, c_s - m_s
        c_nw, c_sw = (c_nw - m_n) * w_f, (c_sw - m_s) * w_f
        c_ne, c_se = (c_ne - m_n) * e_f, (c_se - m_s) * e_f

        def row_smooth(x, lo, hi):
            left = jnp.where(trow == 0, lo, pltpu.roll(x, 1, 0))
            right = jnp.where(trow == tj - 1, hi, pltpu.roll(x, tj - 1, 0))
            return x + 0.25 * (left + right)
        s_n, s_s = row_smooth(c_n, c_nw, c_ne), row_smooth(c_s, c_sw, c_se)
        s_w = c_w1 + 0.25 * (c_w2 + own_w - m_c)
        s_e = c_e1 + 0.25 * (own_e - m_c + c_e2)
        sub = iota((1, 8, 1), 1)
        parts = tj // 8

        def groups(x):
            return [x.reshape(ti, parts, 8, n)[:, q] for q in range(parts)]

        def whole(xs):
            return jnp.concatenate([x[:, None] for x in xs], axis=1).reshape(elems, n)

        def tall(x):
            return jnp.broadcast_to(x[:, None, :], (ti, 8, n))
        m_t, w_t, e_t = tall(m_c), tall(c_w1), tall(c_e1)
        first_w = jnp.where(sub == 0, 0.25, 0.0)
        last_e = jnp.where(sub == 7, 0.25, 0.0)
        p_parts = []
        for q, (c, k) in enumerate(zip(groups(cbuf[...]), groups(cext[0:elems]))):
            x = c - inner_parts[q] * m_t
            if q == 0:
                x = x + first_w * w_t
            if q == parts - 1:
                x = x + last_e * e_t
            p_parts.append(x * k)
        s_rim = jnp.concatenate([s_n, s_s, s_w, s_e], axis=0)
        p_rim = s_rim * cext[elems:elems + h]
        p = whole(p_parts)
        pbuf[g] = p
        hi, lo = cut(p)
        coef = fdot(jnp.concatenate([hi, lo], axis=1), Q)
        rim_w, rim_e = tall(p_rim[2 * tj:2 * tj + ti]), tall(p_rim[2 * tj + ti:2 * tj + 2 * ti])
        down = [pltpu.roll(x, 1, 1) for x in p_parts]
        up = [pltpu.roll(x, 7, 1) for x in p_parts]
        left = [jnp.where(sub == 0, rim_w if q == 0 else down[q - 1], down[q]) for q in range(parts)]
        right = [jnp.where(sub == 7, rim_e if q == parts - 1 else up[q + 1], up[q]) for q in range(parts)]
        rim_h = p_rim[0:2 * tj].astype(BF16)
        nb = [
            jnp.concatenate([rim_h[0:tj], hi[0:elems - tj]], axis=0),
            jnp.concatenate([hi[tj:], rim_h[tj:2 * tj]], axis=0),
            whole(left).astype(BF16),
            whole(right).astype(BF16),
        ]
        lifted = fdot(jnp.concatenate([nb[f] * packs[f] for f in range(4)], axis=1), cwts[...])
        c_hi, c_lo = cut(coef)
        base = [wbuf[q] + lifted[q * tj:(q + 1) * tj] for q in range(ti)]
        for q in range(ti):
            at = slice(q * tj, (q + 1) * tj)
            y = fdot(jnp.concatenate([c_hi[at] * own_block, c_lo[at] * own_block], axis=0), wmat[q])
            wbuf[q] = base[q] + y[0:tj, 0:n] + (y[tj:2 * tj, 0:n] + y[0:tj, n:2 * n])

    def full(g, x):
        hi, lo = cut(pbuf[g])
        mixed = jnp.where(low, hi.astype(F32), lo.astype(F32)).astype(BF16)
        zbuf[g] = x + fdot(jnp.concatenate([mixed, hi], axis=1), RF)

    edges = local_coarse(rhs2)
    local_lifts(rhs2)
    local_blocks(rhs2, True)
    rim_wait(0, "recv")
    fix_rims(0)
    line_wait(0, "recv")
    rim_wait(2, "recv")
    if steps:
        tell(0)

    cext[elems:elems + h] = chalo[...]
    fix(0, *edges)
    fill_sends(1, wbuf)
    start_all(rim_copies(1))
    fill_sums(1, wbuf)
    share_lines(1)
    w1 = wbuf[...].reshape(elems, n)
    fbuf[...] = w1
    for q in range(len(steps)):
        learn(q)
        if q + 1 < len(steps):
            tell(q + 1)
    edges = local_coarse(w1)
    local_lifts(w1)
    local_blocks(w1, False)
    own_n1 = total(rhs2 * rhs2)
    p_one = safe_div(total(rhs2 * w1), own_n1)
    gap = w1 - p_one * rhs2
    gbuf[...] = gap
    own_n2 = total(gap * gap)
    rim_wait(1, "recv")
    fix_rims(1)
    line_wait(1, "recv")

    fix(1, *edges)
    w2 = wbuf[...].reshape(elems, n)
    rhs2, gap = rhs[...].reshape(elems, n), gbuf[...]
    on_rhs, on_gap, square = total(rhs2 * w2), total(gap * w2), total(w2 * w2)
    p_two, q_two = safe_div(on_rhs, own_n1), safe_div(on_gap, own_n2)
    rest = jnp.maximum(square - p_two * on_rhs - q_two * on_gap, 0.0)
    msgs[me] = message([own_n1, p_one, own_n2, p_two, q_two, rest])
    broadcast()
    full(0, rhs2)
    full(1, fbuf[...])
    for g in range(2):
        line_wait(g, "send")
    for g in range(3):
        rim_wait(g, "send")
    bc_wait("send")
    bc_wait("recv")
    Y = msgs[:, 0, :]
    l_n1, l_p, l_n2, l_a, l_b, l_n3 = [Y] + [pltpu.roll(Y, n - q, 1) for q in range(1, 6)]

    def over(x):
        return jnp.sum(x, axis=0, keepdims=True)
    per_len2 = 1.0 / over(l_n1)
    h11 = over(l_p * l_n1) * per_len2
    dev = l_p - h11
    gap2 = over(dev * dev * l_n1 + l_n2)
    per_gap2 = 1.0 / gap2
    ratio = gap2 * per_len2
    e_one = l_a - h11 * l_p
    e_two = l_b - h11
    t12 = over(e_one * l_n1) * per_len2
    h22 = over(dev * e_one * l_n1 + e_two * l_n2) * per_gap2
    g_one = e_one - t12 - h22 * dev
    g_two = e_two - h22
    last2 = over(g_one * g_one * l_n1 + g_two * g_two * l_n2 + l_n3) * per_gap2
    first2 = h11 * h11 + ratio
    lower = h11 * h22 - t12
    c2 = -lower / (lower * lower + last2 * first2)
    c1 = (h11 - c2 * (h11 * t12 + ratio * h22)) / first2 - c2 * h11
    h21 = jnp.sqrt(ratio)
    h12, h32 = t12 / h21, jnp.sqrt(last2)
    c1, c2, h11, h12, h21, h22, h32 = [v[:, 0:1] for v in (c1, c2, h11, h12, h21, h22, h32)]
    out[...] = (c1 * zbuf[0] + c2 * zbuf[1]).reshape(ti, tj, n)
    hr, hc = iota((2, 3), 1), iota((2, 3), 0)
    hess_out[...] = jnp.where(
        hr == 0, jnp.where(hc == 0, h11, h12),
        jnp.where(hr == 1, jnp.where(hc == 0, h21, h22), jnp.where(hc == 0, 0.0, h32)))


def hand_on(sol_in, hess_in, sol_out, hess_out, sem):
    copies = [pltpu.make_async_copy(sol_in, sol_out, sem.at[0]), pltpu.make_async_copy(hess_in, hess_out, sem.at[1])]
    for c in copies:
        c.start()
    for c in copies:
        c.wait()


def solution(mesh):
    nx, ny = mesh.shape["gx"], mesh.shape["gy"]

    def body(rhs, diag, lift, state, basis, cinv):
        ti, tj, n = rhs.shape
        kc = basis.shape[1]
        cflat = jnp.transpose(cinv, (0, 2, 3, 1)).reshape(ti, kc * kc, tj)
        sflat = jnp.transpose(state, (0, 2, 1))
        h = 2 * ti + 2 * tj
        vm = pl.BlockSpec(memory_space=pltpu.VMEM)
        hbm = pl.BlockSpec(memory_space=pltpu.HBM)
        sol, hess = pl.pallas_call(
            functools.partial(kernel, nx, ny, ti, tj, n, kc),
            out_shape=(jax.ShapeDtypeStruct((ti, tj, n), F32), jax.ShapeDtypeStruct((2, 3), F32)),
            in_specs=[hbm] * 6,
            out_specs=(vm, vm),
            scratch_shapes=[
                pltpu.VMEM((ti, tj, n), F32),
                pltpu.VMEM((4, n, n), BF16),
                pltpu.VMEM((ti, 4, tj), jnp.int32),
                pltpu.VMEM((kc, n), F32),
                pltpu.VMEM((ti, kc * kc, tj), F32),
                pltpu.VMEM((ti, tj, n, n), BF16),
                pltpu.VMEM((8 * n, n), BF16),
                pltpu.VMEM((4 * n, n), BF16),
                pltpu.VMEM((ti, tj * kc, 2 * n), BF16),
                pltpu.VMEM((8, ti * tj, n), BF16),
                pltpu.VMEM((4, ti * tj, n), BF16),
                pltpu.VMEM((4, ti, n), BF16),
                pltpu.VMEM((ti * tj + h, n), F32),
                pltpu.VMEM((2, ti * tj, n), F32),
                pltpu.VMEM((2, ti * tj, n), F32),
                pltpu.VMEM((ti * tj, n), F32),
                pltpu.VMEM((ti * tj, n), F32),
                pltpu.VMEM((ti * tj, n), F32),
                pltpu.VMEM((ti, tj, n), F32),
                pltpu.VMEM((2, h, n), BF16),
                pltpu.VMEM((2, h, n), BF16),
                pltpu.VMEM((h, n), F32),
                pltpu.VMEM((h, n), F32),
                pltpu.VMEM((2, 3 * ny, 8, n), F32),
                pltpu.VMEM((nx * ny, 1, n), F32),
                pltpu.SemaphoreType.DMA((5,)),
                pltpu.SemaphoreType.DMA((-(-ti // max(1, ti // 4)),)),
                pltpu.SemaphoreType.DMA((3,)),
                pltpu.SemaphoreType.DMA((3, 4)),
                pltpu.SemaphoreType.DMA((2,)),
                pltpu.SemaphoreType.DMA((2,)),
                pltpu.SemaphoreType.DMA((1,)),
                pltpu.SemaphoreType.DMA((1,)),
                pltpu.SemaphoreType.REGULAR((max(1, (nx - 2).bit_length() - 1),)),
            ],
            compiler_params=pltpu.CompilerParams(collective_id=0, has_side_effects=True,
                                                 vmem_limit_bytes=30000 * 1024),
        )(*[pltpu.with_memory_space_constraint(x, pltpu.HBM) for x in (rhs, diag, lift, sflat, basis.T, cflat)])
        sol, hess = pl.pallas_call(
            hand_on,
            out_shape=(jax.ShapeDtypeStruct(sol.shape, F32), jax.ShapeDtypeStruct(hess.shape, F32)),
            in_specs=[vm, vm],
            out_specs=(hbm, hbm),
            scratch_shapes=[pltpu.SemaphoreType.DMA((2,))],
            compiler_params=pltpu.CompilerParams(vmem_limit_bytes=30000 * 1024),
        )(sol, hess)
        return sol, hess.T

    in_specs = (P("gx", "gy", None), P("gx", "gy", None, None), P(), P("gx", "gy", None), P(),
                P("gx", "gy", None, None))
    return jax.shard_map(body, mesh=mesh, in_specs=in_specs, out_specs=(P("gx", "gy", None), P()), check_vma=False)
```
